32 devices in a mesh: dp: 8 (over z, x), tensor: 4 (over y, core).
Axes of the slice: x: 2, y: 2, z: 4, core: 2. Of those that a mesh axis runs over, the one named last changes fastest.
Arguments:
- tokens: bfloat16 [25088, 768], P(('dp', 'tensor')), may hold values from -6 to 6
- cotangent: bfloat16 [25088, 768], P(('dp', 'tensor')), may hold values from -6 to 6
- block_patches: int32 [32], P('dp'), may hold values from 196 to 784, as said below
- qkv_weight: bfloat16 [3, 768, 768], P(None, 'dp', 'tensor'), may hold values from -0.21875 to 0.21875
- out_weight: bfloat16 [768, 768], P('tensor', 'dp'), may hold values from -0.875 to 0.875
- up_weight: bfloat16 [768, 3072], P('dp', 'tensor'), may hold values from -0.21875 to 0.21875
- down_weight: bfloat16 [3072, 768], P('tensor', 'dp'), may hold values from -0.109375 to 0.109375
- vectors: float32 [9216], replicated, may hold values from -0.7 to 1.7, as said below
- momentum: float32 [1], replicated, may hold values from 0.4 to 0.7
- target_qkv: float32 [3, 768, 768], P(None, 'dp', 'tensor'), may hold values from -0.21875 to 0.21875
- target_out: float32 [768, 768], P('tensor', 'dp'), may hold values from -0.875 to 0.875
- target_up: float32 [768, 3072], P('dp', 'tensor'), may hold values from -0.21875 to 0.21875
- target_down: float32 [3072, 768], P('tensor', 'dp'), may hold values from -0.109375 to 0.109375
- target_vectors: float32 [9216], replicated, may hold values from -0.7 to 1.7, as said below
Outputs:
- output: bfloat16 [25088, 768], P(('dp', 'tensor'))
- grad_tokens: bfloat16 [25088, 768], P(('dp', 'tensor'))
- grad_qkv: float32 [3, 768, 768], P(None, 'dp', 'tensor')
- grad_out: float32 [768, 768], P('tensor', 'dp')
- grad_up: float32 [768, 3072], P('dp', 'tensor')
- grad_down: float32 [3072, 768], P('tensor', 'dp')
- grad_vectors: float32 [9216], replicated
- next_qkv: float32 [3, 768, 768], P(None, 'dp', 'tensor')
- next_out: float32 [768, 768], P('tensor', 'dp')
- next_up: float32 [768, 3072], P('dp', 'tensor')
- next_down: float32 [3072, 768], P('tensor', 'dp')
- next_vectors: float32 [9216], replicated
The draws below stay inside these ranges and needn't reach their ends.
Inputs may be any that keep to these rules, and one draw needn't show every extreme that they name: `block_patches`: each block of 784 rows holds either one image of 784 patches (entry 784) or four images of 196 patches, one after another (entry 196); both kinds occur in every draw. `vectors`: the gains (the first and third pieces of 768) lie between 0.3 and 1.7. `target_vectors`: laid out as vectors, with gains between 0.3 and 1.7.
All inputs are finite; a program needn't handle non-finite values.
Results may differ from the reference program's by a relative error of at most 0.012.
Values may be sent and summed in bfloat16 or wider, within the bound.
A program may use at most 192 MiB of HBM per device.

```python
import jax
import jax.numpy as jnp
from jax import lax

D = 768
H = 12
HD = 64
FF = 3072
PB = 784
NBLK = 32
TOKENS = 25088


def vector_law(key):
    gain_key, bias_key = jax.random.split(key)
    gains = jax.random.uniform(gain_key, (2, D), jnp.float32, 0.5, 1.5)
    biases = 0.2 * jnp.clip(jax.random.normal(bias_key, (6 * D + FF,), jnp.float32), -3.5, 3.5)
    return jnp.concatenate([gains[0], biases[:D], gains[1], biases[D:]])


def draw_vectors(key, part):
    return vector_law(jax.random.fold_in(key, 11))


def draw_target_vectors(key, part):
    return vector_law(jax.random.fold_in(key, 23))


def draw_block_patches(key, part):
    coins = jax.random.randint(jax.random.fold_in(key, 5), (NBLK - 2,), 0, 2).astype(jnp.int32)
    kinds = jnp.concatenate([jnp.array([1, 0], jnp.int32), coins])
    return jnp.where(kinds == 1, PB, PB // 4).astype(jnp.int32)


def block_scale(key, dims, shards, least, high):
    factor_of, own = 1.0, jax.random.fold_in(key, 6)
    for position, parts in shards:
        steps = jnp.exp(jax.random.uniform(jax.random.fold_in(own, position), (parts,), jnp.float32, least / len(shards), high / len(shards)))
        factor_of = factor_of * jnp.repeat(steps, dims[position] // parts).reshape([-1 if axis == position else 1 for axis in range(len(dims))])
    return factor_of


def noise(own_key, shape, spread, limit, cuts=(), kind=jnp.bfloat16):
    entries = jax.random.normal(own_key, shape, jnp.float32) * spread
    if len(cuts) > 0:
        entries = block_scale(own_key, shape, cuts, -0.22, 0.18) * entries
    return jnp.clip(entries, min=-limit, max=limit).astype(kind)


def setup_inputs(seed: int = 0) -> dict:
    key_of = jax.random.split(jax.random.key(seed), 15)
    tokens = noise(key_of[0], (TOKENS, D), 1.0, 6.0, ((0, 32),))
    cotangent = noise(key_of[1], (TOKENS, D), 1.0, 6.0, ((0, 32),))
    block_patches = draw_block_patches(jax.random.fold_in(key_of[14], 71), 0)
    qkv_weight = noise(key_of[3], (3, D, D), D ** -0.5, 0.21875, ((1, 8), (2, 4)))
    out_weight = noise(key_of[4], (D, D), (D // 16) ** -0.5, 0.875, ((0, 4), (1, 8)))
    up_weight = noise(key_of[5], (D, FF), D ** -0.5, 0.21875, ((0, 8), (1, 4)))
    down_weight = noise(key_of[6], (FF, D), FF ** -0.5, 0.109375, ((0, 4), (1, 8)))
    vectors = draw_vectors(jax.random.fold_in(key_of[14], 71), 0)
    momentum = jnp.clip(jax.random.uniform(key_of[8], (1,), jnp.float32, 0.4, 0.7), 0.4, 0.7)
    target_qkv = noise(key_of[9], (3, D, D), D ** -0.5, 0.21875, ((1, 8), (2, 4)), jnp.float32)
    target_out = noise(key_of[10], (D, D), (D // 16) ** -0.5, 0.875, ((0, 4), (1, 8)), jnp.float32)
    target_up = noise(key_of[11], (D, FF), D ** -0.5, 0.21875, ((0, 8), (1, 4)), jnp.float32)
    target_down = noise(key_of[12], (FF, D), FF ** -0.5, 0.109375, ((0, 4), (1, 8)), jnp.float32)
    target_vectors = draw_target_vectors(jax.random.fold_in(key_of[14], 71), 0)
    return {"tokens": tokens, "cotangent": cotangent, "block_patches": block_patches, "qkv_weight": qkv_weight, "out_weight": out_weight, "up_weight": up_weight, "down_weight": down_weight, "vectors": vectors, "momentum": momentum, "target_qkv": target_qkv, "target_out": target_out, "target_up": target_up, "target_down": target_down, "target_vectors": target_vectors}


@jax.custom_vjp
def low(v):
    return lax.optimization_barrier(v.astype(jnp.bfloat16)).astype(jnp.float32)

@jax.custom_vjp
def low_back(v):
    return v

def low_keep(v):
    return (low(v), None)

def low_pass(kept, grad):
    return (grad,)

def back_keep(v):
    return (v, None)

def back_low(kept, grad):
    return (low(grad),)
low.defvjp(low_keep, low_pass)
low_back.defvjp(back_keep, back_low)

def unpack(vectors):
    return (vectors[0:D], vectors[D:2 * D], vectors[2 * D:3 * D], vectors[3 * D:4 * D], vectors[4 * D:5 * D], vectors[5 * D:6 * D], vectors[6 * D:7 * D], vectors[7 * D:7 * D + FF], vectors[7 * D + FF:8 * D + FF])

def layer_norm(values, gain, bias):
    middle = lax.optimization_barrier(jnp.mean(values, axis=-1, keepdims=True))
    centred = values - middle
    variance = lax.optimization_barrier(jnp.mean(centred * centred, axis=-1, keepdims=True))
    return centred * lax.rsqrt(variance + 1e-06) * gain + bias

def product(left, right):
    return jnp.dot(left, right, precision=lax.Precision.HIGHEST)

def attend_block(query, key, value, patches):
    positions = jnp.arange(PB, dtype=jnp.int32)
    images = positions // patches
    allowed = images[:, None] == images[None, :]
    scores = low_back(jnp.einsum('qhd,khd->hqk', query, key, precision=lax.Precision.HIGHEST) * HD ** (-0.5))
    scores = jnp.where(allowed[None], scores, -1e+30)
    softened = low(jax.nn.softmax(scores, axis=-1))
    return jnp.einsum('hqk,khd->qhd', softened, value, precision=lax.Precision.HIGHEST)

def attend_items(items):
    return attend_block(items[0], items[1], items[2], items[3])

def group_forward(values, patches, qkv_weight, out_weight, up_weight, down_weight, vectors):
    gain1, bias1, gain2, bias2, bias_query, bias_value, bias_out, bias_up, bias_down = unpack(vectors)
    count = values.shape[0]
    normed1 = low(layer_norm(values, gain1, bias1))
    mixed = jnp.einsum('td,cde->cte', normed1, qkv_weight, precision=lax.Precision.HIGHEST)
    query = low(low_back(mixed[0] + bias_query)).reshape(count // PB, PB, H, HD)
    key = low(low_back(mixed[1])).reshape(count // PB, PB, H, HD)
    value = low(low_back(mixed[2] + bias_value)).reshape(count // PB, PB, H, HD)
    attended = lax.map(jax.checkpoint(attend_items), (query, key, value, patches))
    attended = low(low_back(attended.reshape(count, D)))
    residual = values + low_back(product(attended, out_weight)) + bias_out
    normed2 = low(layer_norm(residual, gain2, bias2))
    pre_active = low_back(product(normed2, up_weight) + bias_up)
    active = low(jax.nn.gelu(pre_active, approximate=False))
    return residual + product(active, down_weight) + bias_down

def whole_forward(values, qkv_weight, out_weight, up_weight, down_weight, vectors, block_patches):
    groups = NBLK // 4
    stacked = values.reshape(groups, 4 * PB, D)
    patch_groups = block_patches.reshape(groups, 4)
    stepper = jax.checkpoint(group_forward)

    def advance(carry, items):
        return (carry, stepper(items[0], items[1], qkv_weight, out_weight, up_weight, down_weight, vectors))
    _, results = lax.scan(advance, jnp.zeros((), jnp.float32), (stacked, patch_groups))
    return results.reshape(TOKENS, D)

def reference(tokens, cotangent, block_patches, qkv_weight, out_weight, up_weight, down_weight, vectors, momentum, target_qkv, target_out, target_up, target_down, target_vectors):
    online = (tokens.astype(jnp.float32), qkv_weight.astype(jnp.float32), out_weight.astype(jnp.float32), up_weight.astype(jnp.float32), down_weight.astype(jnp.float32), vectors)

    def closed(values, first, second, third, fourth, fifth):
        return whole_forward(values, first, second, third, fourth, fifth, block_patches)
    result, pull = jax.vjp(closed, *online)
    gradients = pull(cotangent.astype(jnp.float32))
    rate = momentum[0]

    def average(target, weight):
        return rate * target + (1.0 - rate) * weight
    return (result.astype(jnp.bfloat16), gradients[0].astype(jnp.bfloat16), gradients[1], gradients[2], gradients[3], gradients[4], gradients[5], average(target_qkv, online[1]), average(target_out, online[2]), average(target_up, online[3]), average(target_down, online[4]), average(target_vectors, online[5]))
```

```python
import jax
import jax.numpy as jnp
from jax import lax
from jax.sharding import PartitionSpec as P

HD = 64
BOTH = ("dp", "tensor")
F32 = jnp.float32
BF16 = jnp.bfloat16


def unpack(vectors, d, ff):
    cuts = [d * i for i in range(8)] + [7 * d + ff, 8 * d + ff]
    return tuple(vectors[a:b] for a, b in zip(cuts[:-1], cuts[1:]))


def norm_parts(values):
    centred = values - jnp.mean(values, axis=-1, keepdims=True)
    inverse = lax.rsqrt(jnp.mean(centred * centred, axis=-1, keepdims=True) + 1e-06)
    return centred * inverse, inverse


def norm_backward(grad_normed, scaled, inverse, gain):
    weighted = grad_normed * gain
    return inverse * (
        weighted
        - jnp.mean(weighted, axis=-1, keepdims=True)
        - scaled * jnp.mean(weighted * scaled, axis=-1, keepdims=True)
    )


def gelu_parts(v):
    cdf = 0.5 * (1.0 + lax.erf(v * (0.5**0.5)))
    return v * cdf, cdf + v * jnp.exp(-0.5 * v * v) * ((2.0 * jnp.pi) ** -0.5)


def dot(a, b, dims):
    return lax.dot_general(a, b, (dims, ((), ())), preferred_element_type=F32)


def pack_shards(qkv, out, up, down):
    first = jnp.concatenate([qkv[0], qkv[1], qkv[2], out.T], axis=1)
    return jnp.stack([first, up, down.T])


def gather_blocks(shards, dp, tensor):
    every = lax.all_gather(shards, BOTH, axis=0)
    b, r, c = shards.shape
    every = every.reshape(dp, tensor, b, r, c).transpose(2, 1, 0, 3, 4)
    return every.reshape(b, tensor, dp * r, c)


def scatter_blocks(blocks, dp, tensor):
    b, t, rows, c = blocks.shape
    r = rows // dp
    pieces = blocks.reshape(b, tensor, dp, r, c).transpose(2, 1, 0, 3, 4)
    pieces = pieces.reshape(dp * tensor, b, r, c)
    return lax.psum_scatter(pieces, BOTH, scatter_dimension=0, tiled=True)[0]


def local_layer(tokens, cotangent, patches, blocks, vectors):
    rows, d = tokens.shape
    tensor, c = blocks.shape[1], blocks.shape[3]
    w = c // 4
    ff = tensor * c
    heads = d // HD
    gain1, bias1, gain2, bias2, bias_q, bias_v, bias_out, bias_up, bias_down = unpack(
        vectors, d, ff
    )
    first, up, downt = blocks[0], blocks[1], blocks[2]
    factor = HD**-0.5

    x = tokens.astype(F32)
    scaled1, inverse1 = norm_parts(x)
    normed1 = (scaled1 * gain1 + bias1).astype(BF16)
    mixed = jnp.einsum("rd,tdc->rtc", normed1, first[:, :, : 3 * w], preferred_element_type=F32)
    query = (mixed[:, :, :w].reshape(rows, d) + bias_q).astype(BF16).reshape(rows, heads, HD)
    key = mixed[:, :, w : 2 * w].reshape(rows, d).astype(BF16).reshape(rows, heads, HD)
    value = (mixed[:, :, 2 * w :].reshape(rows, d) + bias_v).astype(BF16).reshape(rows, heads, HD)
    images = jnp.arange(rows, dtype=jnp.int32) // patches
    allowed = images[:, None] == images[None, :]
    scores = jnp.einsum("qhd,khd->hqk", query, key, preferred_element_type=F32) * factor
    scores = jnp.where(allowed[None], scores, -1e30)
    raised = jnp.exp(scores - jnp.max(scores, axis=-1, keepdims=True))
    soft = raised / jnp.sum(raised, axis=-1, keepdims=True)
    soft_low = soft.astype(BF16)
    attended = jnp.einsum("hqk,khd->qhd", soft_low, value, preferred_element_type=F32).astype(BF16)
    flat = attended.reshape(rows, tensor, w)
    outt = first[:, :, 3 * w :]
    residual = x + jnp.einsum("rte,tde->rd", flat, outt, preferred_element_type=F32) + bias_out
    scaled2, inverse2 = norm_parts(residual)
    normed2 = (scaled2 * gain2 + bias2).astype(BF16)
    pre = jnp.einsum("rd,tdf->rtf", normed2, up, preferred_element_type=F32) + bias_up.reshape(
        tensor, c
    )
    active, slope = gelu_parts(pre)
    active = active.astype(BF16)
    second = jnp.einsum("rtf,tdf->rd", active, downt, preferred_element_type=F32)
    output = (residual + second + bias_down).astype(BF16)

    grad_active = jnp.einsum("rd,tdf->rtf", cotangent, downt, preferred_element_type=F32)
    grad_pre = (grad_active * slope).astype(BF16)
    g_down = jnp.einsum("rd,rtf->tdf", cotangent, active, preferred_element_type=F32)
    g_up = jnp.einsum("rd,rtf->tdf", normed2, grad_pre, preferred_element_type=F32)
    grad_normed2 = jnp.einsum("rtf,tdf->rd", grad_pre, up, preferred_element_type=F32)
    grad_result = cotangent.astype(F32)
    grad_residual = grad_result + norm_backward(grad_normed2, scaled2, inverse2, gain2)
    grad_branch = grad_residual.astype(BF16)
    g_outt = jnp.einsum("rd,rte->tde", grad_branch, flat, preferred_element_type=F32)
    grad_att = jnp.einsum("rd,tde->rte", grad_branch, outt, preferred_element_type=F32)
    grad_att = grad_att.astype(BF16).reshape(rows, heads, HD)
    grad_value = jnp.einsum("hqk,qhd->khd", soft_low, grad_att, preferred_element_type=F32)
    grad_soft = jnp.einsum("qhd,khd->hqk", grad_att, value, preferred_element_type=F32)
    grad_scores = (
        soft * (grad_soft - jnp.sum(soft * grad_soft, axis=-1, keepdims=True))
    ).astype(BF16)
    grad_query = (
        jnp.einsum("hqk,khd->qhd", grad_scores, key, preferred_element_type=F32) * factor
    )
    grad_key = jnp.einsum("hqk,qhd->khd", grad_scores, query, preferred_element_type=F32) * factor
    three = [
        g.astype(BF16).reshape(rows, tensor, w) for g in (grad_query, grad_key, grad_value)
    ]
    grad_mixed = jnp.concatenate(three, axis=2)
    g_qkv = jnp.einsum("rd,rtc->tdc", normed1, grad_mixed, preferred_element_type=F32)
    grad_normed1 = jnp.einsum(
        "rtc,tdc->rd", grad_mixed, first[:, :, : 3 * w], preferred_element_type=F32
    )
    grad_tokens = (grad_residual + norm_backward(grad_normed1, scaled1, inverse1, gain1)).astype(
        BF16
    )
    grads = jnp.stack(
        [
            jnp.concatenate([g_qkv, g_outt], axis=2).astype(BF16),
            g_up.astype(BF16),
            g_down.astype(BF16),
        ]
    )

    def total(values):
        return jnp.sum(values.astype(F32), axis=0).reshape(-1)

    sums = jnp.concatenate(
        [
            total(grad_normed1 * scaled1),
            total(grad_normed1),
            total(grad_normed2 * scaled2),
            total(grad_normed2),
            total(three[0]),
            total(three[2]),
            total(grad_residual),
            total(grad_pre),
            total(grad_result),
        ]
    )
    return output, grad_tokens, grads, sums


def make_body(dp, tensor):
    def body(
        tokens,
        cotangent,
        block_patches,
        qkv,
        out,
        up,
        down,
        vectors,
        momentum,
        target_qkv,
        target_out,
        target_up,
        target_down,
        target_vectors,
    ):
        patches = block_patches[lax.axis_index("tensor")]
        blocks = gather_blocks(pack_shards(qkv, out, up, down), dp, tensor)
        output, grad_tokens, grads, sums = local_layer(
            tokens, cotangent, patches, blocks, vectors
        )
        grads = scatter_blocks(grads, dp, tensor).astype(F32)
        sums = lax.psum(sums, BOTH)
        w = qkv.shape[2]
        rate = momentum[0]

        def average(target, online):
            return rate * target + (1.0 - rate) * online.astype(F32)

        return (
            output,
            grad_tokens,
            jnp.stack([grads[0][:, i * w : (i + 1) * w] for i in range(3)]),
            grads[0][:, 3 * w :].T,
            grads[1],
            grads[2].T,
            sums,
            average(target_qkv, qkv),
            average(target_out, out),
            average(target_up, up),
            average(target_down, down),
            average(target_vectors, vectors),
        )

    return body


def solution(mesh):
    rows, matrices = P(BOTH, None), (
        P(None, "dp", "tensor"),
        P("tensor", "dp"),
        P("dp", "tensor"),
        P("tensor", "dp"),
    )
    return jax.shard_map(
        make_body(mesh.shape["dp"], mesh.shape["tensor"]),
        mesh=mesh,
        in_specs=(rows, rows, P("dp")) + matrices + (P(), P()) + matrices + (P(),),
        out_specs=(rows, rows) + matrices + (P(),) + matrices + (P(),),
        check_vma=False,
    )
```

```python
import jax
import jax.numpy as jnp
from jax import lax
from jax.experimental import pallas as pl
from jax.experimental.pallas import tpu as pltpu
from jax.sharding import PartitionSpec as P

HD = 64
BOTH = ("dp", "tensor")
F32 = jnp.float32
BF16 = jnp.bfloat16
MESH = pl.DeviceIdType.MESH
NCH = 9
HALF = 48


class Place:
    def __init__(self):
        d, t = lax.axis_index("dp"), lax.axis_index("tensor")
        self.x, self.z = lax.rem(d, 2), lax.div(d, 2)
        self.c, self.y = lax.rem(t, 2), lax.div(t, 2)
        self.core = (d, t + 1 - 2 * self.c)
        self.ynb = (d, lax.rem(t + 2, 4))
        self.xnb = (d + 1 - 2 * self.x, t)
        self.zup = (lax.rem(d + 2, 8), t)
        self.zdn = (lax.rem(d + 6, 8), t)

    def zrel(self, s):
        return lax.rem(self.z + 4 - s, 4)

    def barrier(self):
        bar = pltpu.get_barrier_semaphore()
        near = (self.core, self.ynb, self.xnb, self.zup, self.zdn)
        for dev in near:
            pl.semaphore_signal(bar, inc=1, device_id=dev, device_id_type=MESH)
        pl.semaphore_wait(bar, len(near))


class Gather:
    def __init__(self, p, own, w, ss, rs):
        self.p, self.own, self.w, self.ss, self.rs = p, own, w, ss, rs

    def copy(self, src, dst, n, k, dev):
        return pltpu.make_async_remote_copy(
            src, dst, send_sem=self.ss.at[n, k], recv_sem=self.rs.at[n, k], device_id=dev, device_id_type=MESH
        )

    def part(self, n, k):
        p, w = self.p, self.w
        x, y, c, z = p.x, p.y, p.c, p.z
        lo, hi = pl.ds(0, HALF), pl.ds(HALF, HALF)
        if k < 3:
            src = self.own.at[n] if k == 0 else w.at[n, y, c, p.zrel(k), x]
            return src, w.at[n, y, c, p.zrel(k), x], w.at[n, y, c, p.zrel(k + 1), x], p.zup
        line = lambda yy, cc, xx: w.at[n, yy, cc, :, xx]
        if k == 3:
            return line(y, c, x), line(y, c, x), line(y, c, 1 - x), p.xnb
        if k == 4:
            return line(y, c, x), line(y, c, x), line(1 - y, c, x), p.ynb
        if k == 5:
            return line(y, c, x), line(y, c, x), line(y, 1 - c, x), p.core
        if k == 6:
            s = w.at[n, y, c, :, 1 - x, lo]
            return s, s, w.at[n, 1 - y, c, :, 1 - x, lo], p.ynb
        if k == 7:
            return line(y, c, 1 - x), line(y, c, 1 - x), line(y, 1 - c, 1 - x), p.core
        if k == 8:
            s = w.at[n, 1 - y, c, :, x, hi]
            return s, s, w.at[n, 1 - y, c, :, 1 - x, hi], p.xnb
        if k == 9:
            return line(1 - y, c, x), line(1 - y, c, x), line(1 - y, 1 - c, x), p.core
        return line(1 - y, c, 1 - x), line(1 - y, c, 1 - x), line(1 - y, 1 - c, 1 - x), p.core

    def start(self, n, k):
        src, dst, _, dev = self.part(n, k)
        self.copy(src, dst, n, k, dev).start()

    def arrive(self, n, k):
        _, _, mine, dev = self.part(n, k)
        self.copy(mine, mine, n, k, dev).wait_recv()

    def sent(self, n, k):
        src, dst, _, dev = self.part(n, k)
        self.copy(src, dst, n, k, dev).wait_send()

    def stage(self, n, s):
        if s == 0:
            self.start(n, 0)
        elif s < 3:
            self.arrive(n, s - 1)
            self.start(n, s)
        elif s == 3:
            self.arrive(n, 2)
            for k in (3, 4, 5):
                self.start(n, k)
        elif s == 4:
            self.arrive(n, 3)
            self.start(n, 6)
            self.start(n, 7)
            self.arrive(n, 4)
            self.start(n, 8)
            self.start(n, 9)
        elif s == 5:
            self.arrive(n, 6)
            self.arrive(n, 8)
            self.start(n, 10)
        else:
            for k in (5, 7, 9, 10):
                self.arrive(n, k)

    STAGES = 7
    COPIES = 11

    def finish(self, n):
        for k in range(self.COPIES):
            self.sent(n, k)


class Scatter:
    STAGES = 7
    COPIES = 8

    def __init__(self, p, g, out, rc, rd, rl, rz, ss, rs):
        self.p, self.g, self.out, self.rc, self.rd, self.rl, self.rz = p, g, out, rc, rd, rl, rz
        self.ss, self.rs = ss, rs

    def part(self, n, k):
        p, g = self.p, self.g
        x, y, c = p.x, p.y, p.c
        lo, hi = pl.ds(0, HALF), pl.ds(HALF, HALF)
        if k == 0:
            return g.at[n, :, 1 - c], self.rc.at[n], p.core
        if k == 1:
            return g.at[n, 1 - y, c, :, 1 - x, lo], self.rd.at[n, 0], p.ynb
        if k == 2:
            return g.at[n, 1 - y, c, :, 1 - x, hi], self.rd.at[n, 1], p.xnb
        if k == 3:
            return g.at[n, y, c, :, 1 - x], self.rl.at[n, 0], p.xnb
        if k == 4:
            return g.at[n, 1 - y, c, :, x], self.rl.at[n, 1], p.ynb
        return g.at[n, y, c, p.zrel(k - 4), x], self.rz.at[n, k - 5], p.zup

    def copy(self, n, k):
        src, dst, dev = self.part(n, k)
        return pltpu.make_async_remote_copy(
            src, dst, send_sem=self.ss.at[n, k], recv_sem=self.rs.at[n, k], device_id=dev, device_id_type=MESH
        )

    def start(self, n, k):
        self.copy(n, k).start()

    def arrive(self, n, k):
        self.copy(n, k).wait_recv()

    def finish(self, n):
        for k in range(self.COPIES):
            self.copy(n, k).wait_send()

    def add(self, ref, *others):
        total = ref[...].astype(F32)
        for o in others:
            total += o[...].astype(F32)
        ref[...] = total.astype(BF16)

    def stage(self, n, s):
        p, g = self.p, self.g
        x, y, c = p.x, p.y, p.c
        lo, hi = pl.ds(0, HALF), pl.ds(HALF, HALF)
        if s == 0:
            self.start(n, 0)
        elif s == 1:
            self.arrive(n, 0)
            self.add(g.at[n, 1 - y, c, :, 1 - x], self.rc.at[n, 1 - y, :, 1 - x])
            self.start(n, 1)
            self.start(n, 2)
            self.add(g.at[n, y, c], self.rc.at[n, y])
            self.add(g.at[n, 1 - y, c, :, x], self.rc.at[n, 1 - y, :, x])
        elif s == 2:
            self.arrive(n, 1)
            self.add(g.at[n, y, c, :, 1 - x, lo], self.rd.at[n, 0])
            self.start(n, 3)
            self.arrive(n, 2)
            self.add(g.at[n, 1 - y, c, :, x, hi], self.rd.at[n, 1])
            self.start(n, 4)
        elif s == 3:
            self.arrive(n, 3)
            self.arrive(n, 4)
            self.add(g.at[n, y, c, :, x], self.rl.at[n, 0], self.rl.at[n, 1])
            self.start(n, 5)
        elif s < 6:
            self.arrive(n, s + 1)
            self.add(g.at[n, y, c, p.zrel(s - 2), x], self.rz.at[n, s - 4])
            self.start(n, s + 2)
        else:
            self.arrive(n, 7)
            self.out[n] = g[n, y, c, p.z, x].astype(F32) + self.rz[n, 2].astype(F32)


WSHAPE = (NCH, 2, 2, 4, 2, 96, 256)


def scatter_scratch():
    return [
        pltpu.VMEM((NCH, 2, 4, 2, 96, 256), BF16),
        pltpu.VMEM((NCH, 2, 4, HALF, 256), BF16),
        pltpu.VMEM((NCH, 2, 4, 96, 256), BF16),
        pltpu.VMEM((NCH, 3, 96, 256), BF16),
        pltpu.SemaphoreType.DMA((NCH, Scatter.COPIES)),
        pltpu.SemaphoreType.DMA((NCH, Scatter.COPIES)),
    ]


def wave(engine, count, depth):
    for tick in range(count + engine.STAGES - 1):
        for s in reversed(range(engine.STAGES)):
            n = tick - s
            if 0 <= n < count:
                engine.stage(n, s)


def gather_kernel(own, w, ss, rs):
    p = Place()
    p.barrier()
    gather = Gather(p, own, w, ss, rs)
    for n in range(NCH):
        w[n, p.y, p.c, p.z, p.x] = own[n]
    wave(gather, NCH, 1)
    for n in range(NCH):
        gather.finish(n)


def scatter_kernel(g_in, out, g, rc, rd, rl, rz, ss, rs, ls):
    p = Place()
    local = pltpu.make_async_copy(g_in, g, ls)
    local.start()
    p.barrier()
    local.wait()
    engine = Scatter(p, g, out, rc, rd, rl, rz, ss, rs)
    wave(engine, NCH, 1)
    for n in range(NCH):
        engine.finish(n)


def gather_call(own):
    return pl.pallas_call(
        gather_kernel,
        out_shape=jax.ShapeDtypeStruct(WSHAPE, BF16),
        in_specs=[pl.BlockSpec(memory_space=pltpu.VMEM)],
        out_specs=pl.BlockSpec(memory_space=pltpu.VMEM),
        scratch_shapes=[pltpu.SemaphoreType.DMA((NCH, Gather.COPIES)), pltpu.SemaphoreType.DMA((NCH, Gather.COPIES))],
        compiler_params=pltpu.CompilerParams(collective_id=0, has_side_effects=True, vmem_limit_bytes=60 << 20),
    )(own)


def scatter_call(g):
    return pl.pallas_call(
        scatter_kernel,
        out_shape=jax.ShapeDtypeStruct((NCH, 96, 256), F32),
        in_specs=[pl.BlockSpec(memory_space=pl.ANY)],
        out_specs=pl.BlockSpec(memory_space=pltpu.VMEM),
        scratch_shapes=[pltpu.VMEM(WSHAPE, BF16)] + scatter_scratch() + [pltpu.SemaphoreType.DMA],
        compiler_params=pltpu.CompilerParams(collective_id=1, has_side_effects=True, vmem_limit_bytes=60 << 20),
    )(g)


def to_chunks(blocks):
    b, r, c = blocks.shape
    cut = blocks.reshape(b, r, 3, c // 3).transpose(0, 2, 1, 3)
    return jnp.concatenate([cut[0], cut[1:].transpose(1, 0, 2, 3).reshape(6, r, c // 3)])


def from_chunks(chunks):
    r, c = chunks.shape[1:]
    rest = chunks[3:].reshape(3, 2, r, c).transpose(1, 0, 2, 3)
    return jnp.concatenate([chunks[None, :3], rest]).transpose(0, 2, 1, 3).reshape(3, r, 3 * c)


def ring_gather(shards):
    w = gather_call(to_chunks(shards))
    w = w.reshape(NCH, 4, 768, 256)
    return jnp.stack([from_chunks(w[:, t]) for t in range(4)], axis=1)


def ring_scatter(blocks):
    g = jnp.stack([to_chunks(blocks[:, t]) for t in range(4)], axis=1)
    return from_chunks(scatter_call(g.reshape(WSHAPE)))


def unpack(vectors, d, ff):
    cuts = [d * i for i in range(8)] + [7 * d + ff, 8 * d + ff]
    return tuple(vectors[a:b] for a, b in zip(cuts[:-1], cuts[1:]))


def norm_parts(values):
    centred = values - jnp.mean(values, axis=-1, keepdims=True)
    inverse = lax.rsqrt(jnp.mean(centred * centred, axis=-1, keepdims=True) + 1e-06)
    return centred * inverse, inverse


def norm_backward(grad_normed, scaled, inverse, gain):
    weighted = grad_normed * gain
    return inverse * (
        weighted
        - jnp.mean(weighted, axis=-1, keepdims=True)
        - scaled * jnp.mean(weighted * scaled, axis=-1, keepdims=True)
    )


def gelu_parts(v):
    cdf = 0.5 * (1.0 + lax.erf(v * (0.5**0.5)))
    return v * cdf, cdf + v * jnp.exp(-0.5 * v * v) * ((2.0 * jnp.pi) ** -0.5)


def dot(a, b, dims):
    return lax.dot_general(a, b, (dims, ((), ())), preferred_element_type=F32)


def pack_shards(qkv, out, up, down):
    first = jnp.concatenate([qkv[0], qkv[1], qkv[2], out.T], axis=1)
    return jnp.stack([first, up, down.T])


def gather_blocks(shards, dp, tensor):
    every = lax.all_gather(shards, BOTH, axis=0)
    b, r, c = shards.shape
    every = every.reshape(dp, tensor, b, r, c).transpose(2, 1, 0, 3, 4)
    return every.reshape(b, tensor, dp * r, c)


def scatter_blocks(blocks, dp, tensor):
    b, t, rows, c = blocks.shape
    r = rows // dp
    pieces = blocks.reshape(b, tensor, dp, r, c).transpose(2, 1, 0, 3, 4)
    pieces = pieces.reshape(dp * tensor, b, r, c)
    return lax.psum_scatter(pieces, BOTH, scatter_dimension=0, tiled=True)[0]


def local_layer(tokens, cotangent, patches, blocks, vectors):
    rows, d = tokens.shape
    tensor, c = blocks.shape[1], blocks.shape[3]
    w = c // 4
    ff = tensor * c
    heads = d // HD
    gain1, bias1, gain2, bias2, bias_q, bias_v, bias_out, bias_up, bias_down = unpack(
        vectors, d, ff
    )
    first, up, downt = blocks[0], blocks[1], blocks[2]
    factor = HD**-0.5

    x = tokens.astype(F32)
    scaled1, inverse1 = norm_parts(x)
    normed1 = (scaled1 * gain1 + bias1).astype(BF16)
    mixed = jnp.einsum("rd,tdc->rtc", normed1, first[:, :, : 3 * w], preferred_element_type=F32)
    query = (mixed[:, :, :w].reshape(rows, d) + bias_q).astype(BF16).reshape(rows, heads, HD)
    key = mixed[:, :, w : 2 * w].reshape(rows, d).astype(BF16).reshape(rows, heads, HD)
    value = (mixed[:, :, 2 * w :].reshape(rows, d) + bias_v).astype(BF16).reshape(rows, heads, HD)
    images = jnp.arange(rows, dtype=jnp.int32) // patches
    allowed = images[:, None] == images[None, :]
    scores = jnp.einsum("qhd,khd->hqk", query, key, preferred_element_type=F32) * factor
    scores = jnp.where(allowed[None], scores, -1e30)
    raised = jnp.exp(scores - jnp.max(scores, axis=-1, keepdims=True))
    soft = raised / jnp.sum(raised, axis=-1, keepdims=True)
    soft_low = soft.astype(BF16)
    attended = jnp.einsum("hqk,khd->qhd", soft_low, value, preferred_element_type=F32).astype(BF16)
    flat = attended.reshape(rows, tensor, w)
    outt = first[:, :, 3 * w :]
    residual = x + jnp.einsum("rte,tde->rd", flat, outt, preferred_element_type=F32) + bias_out
    scaled2, inverse2 = norm_parts(residual)
    normed2 = (scaled2 * gain2 + bias2).astype(BF16)
    pre = jnp.einsum("rd,tdf->rtf", normed2, up, preferred_element_type=F32) + bias_up.reshape(
        tensor, c
    )
    active, slope = gelu_parts(pre)
    active = active.astype(BF16)
    second = jnp.einsum("rtf,tdf->rd", active, downt, preferred_element_type=F32)
    output = (residual + second + bias_down).astype(BF16)

    grad_active = jnp.einsum("rd,tdf->rtf", cotangent, downt, preferred_element_type=F32)
    grad_pre = (grad_active * slope).astype(BF16)
    g_down = jnp.einsum("rd,rtf->tdf", cotangent, active, preferred_element_type=F32)
    g_up = jnp.einsum("rd,rtf->tdf", normed2, grad_pre, preferred_element_type=F32)
    grad_normed2 = jnp.einsum("rtf,tdf->rd", grad_pre, up, preferred_element_type=F32)
    grad_result = cotangent.astype(F32)
    grad_residual = grad_result + norm_backward(grad_normed2, scaled2, inverse2, gain2)
    grad_branch = grad_residual.astype(BF16)
    g_outt = jnp.einsum("rd,rte->tde", grad_branch, flat, preferred_element_type=F32)
    grad_att = jnp.einsum("rd,tde->rte", grad_branch, outt, preferred_element_type=F32)
    grad_att = grad_att.astype(BF16).reshape(rows, heads, HD)
    grad_value = jnp.einsum("hqk,qhd->khd", soft_low, grad_att, preferred_element_type=F32)
    grad_soft = jnp.einsum("qhd,khd->hqk", grad_att, value, preferred_element_type=F32)
    grad_scores = (
        soft * (grad_soft - jnp.sum(soft * grad_soft, axis=-1, keepdims=True))
    ).astype(BF16)
    grad_query = (
        jnp.einsum("hqk,khd->qhd", grad_scores, key, preferred_element_type=F32) * factor
    )
    grad_key = jnp.einsum("hqk,qhd->khd", grad_scores, query, preferred_element_type=F32) * factor
    three = [
        g.astype(BF16).reshape(rows, tensor, w) for g in (grad_query, grad_key, grad_value)
    ]
    grad_mixed = jnp.concatenate(three, axis=2)
    g_qkv = jnp.einsum("rd,rtc->tdc", normed1, grad_mixed, preferred_element_type=F32)
    grad_normed1 = jnp.einsum(
        "rtc,tdc->rd", grad_mixed, first[:, :, : 3 * w], preferred_element_type=F32
    )
    grad_tokens = (grad_residual + norm_backward(grad_normed1, scaled1, inverse1, gain1)).astype(
        BF16
    )
    grads = jnp.stack(
        [
            jnp.concatenate([g_qkv, g_outt], axis=2).astype(BF16),
            g_up.astype(BF16),
            g_down.astype(BF16),
        ]
    )

    def total(values):
        return jnp.sum(values.astype(F32), axis=0).reshape(-1)

    sums = jnp.concatenate(
        [
            total(grad_normed1 * scaled1),
            total(grad_normed1),
            total(grad_normed2 * scaled2),
            total(grad_normed2),
            total(three[0]),
            total(three[2]),
            total(grad_residual),
            total(grad_pre),
            total(grad_result),
        ]
    )
    return output, grad_tokens, grads, sums


def make_body(dp, tensor):
    def body(
        tokens,
        cotangent,
        block_patches,
        qkv,
        out,
        up,
        down,
        vectors,
        momentum,
        target_qkv,
        target_out,
        target_up,
        target_down,
        target_vectors,
    ):
        patches = block_patches[lax.axis_index("tensor")]
        ringed = dp == 8 and tensor == 4
        shards = pack_shards(qkv, out, up, down)
        blocks = ring_gather(shards) if ringed else gather_blocks(shards, dp, tensor)
        output, grad_tokens, grads, sums = local_layer(
            tokens, cotangent, patches, blocks, vectors
        )
        grads = ring_scatter(grads) if ringed else scatter_blocks(grads, dp, tensor).astype(F32)
        sums = lax.psum(sums, BOTH)
        w = qkv.shape[2]
        rate = momentum[0]

        def average(target, online):
            return rate * target + (1.0 - rate) * online.astype(F32)

        return (
            output,
            grad_tokens,
            jnp.stack([grads[0][:, i * w : (i + 1) * w] for i in range(3)]),
            grads[0][:, 3 * w :].T,
            grads[1],
            grads[2].T,
            sums,
            average(target_qkv, qkv),
            average(target_out, out),
            average(target_up, up),
            average(target_down, down),
            average(target_vectors, vectors),
        )

    return body


def solution(mesh):
    rows, matrices = P(BOTH, None), (
        P(None, "dp", "tensor"),
        P("tensor", "dp"),
        P("dp", "tensor"),
        P("tensor", "dp"),
    )
    return jax.shard_map(
        make_body(mesh.shape["dp"], mesh.shape["tensor"]),
        mesh=mesh,
        in_specs=(rows, rows, P("dp")) + matrices + (P(), P()) + matrices + (P(),),
        out_specs=(rows, rows) + matrices + (P(),) + matrices + (P(),),
        check_vma=False,
    )
```

```python
import functools
import math

import jax
import jax.numpy as jnp
from jax import lax
from jax.experimental import pallas as pl
from jax.experimental.pallas import tpu as pltpu
from jax.sharding import PartitionSpec as P

F32 = jnp.float32
BF16 = jnp.bfloat16
MESH = pl.DeviceIdType.MESH
NCH = 9
HALF = 48


class Place:
    def __init__(self):
        d, t = lax.axis_index("dp"), lax.axis_index("tensor")
        self.x, self.z = lax.rem(d, 2), lax.div(d, 2)
        self.c, self.y = lax.rem(t, 2), lax.div(t, 2)
        self.core = (d, t + 1 - 2 * self.c)
        self.ynb = (d, lax.rem(t + 2, 4))
        self.xnb = (d + 1 - 2 * self.x, t)
        self.zup = (lax.rem(d + 2, 8), t)
        self.zdn = (lax.rem(d + 6, 8), t)
        self.zfar = (lax.rem(d + 4, 8), t)
        self.zpair = self.z + 1 - 2 * lax.rem(self.z, 2)

    def zrel(self, s):
        return lax.rem(self.z + 4 - s, 4)

    def barrier(self):
        bar = pltpu.get_barrier_semaphore()
        near = (self.core, self.ynb, self.xnb, self.zup, self.zdn, self.zfar)
        for dev in near:
            pl.semaphore_signal(bar, inc=1, device_id=dev, device_id_type=MESH)
        pl.semaphore_wait(bar, len(near))


class Gather:
    def __init__(self, p, own, w, ss, rs):
        self.p, self.own, self.w, self.ss, self.rs = p, own, w, ss, rs

    def copy(self, src, dst, n, k, dev):
        return pltpu.make_async_remote_copy(
            src, dst, send_sem=self.ss.at[n, k], recv_sem=self.rs.at[n, k], device_id=dev, device_id_type=MESH
        )

    def part(self, n, k):
        p, w = self.p, self.w
        x, y, c, z = p.x, p.y, p.c, p.z
        lo, hi = pl.ds(0, HALF), pl.ds(HALF, HALF)
        if k < 3:
            src = self.own.at[n] if k == 0 else w.at[n, y, c, p.zrel(k), x]
            return src, w.at[n, y, c, p.zrel(k), x], w.at[n, y, c, p.zrel(k + 1), x], p.zup
        line = lambda yy, cc, xx: w.at[n, yy, cc, :, xx]
        if k == 3:
            return line(y, c, x), line(y, c, x), line(y, c, 1 - x), p.xnb
        if k == 4:
            return line(y, c, x), line(y, c, x), line(1 - y, c, x), p.ynb
        if k == 5:
            return line(y, c, x), line(y, c, x), line(y, 1 - c, x), p.core
        if k == 6:
            s = w.at[n, y, c, :, 1 - x, lo]
            return s, s, w.at[n, 1 - y, c, :, 1 - x, lo], p.ynb
        if k == 7:
            return line(y, c, 1 - x), line(y, c, 1 - x), line(y, 1 - c, 1 - x), p.core
        if k == 8:
            s = w.at[n, 1 - y, c, :, x, hi]
            return s, s, w.at[n, 1 - y, c, :, 1 - x, hi], p.xnb
        if k == 9:
            return line(1 - y, c, x), line(1 - y, c, x), line(1 - y, 1 - c, x), p.core
        return line(1 - y, c, 1 - x), line(1 - y, c, 1 - x), line(1 - y, 1 - c, 1 - x), p.core

    def start(self, n, k):
        src, dst, _, dev = self.part(n, k)
        self.copy(src, dst, n, k, dev).start()

    def arrive(self, n, k):
        _, _, mine, dev = self.part(n, k)
        self.copy(mine, mine, n, k, dev).wait_recv()

    def sent(self, n, k):
        src, dst, _, dev = self.part(n, k)
        self.copy(src, dst, n, k, dev).wait_send()

    def stage(self, n, s):
        if s == 0:
            self.start(n, 0)
        elif s < 3:
            self.arrive(n, s - 1)
            self.start(n, s)
        elif s == 3:
            self.arrive(n, 2)
            for k in (3, 4, 5):
                self.start(n, k)
        elif s == 4:
            self.arrive(n, 3)
            self.start(n, 6)
            self.start(n, 7)
            self.arrive(n, 4)
            self.start(n, 8)
            self.start(n, 9)
        elif s == 5:
            self.arrive(n, 6)
            self.arrive(n, 8)
            self.start(n, 10)
        else:
            for k in (5, 7, 9, 10):
                self.arrive(n, k)

    STAGES = 7
    COPIES = 11

    def finish(self, n):
        for k in range(self.COPIES):
            self.sent(n, k)


class Scatter:
    STAGES = 7
    COPIES = 8

    def __init__(self, p, g, out, rc, rd, rl, rz, ss, rs):
        self.p, self.g, self.out, self.rc, self.rd, self.rl, self.rz = p, g, out, rc, rd, rl, rz
        self.ss, self.rs = ss, rs

    def part(self, m, k):
        p, g = self.p, self.g
        n, o = self.chunk(m), lax.rem(m, 2)
        x, y, c = p.x, p.y, p.c
        lo, hi = pl.ds(0, HALF), pl.ds(HALF, HALF)
        if k == 0:
            return g.at[n, :, 1 - c], self.rc.at[o], p.core
        if k == 1:
            return g.at[n, 1 - y, c, :, 1 - x, lo], self.rd.at[o, 0], p.ynb
        if k == 2:
            return g.at[n, 1 - y, c, :, 1 - x, hi], self.rd.at[o, 1], p.xnb
        if k == 3:
            return g.at[n, y, c, :, 1 - x], self.rl.at[o, 0], p.xnb
        if k == 4:
            return g.at[n, 1 - y, c, :, x], self.rl.at[o, 1], p.ynb
        return g.at[n, y, c, p.zrel(k - 4), x], self.rz.at[m, k - 5], p.zup

    def copy(self, m, k):
        src, dst, dev = self.part(m, k)
        return pltpu.make_async_remote_copy(
            src, dst, send_sem=self.ss.at[m, k], recv_sem=self.rs.at[m, k], device_id=dev, device_id_type=MESH
        )

    def start(self, m, k):
        self.copy(m, k).start()

    def arrive(self, m, k):
        self.copy(m, k).wait_recv()

    def finish(self, m):
        for k in range(self.COPIES):
            self.copy(m, k).wait_send()

    def add(self, ref, *others):
        total = ref[...].astype(F32)
        for o in others:
            total += o[...].astype(F32)
        ref[...] = total.astype(BF16)

    def chunk(self, m):
        return lax.rem(m + 3, NCH)

    def stage(self, m, s):
        p, g = self.p, self.g
        n, o = self.chunk(m), lax.rem(m, 2)
        x, y, c = p.x, p.y, p.c
        lo, hi = pl.ds(0, HALF), pl.ds(HALF, HALF)
        if s == 0:
            self.start(m, 0)
        elif s == 1:
            self.arrive(m, 0)
            self.add(g.at[n, 1 - y, c, :, 1 - x], self.rc.at[o, 1 - y, :, 1 - x])
            self.start(m, 1)
            self.start(m, 2)
            self.add(g.at[n, y, c], self.rc.at[o, y])
            self.add(g.at[n, 1 - y, c, :, x], self.rc.at[o, 1 - y, :, x])
        elif s == 2:
            self.arrive(m, 1)
            self.add(g.at[n, y, c, :, 1 - x, lo], self.rd.at[o, 0])
            self.start(m, 3)
            self.arrive(m, 2)
            self.add(g.at[n, 1 - y, c, :, x, hi], self.rd.at[o, 1])
            self.start(m, 4)
        elif s == 3:
            self.arrive(m, 3)
            self.arrive(m, 4)
            self.add(g.at[n, y, c, :, x], self.rl.at[o, 0], self.rl.at[o, 1])
            self.start(m, 5)
        elif s < 6:
            self.arrive(m, s + 1)
            self.add(g.at[n, y, c, p.zrel(s - 2), x], self.rz.at[m, s - 4])
            self.start(m, s + 2)
        else:
            self.arrive(m, 7)
            self.out[n] = g[n, y, c, p.z, x].astype(F32) + self.rz[m, 2].astype(F32)


WSHAPE = (NCH, 2, 2, 4, 2, 96, 256)
ROWS = 784
DM = 768
PARTS = ((0, 400), (400, 384))
STEP = 112
LOG2E = math.log2(math.e)
CS = LOG2E / 8
BIG = 1e30


def nt(a, b):
    return lax.dot_general(a, b, (((1,), (1,)), ((), ())), preferred_element_type=F32)


def tn(a, b):
    return lax.dot_general(a, b, (((0,), (0,)), ((), ())), preferred_element_type=F32)


def nn(a, b):
    return jnp.dot(a, b, preferred_element_type=F32)


def split3(a):
    one = a.astype(BF16)
    rest = a - one.astype(F32)
    two = rest.astype(BF16)
    return one, two, (rest - two.astype(F32)).astype(BF16)


def turn(a):
    return pltpu.roll(a.astype(F32), 64, 1)


def standard(values):
    centred = values - jnp.mean(values, axis=-1, keepdims=True)
    inverse = lax.rsqrt(jnp.mean(centred * centred, axis=-1, keepdims=True) + 1e-06)
    return centred * inverse, inverse


def norm_pull(grad, scaled, inverse, gain):
    g = grad * gain
    return inverse * (
        g - jnp.mean(g, axis=-1, keepdims=True) - scaled * jnp.mean(g * scaled, axis=-1, keepdims=True)
    )


def gelu_slope(v):
    cdf = 0.5 + 0.5 * lax.erf(v * math.sqrt(0.5))
    return v * cdf, cdf + v * (jnp.exp(-0.5 * v * v) * (1.0 / math.sqrt(2.0 * math.pi)))


def rows_of(i):
    return pl.ds(pl.multiple_of(i * STEP, 16), STEP)


def fold(values):
    return jnp.sum(values.reshape(STEP // 8, 8, values.shape[1]), axis=0)


class Layer:
    def __init__(self, refs):
        self.__dict__.update(refs)

    def mat(self, n, y, c):
        return self.w[n, y, c].reshape(DM, 256)

    def put(self, n, y, c, value):
        self.w[n, y, c] = value.astype(BF16).reshape(4, 2, 96, 256)

    def masks(self):
        row = lax.broadcasted_iota(jnp.int32, (ROWS, 128), 0)
        lane = lax.broadcasted_iota(jnp.int32, (ROWS, 128), 1)
        p = jnp.broadcast_to(self.pat[0:1, :], (ROWS, 128))
        image = sum(jnp.where(row >= k * p, 1, 0) for k in (1, 2, 3))
        same = jnp.where(image == lane - 64, 1.0, 0.0)
        slot = (lane >= 64) & (lane < 68)
        self.mq[...] = jnp.where(slot, (same - 1.0) * BIG, 0.0).astype(BF16)
        self.mk[...] = jnp.where(slot, same, jnp.where((lane >= 68) & (lane < 71), 1.0, 0.0)).astype(BF16)

    def norm1(self):
        def step(i, _):
            r = rows_of(i)
            scaled, _ = standard(self.tok[r, :].astype(F32))
            self.n1[r, :] = (scaled * self.vec[0:1, :] + self.vec[1:2, :]).astype(BF16)
            return 0

        lax.fori_loop(0, ROWS // STEP, step, 0)

    def attend(self, i):
        j, y = lax.div(i, 2), lax.rem(i, 2)
        lane = lax.broadcasted_iota(jnp.int32, (ROWS, 128), 1)
        left = lane < 64
        out_halves = []
        for c in range(2):
            h = i * 2 + c
            mixed = (nn(self.n1[...], self.mat(j, y, c)) + self.bias[h]).astype(BF16)
            self.qa[h] = jnp.where(left, mixed[:, :128], self.mq[...])
            self.ka[h] = jnp.where(left, mixed[:, 128:], self.mk[...])
            self.va[h] = jnp.where(left, jnp.ones((), BF16), mixed[:, :128])
            out_halves.append(self.mat(j, y, c)[:, 128:])
        first = lax.broadcasted_iota(jnp.int32, (DM, 128), 1) < 64
        self.ot[j, y] = jnp.where(first, turn(out_halves[0]), out_halves[1].astype(F32)).astype(BF16)
        for r0, n in PARTS:
            r = pl.ds(r0, n)
            lanes = lax.broadcasted_iota(jnp.int32, (n, 128), 1)
            results = []
            for c in range(2):
                h = i * 2 + c
                q = self.qa[h, r, :]
                s = nt(q, self.ka[h])
                top = jnp.max(s, axis=1, keepdims=True) * CS
                p = jnp.exp2(s * CS - top).astype(BF16)
                a = nn(p, self.va[h])
                total = pltpu.roll(a, 64, 1)
                results.append(a * (1.0 / total))
                h1, h2, h3 = split3((top + jnp.log2(total)) * (-1.0 / CS))
                self.qa[h, r, :] = jnp.where(
                    lanes == 68, h1, jnp.where(lanes == 69, h2, jnp.where(lanes == 70, h3, q))
                )
            pair = jnp.where(lanes < 64, pltpu.roll(results[0], 64, 1), results[1])
            self.att[j, y, r, :] = pair.astype(BF16)

    def pair(self, ref, j, r=slice(None)):
        return jnp.concatenate([ref[j, 0, r, :], ref[j, 1, r, :]], axis=1)

    def project(self):
        for r0, n in PARTS:
            r = pl.ds(r0, n)
            total = sum(nt(self.pair(self.att, j, r), self.pair(self.ot, j)) for j in range(3))
            self.res[r, :] = total + (self.tok[r, :].astype(F32) + self.vec[6:7, :])

        def step(i, _):
            r = rows_of(i)
            v = self.res[r, :]
            scaled, _ = standard(v)
            self.n2[r, :] = (scaled * self.vec[2:3, :] + self.vec[3:4, :]).astype(BF16)
            self.acc[r, :] = v + self.vec[11:12, :]
            self.gn[r, :] = jnp.zeros((STEP, DM), F32)
            return 0

        lax.fori_loop(0, ROWS // STEP, step, 0)

    def feed(self, i):
        j, y = lax.div(i, 2), lax.rem(i, 2)
        nb, nc = 3 + 2 * j, 4 + 2 * j
        sums = [0.0, 0.0]
        for r0, n in PARTS:
            r = pl.ds(r0, n)
            for c in range(2):
                cols = slice(c * 256, c * 256 + 256)
                pre = nn(self.n2[r, :], self.mat(nb, y, c)) + self.bias[12 + i * 2 + c]
                up = nn(self.cot[r, :], self.mat(nc, y, c))
                active, slope = gelu_slope(pre)
                grad = (up * slope).astype(BF16)
                self.act[r, cols] = active.astype(BF16)
                self.gp[r, cols] = grad
                sums[c] += jnp.sum(grad.astype(F32).reshape(n // 8, 8, 256), axis=0)
            self.acc[r, :] += nt(self.act[r, 0:256], self.mat(nc, y, 0)) + nt(
                self.act[r, 256:512], self.mat(nc, y, 1)
            )
            self.gn[r, :] += nt(self.gp[r, 0:256], self.mat(nb, y, 0)) + nt(
                self.gp[r, 256:512], self.mat(nb, y, 1)
            )
        for c in range(2):
            cols = slice(c * 256, c * 256 + 256)
            self.hs[12 + i * 2 + c] = jnp.sum(sums[c], axis=0, keepdims=True)
            self.put(nc, y, c, tn(self.cot[...], self.act[:, cols]))
            self.put(nb, y, c, tn(self.n2[...], self.gp[:, cols]))

    def residual_back(self):
        self.vs[...] = jnp.zeros(self.vs.shape, F32)

        def step(i, _):
            r = rows_of(i)
            self.out[r, :] = self.acc[r, :].astype(BF16)
            scaled, inverse = standard(self.res[r, :])
            g = self.gn[r, :]
            ct = self.cot[r, :].astype(F32)
            grad = ct + norm_pull(g, scaled, inverse, self.vec[2:3, :])
            self.res[r, :] = grad
            self.gb[r, :] = grad.astype(BF16)
            self.gn[r, :] = jnp.zeros((STEP, DM), F32)
            for k, v in ((2, g * scaled), (3, g), (4, grad), (5, ct)):
                self.vs[k] += fold(v)
            return 0

        lax.fori_loop(0, ROWS // STEP, step, 0)

    def attend_back(self, i):
        j, y = lax.div(i, 2), lax.rem(i, 2)
        lane = lax.broadcasted_iota(jnp.int32, (ROWS, 128), 1)
        left = lane < 64
        low = nn(self.gb[...], self.ot[j, y]).astype(BF16)
        wide = low.astype(F32)
        product = wide * self.att[j, y].astype(F32)
        for c in range(2):
            h = i * 2 + c
            delta = jnp.sum(jnp.where(left == (c == 0), product, 0.0), axis=1, keepdims=True)
            d1, d2, d3 = split3(jnp.broadcast_to(-delta, (ROWS, 128)))
            moved = pltpu.roll(wide, 64, 1).astype(BF16) if c == 0 else low
            none = jnp.zeros((), BF16)
            extra = jnp.where(lane == 0, d1, jnp.where(lane == 1, d2, jnp.where(lane == 2, d3, none)))
            self.da[...] = jnp.where(left, extra, moved)
            dv = dk = 0.0
            for r0, n in PARTS:
                r = pl.ds(r0, n)
                q, d = self.qa[h, r, :], self.da[r, :]
                p = jnp.exp2(nt(q, self.ka[h]) * CS)
                ds = (p * nt(d, self.va[h])).astype(BF16)
                dv += tn(p.astype(BF16), d)
                dk += tn(ds, q)
                self.dq[c, r, 0:128] = (nn(ds, self.ka[h]) * 0.125).astype(BF16)
            self.dq[c, :, 0:128] = jnp.where(left, self.dq[c, :, 0:128], dv.astype(BF16))
            self.dq[c, :, 128:256] = jnp.where(left, (dk * 0.125).astype(BF16), none)
            sums = jnp.sum(self.dq[c].astype(F32).reshape(ROWS // 8, 8, 256), axis=0)
            self.hs[h] = jnp.sum(sums, axis=0, keepdims=True)
        for r0, n in PARTS:
            r = pl.ds(r0, n)
            self.gn[r, :] += nt(self.dq[0, r, :], self.mat(j, y, 0)) + nt(
                self.dq[1, r, :], self.mat(j, y, 1)
            )
        outg = tn(self.gb[...], self.att[j, y])
        first = lax.broadcasted_iota(jnp.int32, (DM, 128), 1) < 64
        for c in range(2):
            g = tn(self.n1[...], self.dq[c])
            mine = pltpu.roll(outg, 64, 1) if c == 0 else outg
            self.put(j, y, c, jnp.concatenate([g[:, :128], jnp.where(first, g[:, 128:], mine)], axis=1))

    def token_back(self):
        def step(i, _):
            r = rows_of(i)
            scaled, inverse = standard(self.tok[r, :].astype(F32))
            g = self.gn[r, :]
            grad = self.res[r, :] + norm_pull(g, scaled, inverse, self.vec[0:1, :])
            self.gtok[r, :] = grad.astype(BF16)
            self.vs[0] += fold(g * scaled)
            self.vs[1] += fold(g)
            return 0

        lax.fori_loop(0, ROWS // STEP, step, 0)

    def collect(self):
        for h in range(24):
            self.vsum[h : h + 1, :] = self.hs[h]
        for k in range(6):
            row = jnp.sum(self.vs[k], axis=0, keepdims=True)
            for b in range(3):
                self.vsum[24 + 3 * k + b : 25 + 3 * k + b, :] = row[:, 256 * b : 256 * b + 256]
        self.vsum[42:48, :] = jnp.zeros((6, 256), F32)


def layer_scratch():
    return dict(
        w=pltpu.VMEM(WSHAPE, BF16),
        n1=pltpu.VMEM((ROWS, DM), BF16),
        n2=pltpu.VMEM((ROWS, DM), BF16),
        gb=pltpu.VMEM((ROWS, DM), BF16),
        qa=pltpu.VMEM((12, ROWS, 128), BF16),
        ka=pltpu.VMEM((12, ROWS, 128), BF16),
        va=pltpu.VMEM((12, ROWS, 128), BF16),
        att=pltpu.VMEM((3, 2, ROWS, 128), BF16),
        ot=pltpu.VMEM((3, 2, DM, 128), BF16),
        res=pltpu.VMEM((ROWS, DM), F32),
        acc=pltpu.VMEM((ROWS, DM), F32),
        gn=pltpu.VMEM((ROWS, DM), F32),
        mq=pltpu.VMEM((ROWS, 128), BF16),
        mk=pltpu.VMEM((ROWS, 128), BF16),
        act=pltpu.VMEM((ROWS, 512), BF16),
        gp=pltpu.VMEM((ROWS, 512), BF16),
        da=pltpu.VMEM((ROWS, 128), BF16),
        dq=pltpu.VMEM((2, ROWS, 256), BF16),
        vs=pltpu.VMEM((6, 8, DM), F32),
        hs=pltpu.VMEM((24, 1, 256), F32),
    )


NAMES_IN = ("tok", "cot", "own", "vec", "bias", "pat")
NAMES_OUT = ("out", "gtok", "gsh", "vsum")


def slots_of(u):
    late = u - 7
    early_ok = (u >= 0) & (u <= 5)
    late_ok = (late >= 0) & (late <= 4) & (lax.rem(jnp.maximum(late, 0), 2) == 0)
    return jnp.where(early_ok, u, 6 + lax.div(jnp.maximum(late, 0), 2)), early_ok | late_ok


def gather_slot(gather, t):
    for s in reversed(range(gather.STAGES)):
        n = t - s
        if isinstance(t, int):
            if 0 <= n < NCH:
                gather.stage(n, s)
        else:
            pl.when((n >= 0) & (n < NCH))(functools.partial(gather.stage, n, s))


def scatter_slot(scatter, t):
    for s in reversed(range(scatter.STAGES)):
        m, ok = slots_of(t - s)
        pl.when(ok)(functools.partial(scatter.stage, m, s))


class Totals:
    def __init__(self, p, value, vr, ss, rs):
        self.p, self.value, self.vr, self.ss, self.rs = p, value, vr, ss, rs
        z1 = (lax.rem(p.zpair * 2 + p.x, 8), lax.axis_index("tensor"))
        self.devs = (p.core, p.ynb, p.xnb, z1, p.zfar)

    def copy(self, k):
        src = self.vr.at[0, k]
        return pltpu.make_async_remote_copy(
            src, self.vr.at[1, k], send_sem=self.ss.at[k], recv_sem=self.rs.at[k],
            device_id=self.devs[k], device_id_type=MESH,
        )

    def start(self, k, total):
        self.vr[0, k] = total
        self.copy(k).start()

    def end(self, k):
        self.copy(k).wait_recv()
        return self.vr[0, k] + self.vr[1, k]


def mega_kernel(names, *refs):
    r = dict(zip(names, refs))
    layer = Layer(r)
    p = Place()
    p.barrier()
    gather = Gather(p, r["own"], r["w"], r["gss"], r["grs"])
    scatter = Scatter(p, r["w"], r["gsh"], r["rc"], r["rd"], r["rl"], r["rz"], r["sss"], r["srs"])
    totals = Totals(p, r["vsum"], r["vr"], r["vss"], r["vrs"])

    for n in range(NCH):
        r["w"][n, p.y, p.c, p.z, p.x] = r["own"][n]
    gather_slot(gather, 0)
    layer.masks()
    gather_slot(gather, 1)
    layer.norm1()
    lax.fori_loop(2, 6, lambda t, c: (gather_slot(gather, t), c)[1], 0)

    def attend(i, _):
        pl.when(lax.rem(i, 2) == 0)(lambda: gather_slot(gather, 6 + lax.div(i, 2)))
        layer.attend(i)
        return 0

    lax.fori_loop(0, 6, attend, 0)
    gather_slot(gather, jnp.int32(9))
    layer.project()
    gather_slot(gather, jnp.int32(10))

    def feed(i, _):
        @pl.when(lax.rem(i, 2) == 0)
        def _():
            gather.finish(3 + i)
            gather.finish(4 + i)

        layer.feed(i)
        gather_slot(gather, 11 + i)
        scatter_slot(scatter, i - 1)
        return 0

    lax.fori_loop(0, 6, feed, 0)
    layer.residual_back()
    scatter_slot(scatter, jnp.int32(5))
    for n in range(3):
        gather.finish(n)

    def back(i, _):
        layer.attend_back(i)
        scatter_slot(scatter, 6 + i)
        return 0

    lax.fori_loop(0, 6, back, 0)
    layer.token_back()
    layer.collect()
    value = r["vsum"][...]
    scatter_slot(scatter, jnp.int32(12))
    for k in range(5):
        totals.start(k, value)
        scatter_slot(scatter, jnp.int32(13 + k))
        value = totals.end(k)
    r["vsum"][...] = value
    lax.fori_loop(0, NCH, lambda m, c: (scatter.finish(m), c)[1], 0)
    for k in range(5):
        totals.copy(k).wait_send()


def mega_scratch():
    two = 2
    return dict(
        layer_scratch(),
        rc=pltpu.VMEM((two, 2, 4, 2, 96, 256), BF16),
        rd=pltpu.VMEM((two, 2, 4, HALF, 256), BF16),
        rl=pltpu.VMEM((two, 2, 4, 96, 256), BF16),
        rz=pltpu.VMEM((NCH, 3, 96, 256), BF16),
        vr=pltpu.VMEM((2, 5, 48, 256), F32),
        gss=pltpu.SemaphoreType.DMA((NCH, Gather.COPIES)),
        grs=pltpu.SemaphoreType.DMA((NCH, Gather.COPIES)),
        sss=pltpu.SemaphoreType.DMA((NCH, Scatter.COPIES)),
        srs=pltpu.SemaphoreType.DMA((NCH, Scatter.COPIES)),
        vss=pltpu.SemaphoreType.DMA((5,)),
        vrs=pltpu.SemaphoreType.DMA((5,)),
    )


def mega_call(*args):
    scratch = mega_scratch()
    names = NAMES_IN + NAMES_OUT + tuple(scratch)
    vm = pl.BlockSpec(memory_space=pltpu.VMEM)
    shape = jax.ShapeDtypeStruct
    return pl.pallas_call(
        functools.partial(mega_kernel, names),
        out_shape=(
            shape((ROWS, DM), BF16),
            shape((ROWS, DM), BF16),
            shape((NCH, 96, 256), F32),
            shape((48, 256), F32),
        ),
        in_specs=[vm] * len(NAMES_IN),
        out_specs=(vm,) * len(NAMES_OUT),
        scratch_shapes=list(scratch.values()),
        compiler_params=pltpu.CompilerParams(collective_id=0, has_side_effects=True, vmem_limit_bytes=62 << 20),
    )(*args)


HD = 64
BOTH = ("dp", "tensor")


def unpack(vectors, d, ff):
    cuts = [d * i for i in range(8)] + [7 * d + ff, 8 * d + ff]
    return tuple(vectors[a:b] for a, b in zip(cuts[:-1], cuts[1:]))


def norm_parts(values):
    centred = values - jnp.mean(values, axis=-1, keepdims=True)
    inverse = lax.rsqrt(jnp.mean(centred * centred, axis=-1, keepdims=True) + 1e-06)
    return centred * inverse, inverse


def norm_backward(grad_normed, scaled, inverse, gain):
    weighted = grad_normed * gain
    return inverse * (
        weighted
        - jnp.mean(weighted, axis=-1, keepdims=True)
        - scaled * jnp.mean(weighted * scaled, axis=-1, keepdims=True)
    )


def gelu_parts(v):
    cdf = 0.5 * (1.0 + lax.erf(v * (0.5**0.5)))
    return v * cdf, cdf + v * jnp.exp(-0.5 * v * v) * ((2.0 * jnp.pi) ** -0.5)


def dot(a, b, dims):
    return lax.dot_general(a, b, (dims, ((), ())), preferred_element_type=F32)


def pack_shards(qkv, out, up, down):
    first = jnp.concatenate([qkv[0], qkv[1], qkv[2], out.T], axis=1)
    return jnp.stack([first, up, down.T])


def gather_blocks(shards, dp, tensor):
    every = lax.all_gather(shards, BOTH, axis=0)
    b, r, c = shards.shape
    every = every.reshape(dp, tensor, b, r, c).transpose(2, 1, 0, 3, 4)
    return every.reshape(b, tensor, dp * r, c)


def scatter_blocks(blocks, dp, tensor):
    b, t, rows, c = blocks.shape
    r = rows // dp
    pieces = blocks.reshape(b, tensor, dp, r, c).transpose(2, 1, 0, 3, 4)
    pieces = pieces.reshape(dp * tensor, b, r, c)
    return lax.psum_scatter(pieces, BOTH, scatter_dimension=0, tiled=True)[0]


def local_layer(tokens, cotangent, patches, blocks, vectors):
    rows, d = tokens.shape
    tensor, c = blocks.shape[1], blocks.shape[3]
    w = c // 4
    ff = tensor * c
    heads = d // HD
    gain1, bias1, gain2, bias2, bias_q, bias_v, bias_out, bias_up, bias_down = unpack(
        vectors, d, ff
    )
    first, up, downt = blocks[0], blocks[1], blocks[2]
    factor = HD**-0.5

    x = tokens.astype(F32)
    scaled1, inverse1 = norm_parts(x)
    normed1 = (scaled1 * gain1 + bias1).astype(BF16)
    mixed = jnp.einsum("rd,tdc->rtc", normed1, first[:, :, : 3 * w], preferred_element_type=F32)
    query = (mixed[:, :, :w].reshape(rows, d) + bias_q).astype(BF16).reshape(rows, heads, HD)
    key = mixed[:, :, w : 2 * w].reshape(rows, d).astype(BF16).reshape(rows, heads, HD)
    value = (mixed[:, :, 2 * w :].reshape(rows, d) + bias_v).astype(BF16).reshape(rows, heads, HD)
    images = jnp.arange(rows, dtype=jnp.int32) // patches
    allowed = images[:, None] == images[None, :]
    scores = jnp.einsum("qhd,khd->hqk", query, key, preferred_element_type=F32) * factor
    scores = jnp.where(allowed[None], scores, -1e30)
    raised = jnp.exp(scores - jnp.max(scores, axis=-1, keepdims=True))
    soft = raised / jnp.sum(raised, axis=-1, keepdims=True)
    soft_low = soft.astype(BF16)
    attended = jnp.einsum("hqk,khd->qhd", soft_low, value, preferred_element_type=F32).astype(BF16)
    flat = attended.reshape(rows, tensor, w)
    outt = first[:, :, 3 * w :]
    residual = x + jnp.einsum("rte,tde->rd", flat, outt, preferred_element_type=F32) + bias_out
    scaled2, inverse2 = norm_parts(residual)
    normed2 = (scaled2 * gain2 + bias2).astype(BF16)
    pre = jnp.einsum("rd,tdf->rtf", normed2, up, preferred_element_type=F32) + bias_up.reshape(
        tensor, c
    )
    active, slope = gelu_parts(pre)
    active = active.astype(BF16)
    second = jnp.einsum("rtf,tdf->rd", active, downt, preferred_element_type=F32)
    output = (residual + second + bias_down).astype(BF16)

    grad_active = jnp.einsum("rd,tdf->rtf", cotangent, downt, preferred_element_type=F32)
    grad_pre = (grad_active * slope).astype(BF16)
    g_down = jnp.einsum("rd,rtf->tdf", cotangent, active, preferred_element_type=F32)
    g_up = jnp.einsum("rd,rtf->tdf", normed2, grad_pre, preferred_element_type=F32)
    grad_normed2 = jnp.einsum("rtf,tdf->rd", grad_pre, up, preferred_element_type=F32)
    grad_result = cotangent.astype(F32)
    grad_residual = grad_result + norm_backward(grad_normed2, scaled2, inverse2, gain2)
    grad_branch = grad_residual.astype(BF16)
    g_outt = jnp.einsum("rd,rte->tde", grad_branch, flat, preferred_element_type=F32)
    grad_att = jnp.einsum("rd,tde->rte", grad_branch, outt, preferred_element_type=F32)
    grad_att = grad_att.astype(BF16).reshape(rows, heads, HD)
    grad_value = jnp.einsum("hqk,qhd->khd", soft_low, grad_att, preferred_element_type=F32)
    grad_soft = jnp.einsum("qhd,khd->hqk", grad_att, value, preferred_element_type=F32)
    grad_scores = (
        soft * (grad_soft - jnp.sum(soft * grad_soft, axis=-1, keepdims=True))
    ).astype(BF16)
    grad_query = (
        jnp.einsum("hqk,khd->qhd", grad_scores, key, preferred_element_type=F32) * factor
    )
    grad_key = jnp.einsum("hqk,qhd->khd", grad_scores, query, preferred_element_type=F32) * factor
    three = [
        g.astype(BF16).reshape(rows, tensor, w) for g in (grad_query, grad_key, grad_value)
    ]
    grad_mixed = jnp.concatenate(three, axis=2)
    g_qkv = jnp.einsum("rd,rtc->tdc", normed1, grad_mixed, preferred_element_type=F32)
    grad_normed1 = jnp.einsum(
        "rtc,tdc->rd", grad_mixed, first[:, :, : 3 * w], preferred_element_type=F32
    )
    grad_tokens = (grad_residual + norm_backward(grad_normed1, scaled1, inverse1, gain1)).astype(
        BF16
    )
    grads = jnp.stack(
        [
            jnp.concatenate([g_qkv, g_outt], axis=2).astype(BF16),
            g_up.astype(BF16),
            g_down.astype(BF16),
        ]
    )

    def total(values):
        return jnp.sum(values.astype(F32), axis=0).reshape(-1)

    sums = jnp.concatenate(
        [
            total(grad_normed1 * scaled1),
            total(grad_normed1),
            total(grad_normed2 * scaled2),
            total(grad_normed2),
            total(three[0]),
            total(three[2]),
            total(grad_residual),
            total(grad_pre),
            total(grad_result),
        ]
    )
    return output, grad_tokens, grads, sums


def own_chunks(qkv, out, up, down):
    r = up.shape[0]
    four = jnp.stack([a.reshape(r, 3, HD) for a in (qkv[0], qkv[2], qkv[1], out.T)], axis=2)
    first = four.transpose(1, 0, 2, 3).reshape(3, r, 256)
    rest = jnp.stack([up.reshape(r, 3, 256), down.T.reshape(r, 3, 256)])
    return jnp.concatenate([first, rest.transpose(2, 0, 1, 3).reshape(6, r, 256)])


def own_gradients(chunks):
    r = chunks.shape[1]
    four = chunks[:3].reshape(3, r, 4, HD)
    qkv = jnp.stack([four[:, :, k].transpose(1, 0, 2).reshape(r, 192) for k in (0, 2, 1)])
    out = four[:, :, 3].transpose(0, 2, 1).reshape(192, r)
    rest = chunks[3:].reshape(3, 2, r, 256)
    up = rest[:, 0].transpose(1, 0, 2).reshape(r, 768)
    down = rest[:, 1].transpose(0, 2, 1).reshape(768, r)
    return qkv, out, up, down


def by_head(piece):
    return piece.reshape(4, 3, HD).transpose(1, 0, 2).reshape(12, HD)


def bias_rows(vectors):
    rows = vectors.reshape(12, DM)
    heads = jnp.concatenate([by_head(rows[4]), by_head(rows[5]), jnp.zeros((12, 128), F32)], axis=1)
    units = rows[7:11].reshape(4, 3, 256).transpose(1, 0, 2).reshape(12, 256)
    return jnp.concatenate([heads, units]).reshape(24, 1, 256)


def vector_gradient(sums):
    six = sums[24:42].reshape(6, DM)
    heads = sums[:12, :128].reshape(3, 4, 2, HD).transpose(2, 1, 0, 3).reshape(2, DM)
    units = sums[12:24].reshape(3, 4, 256).transpose(1, 0, 2).reshape(4, DM)
    return jnp.concatenate([six[:4], heads, six[4:5], units, six[5:6]]).reshape(-1)


def ringed(tokens, cotangent, patches, qkv, out, up, down, vectors):
    output, grad_tokens, grads, sums = mega_call(
        tokens,
        cotangent,
        own_chunks(qkv, out, up, down),
        vectors.reshape(12, DM),
        bias_rows(vectors),
        jnp.full((8, 128), patches, jnp.int32),
    )
    return (output, grad_tokens) + own_gradients(grads) + (vector_gradient(sums),)


def general(dp, tensor, tokens, cotangent, patches, qkv, out, up, down, vectors):
    blocks = gather_blocks(pack_shards(qkv, out, up, down), dp, tensor)
    output, grad_tokens, grads, sums = local_layer(tokens, cotangent, patches, blocks, vectors)
    grads = scatter_blocks(grads, dp, tensor).astype(F32)
    w = qkv.shape[2]
    return (
        output,
        grad_tokens,
        jnp.stack([grads[0][:, i * w : (i + 1) * w] for i in range(3)]),
        grads[0][:, 3 * w :].T,
        grads[1],
        grads[2].T,
        lax.psum(sums, BOTH),
    )


def make_body(dp, tensor):
    layer = ringed if (dp, tensor) == (8, 4) else functools.partial(general, dp, tensor)

    def body(
        tokens,
        cotangent,
        block_patches,
        qkv,
        out,
        up,
        down,
        vectors,
        momentum,
        target_qkv,
        target_out,
        target_up,
        target_down,
        target_vectors,
    ):
        patches = block_patches[lax.axis_index("tensor")]
        results = layer(tokens, cotangent, patches, qkv, out, up, down, vectors)
        rate = momentum[0]

        def average(target, online):
            return rate * target + (1.0 - rate) * online.astype(F32)

        return results + (
            average(target_qkv, qkv),
            average(target_out, out),
            average(target_up, up),
            average(target_down, down),
            average(target_vectors, vectors),
        )

    return body


def solution(mesh):
    rows, matrices = P(BOTH, None), (
        P(None, "dp", "tensor"),
        P("tensor", "dp"),
        P("dp", "tensor"),
        P("tensor", "dp"),
    )
    return jax.shard_map(
        make_body(mesh.shape["dp"], mesh.shape["tensor"]),
        mesh=mesh,
        in_specs=(rows, rows, P("dp")) + matrices + (P(), P()) + matrices + (P(),),
        out_specs=(rows, rows) + matrices + (P(),) + matrices + (P(),),
        check_vma=False,
    )
```

```python
import functools
import math

import jax
import jax.numpy as jnp
from jax import lax
from jax.experimental import pallas as pl
from jax.experimental.pallas import tpu as pltpu
from jax.sharding import PartitionSpec as P

F32 = jnp.float32
BF16 = jnp.bfloat16
MESH = pl.DeviceIdType.MESH
NCH = 9
HALF = 48


class Place:
    def __init__(self):
        d, t = lax.axis_index("dp"), lax.axis_index("tensor")
        self.x, self.z = lax.rem(d, 2), lax.div(d, 2)
        self.c, self.y = lax.rem(t, 2), lax.div(t, 2)
        self.core = (d, t + 1 - 2 * self.c)
        self.ynb = (d, lax.rem(t + 2, 4))
        self.xnb = (d + 1 - 2 * self.x, t)
        self.zup = (lax.rem(d + 2, 8), t)
        self.zdn = (lax.rem(d + 6, 8), t)
        self.zfar = (lax.rem(d + 4, 8), t)
        self.zpair = self.z + 1 - 2 * lax.rem(self.z, 2)

    def zrel(self, s):
        return lax.rem(self.z + 4 - s, 4)

    def barrier(self):
        bar = pltpu.get_barrier_semaphore()
        near = (self.core, self.ynb, self.xnb, self.zup, self.zdn, self.zfar)
        for dev in near:
            pl.semaphore_signal(bar, inc=1, device_id=dev, device_id_type=MESH)
        pl.semaphore_wait(bar, len(near))


class Gather:
    STAGES = 7
    COPIES = 11

    def __init__(self, p, own, w, ss, rs):
        self.p, self.own, self.w, self.ss, self.rs = p, own, w, ss, rs

    def copy(self, src, dst, n, k, dev):
        return pltpu.make_async_remote_copy(
            src, dst, send_sem=self.ss.at[n, k], recv_sem=self.rs.at[n, k], device_id=dev, device_id_type=MESH
        )

    def part(self, n, k):
        p, w = self.p, self.w
        x, y, c = p.x, p.y, p.c
        lo, hi = pl.ds(0, HALF), pl.ds(HALF, HALF)
        line = lambda yy, cc, xx: w.at[n, yy, cc, :, xx]
        if k < 3:
            return w.at[n, y, c, p.zrel(k), x], w.at[n, y, c, p.zrel(k + 1), x], p.zup
        if k == 3:
            return line(y, c, x), line(y, c, 1 - x), p.xnb
        if k == 4:
            return line(y, c, x), line(1 - y, c, x), p.ynb
        if k == 5:
            return line(y, c, x), line(y, 1 - c, x), p.core
        if k == 6:
            return w.at[n, y, c, :, 1 - x, lo], w.at[n, 1 - y, c, :, 1 - x, lo], p.ynb
        if k == 7:
            return line(y, c, 1 - x), line(y, 1 - c, 1 - x), p.core
        if k == 8:
            return w.at[n, 1 - y, c, :, x, hi], w.at[n, 1 - y, c, :, 1 - x, hi], p.xnb
        if k == 9:
            return line(1 - y, c, x), line(1 - y, 1 - c, x), p.core
        return line(1 - y, c, 1 - x), line(1 - y, 1 - c, 1 - x), p.core

    def start(self, n, k):
        src, _, dev = self.part(n, k)
        self.copy(src, src, n, k, dev).start()

    def pass_on(self, n, s):
        p = self.p
        at = self.w.at[n, p.y, p.c, p.zrel(s), p.x]
        src = self.own.at[n] if s == 0 else at
        if s < 3:
            self.copy(src, at, n, s, p.zup).start()
        for k, dev in ((3, p.xnb), (4, p.ynb), (5, p.core)):
            self.copy(src, at, n, k, dev).start()

    def arrive(self, n, k):
        _, mine, dev = self.part(n, k)
        self.copy(mine, mine, n, k, dev).wait_recv()

    def finish(self, n):
        for k in range(self.COPIES):
            src, _, dev = self.part(n, k)
            self.copy(src, src, n, k, dev).wait_send()

    def stage(self, n, s):
        if s < 4:
            if s > 0:
                self.arrive(n, s - 1)
            self.pass_on(n, s)
        elif s == 4:
            self.arrive(n, 3)
            self.start(n, 6)
            self.start(n, 7)
            self.arrive(n, 4)
            self.start(n, 8)
            self.start(n, 9)
        elif s == 5:
            self.arrive(n, 6)
            self.arrive(n, 8)
            self.start(n, 10)
        else:
            for k in (5, 7, 9, 10):
                self.arrive(n, k)


class Scatter:
    STAGES = 7
    COPIES = 8

    def __init__(self, p, g, out, rc, rd, rl, rz, ss, rs):
        self.p, self.g, self.out, self.rc, self.rd, self.rl, self.rz = p, g, out, rc, rd, rl, rz
        self.ss, self.rs = ss, rs

    def part(self, m, k):
        p, g = self.p, self.g
        n, o = self.chunk(m), m
        x, y, c = p.x, p.y, p.c
        lo, hi = pl.ds(0, HALF), pl.ds(HALF, HALF)
        if k == 0:
            return g.at[n, :, 1 - c], self.rc.at[o], p.core
        if k == 1:
            return g.at[n, 1 - y, c, :, 1 - x, lo], self.rd.at[o, 0], p.ynb
        if k == 2:
            return g.at[n, 1 - y, c, :, 1 - x, hi], self.rd.at[o, 1], p.xnb
        if k == 3:
            return g.at[n, y, c, :, 1 - x], self.rl.at[o, 0], p.xnb
        if k == 4:
            return g.at[n, 1 - y, c, :, x], self.rl.at[o, 1], p.ynb
        return g.at[n, y, c, p.zrel(k - 4), x], self.rz.at[m, k - 5], p.zup

    def copy(self, m, k):
        src, dst, dev = self.part(m, k)
        return pltpu.make_async_remote_copy(
            src, dst, send_sem=self.ss.at[m, k], recv_sem=self.rs.at[m, k], device_id=dev, device_id_type=MESH
        )

    def start(self, m, k):
        self.copy(m, k).start()

    def arrive(self, m, k):
        self.copy(m, k).wait_recv()

    def finish(self, m):
        for k in range(self.COPIES):
            self.copy(m, k).wait_send()

    def add(self, ref, *others):
        total = ref[...].astype(F32)
        for o in others:
            total += o[...].astype(F32)
        ref[...] = total.astype(BF16)

    def chunk(self, m):
        return lax.rem(m + 3, NCH)

    def stage(self, m, s):
        p, g = self.p, self.g
        n, o = self.chunk(m), m
        x, y, c = p.x, p.y, p.c
        lo, hi = pl.ds(0, HALF), pl.ds(HALF, HALF)
        if s == 0:
            self.start(m, 0)
        elif s == 1:
            self.arrive(m, 0)
            self.add(g.at[n, 1 - y, c, :, 1 - x], self.rc.at[o, 1 - y, :, 1 - x])
            self.start(m, 1)
            self.start(m, 2)
            self.add(g.at[n, y, c], self.rc.at[o, y])
            self.add(g.at[n, 1 - y, c, :, x], self.rc.at[o, 1 - y, :, x])
        elif s == 2:
            self.arrive(m, 1)
            self.add(g.at[n, y, c, :, 1 - x, lo], self.rd.at[o, 0])
            self.start(m, 3)
            self.arrive(m, 2)
            self.add(g.at[n, 1 - y, c, :, x, hi], self.rd.at[o, 1])
            self.start(m, 4)
        elif s == 3:
            self.arrive(m, 3)
            self.arrive(m, 4)
            self.add(g.at[n, y, c, :, x], self.rl.at[o, 0], self.rl.at[o, 1])
            self.start(m, 5)
        elif s < 6:
            self.arrive(m, s + 1)
            self.add(g.at[n, y, c, p.zrel(s - 2), x], self.rz.at[m, s - 4])
            self.start(m, s + 2)
        else:
            self.arrive(m, 7)
            self.out[n] = g[n, y, c, p.z, x].astype(F32) + self.rz[m, 2].astype(F32)


WSHAPE = (NCH, 2, 2, 4, 2, 96, 256)
ROWS = 784
DM = 768
PARTS = ((0, 400), (400, 384))
STEP = 112
LOG2E = math.log2(math.e)
CS = LOG2E / 8
BIG = 1e30


def nt(a, b):
    return lax.dot_general(a, b, (((1,), (1,)), ((), ())), preferred_element_type=F32)


def tn(a, b):
    return lax.dot_general(a, b, (((0,), (0,)), ((), ())), preferred_element_type=F32)


def nn(a, b):
    return jnp.dot(a, b, preferred_element_type=F32)


def split3(a):
    one = a.astype(BF16)
    rest = a - one.astype(F32)
    two = rest.astype(BF16)
    return one, two, (rest - two.astype(F32)).astype(BF16)


def turn(a):
    return pltpu.roll(a.astype(F32), 64, 1)


def standard(values):
    centred = values - jnp.mean(values, axis=-1, keepdims=True)
    inverse = lax.rsqrt(jnp.mean(centred * centred, axis=-1, keepdims=True) + 1e-06)
    return centred * inverse, inverse


def norm_pull(grad, scaled, inverse, gain):
    g = grad * gain
    return inverse * (
        g - jnp.mean(g, axis=-1, keepdims=True) - scaled * jnp.mean(g * scaled, axis=-1, keepdims=True)
    )


def gelu_slope(v):
    cdf = 0.5 + 0.5 * lax.erf(v * math.sqrt(0.5))
    return v * cdf, cdf + v * (jnp.exp(-0.5 * v * v) * (1.0 / math.sqrt(2.0 * math.pi)))


def rows_of(i):
    return pl.ds(pl.multiple_of(i * STEP, 16), STEP)


def fold(values):
    return jnp.sum(values.reshape(STEP // 8, 8, values.shape[1]), axis=0)


def head_slot(g):
    return (g % 3) * 4 + g // 3


class Layer:
    def __init__(self, refs):
        self.__dict__.update(refs)

    def mat(self, n, y, c):
        return self.w[n, y, c].reshape(DM, 256)

    def put(self, n, y, c, value):
        self.w[n, y, c] = value.astype(BF16).reshape(4, 2, 96, 256)

    def pack(self):
        outt = self.wout[...].astype(F32).T
        q, k, v = (self.qkv[a].astype(F32) for a in range(3))
        for j in range(3):
            cols, wide = slice(64 * j, 64 * j + 64), slice(256 * j, 256 * j + 256)
            self.own[j] = jnp.concatenate([a[:, cols] for a in (q, v, k, outt)], axis=1).astype(BF16)
            self.own[3 + 2 * j] = self.up[:, wide]
            self.own[4 + 2 * j] = self.down[:, wide]

    def prepare(self, t):
        for k in range(12):
            for b in range(6):
                self.vec[k : k + 1, 128 * b : 128 * b + 128] = self.flat[6 * k + b : 6 * k + b + 1, :]
        none = jnp.zeros((1, 128), F32)
        for g in range(12):
            cols = slice(64 * g, 64 * g + 64)
            self.bias[head_slot(g)] = jnp.concatenate([self.vec[4:5, cols], self.vec[5:6, cols], none], axis=1)
            self.bias[12 + head_slot(g)] = self.vec[7 + g // 3 : 8 + g // 3, 256 * (g % 3) : 256 * (g % 3) + 256]
        self.patches = self.pat[t]

    def masks(self):
        row = lax.broadcasted_iota(jnp.int32, (ROWS, 128), 0)
        lane = lax.broadcasted_iota(jnp.int32, (ROWS, 128), 1)
        p = jnp.full((ROWS, 128), self.patches, jnp.int32)
        image = sum(jnp.where(row >= k * p, 1, 0) for k in (1, 2, 3))
        same = jnp.where(image == lane - 64, 1.0, 0.0)
        slot = (lane >= 64) & (lane < 68)
        self.mq[...] = jnp.where(slot, (same - 1.0) * BIG, 0.0).astype(BF16)
        self.mk[...] = jnp.where(slot, same, jnp.where((lane >= 68) & (lane < 71), 1.0, 0.0)).astype(BF16)

    def norm1(self):
        def step(i, _):
            r = rows_of(i)
            scaled, _ = standard(self.tok[r, :].astype(F32))
            self.n1[r, :] = (scaled * self.vec[0:1, :] + self.vec[1:2, :]).astype(BF16)
            return 0

        lax.fori_loop(0, ROWS // STEP, step, 0)

    def attend(self, i):
        j, y = lax.div(i, 2), lax.rem(i, 2)
        lane = lax.broadcasted_iota(jnp.int32, (ROWS, 128), 1)
        left = lane < 64
        out_halves = []
        for c in range(2):
            h = i * 2 + c
            mixed = (nn(self.n1[...], self.mat(j, y, c)) + self.bias[h]).astype(BF16)
            self.qa[h] = jnp.where(left, mixed[:, :128], self.mq[...])
            self.ka[h] = jnp.where(left, mixed[:, 128:], self.mk[...])
            self.va[h] = jnp.where(left, jnp.ones((), BF16), mixed[:, :128])
            out_halves.append(self.mat(j, y, c)[:, 128:])
        first = lax.broadcasted_iota(jnp.int32, (DM, 128), 1) < 64
        self.ot[j, y] = jnp.where(first, turn(out_halves[0]), out_halves[1].astype(F32)).astype(BF16)
        for r0, n in PARTS:
            r = pl.ds(r0, n)
            lanes = lax.broadcasted_iota(jnp.int32, (n, 128), 1)
            results = []
            for c in range(2):
                h = i * 2 + c
                q = self.qa[h, r, :]
                s = nt(q, self.ka[h])
                top = jnp.max(s, axis=1, keepdims=True) * CS
                p = jnp.exp2(s * CS - top).astype(BF16)
                a = nn(p, self.va[h])
                total = pltpu.roll(a, 64, 1)
                results.append(a * (1.0 / total))
                h1, h2, h3 = split3((top + jnp.log2(total)) * (-1.0 / CS))
                self.qa[h, r, :] = jnp.where(
                    lanes == 68, h1, jnp.where(lanes == 69, h2, jnp.where(lanes == 70, h3, q))
                )
            pair = jnp.where(lanes < 64, pltpu.roll(results[0], 64, 1), results[1])
            self.att[j, y, r, :] = pair.astype(BF16)

    def pair(self, ref, j, r=slice(None)):
        return jnp.concatenate([ref[j, 0, r, :], ref[j, 1, r, :]], axis=1)

    def project(self):
        for r0, n in PARTS:
            r = pl.ds(r0, n)
            total = sum(nt(self.pair(self.att, j, r), self.pair(self.ot, j)) for j in range(3))
            self.res[r, :] = total + (self.tok[r, :].astype(F32) + self.vec[6:7, :])

        def step(i, _):
            r = rows_of(i)
            v = self.res[r, :]
            scaled, _ = standard(v)
            self.n2[r, :] = (scaled * self.vec[2:3, :] + self.vec[3:4, :]).astype(BF16)
            self.acc[r, :] = v + self.vec[11:12, :]
            self.gn[r, :] = jnp.zeros((STEP, DM), F32)
            return 0

        lax.fori_loop(0, ROWS // STEP, step, 0)

    def feed(self, i, pause):
        j, y = lax.div(i, 2), lax.rem(i, 2)
        nb, nc = 3 + 2 * j, 4 + 2 * j
        sums = [0.0, 0.0]
        for r0, n in PARTS:
            r = pl.ds(r0, n)
            for c in range(2):
                cols = slice(c * 256, c * 256 + 256)
                pre = nn(self.n2[r, :], self.mat(nb, y, c)) + self.bias[12 + i * 2 + c]
                up = nn(self.cot[r, :], self.mat(nc, y, c))
                active, slope = gelu_slope(pre)
                grad = (up * slope).astype(BF16)
                self.act[r, cols] = active.astype(BF16)
                self.gp[r, cols] = grad
                sums[c] += jnp.sum(grad.astype(F32).reshape(n // 8, 8, 256), axis=0)
            self.acc[r, :] += nt(self.act[r, 0:256], self.mat(nc, y, 0)) + nt(
                self.act[r, 256:512], self.mat(nc, y, 1)
            )
            self.gn[r, :] += nt(self.gp[r, 0:256], self.mat(nb, y, 0)) + nt(
                self.gp[r, 256:512], self.mat(nb, y, 1)
            )
        pause(0)
        for c in range(2):
            cols = slice(c * 256, c * 256 + 256)
            self.hs[12 + i * 2 + c] = jnp.sum(sums[c], axis=0, keepdims=True)
            self.put(nc, y, c, tn(self.cot[...], self.act[:, cols]))
            self.put(nb, y, c, tn(self.n2[...], self.gp[:, cols]))
        pause(1)

    def residual_back(self):
        self.vs[...] = jnp.zeros(self.vs.shape, F32)

        def step(i, _):
            r = rows_of(i)
            self.out[r, :] = self.acc[r, :].astype(BF16)
            scaled, inverse = standard(self.res[r, :])
            g = self.gn[r, :]
            ct = self.cot[r, :].astype(F32)
            grad = ct + norm_pull(g, scaled, inverse, self.vec[2:3, :])
            self.res[r, :] = grad
            self.gb[r, :] = grad.astype(BF16)
            self.gn[r, :] = jnp.zeros((STEP, DM), F32)
            for k, v in ((2, g * scaled), (3, g), (4, grad), (5, ct)):
                self.vs[k] += fold(v)
            return 0

        lax.fori_loop(0, ROWS // STEP, step, 0)

    def attend_back(self, i, pause):
        j, y = lax.div(i, 2), lax.rem(i, 2)
        lane = lax.broadcasted_iota(jnp.int32, (ROWS, 128), 1)
        left = lane < 64
        low = nn(self.gb[...], self.ot[j, y]).astype(BF16)
        wide = low.astype(F32)
        product = wide * self.att[j, y].astype(F32)
        for c in range(2):
            h = i * 2 + c
            delta = jnp.sum(jnp.where(left == (c == 0), product, 0.0), axis=1, keepdims=True)
            d1, d2, d3 = split3(jnp.broadcast_to(-delta, (ROWS, 128)))
            moved = pltpu.roll(wide, 64, 1).astype(BF16) if c == 0 else low
            none = jnp.zeros((), BF16)
            extra = jnp.where(lane == 0, d1, jnp.where(lane == 1, d2, jnp.where(lane == 2, d3, none)))
            self.da[...] = jnp.where(left, extra, moved)
            dv = dk = 0.0
            for r0, n in PARTS:
                r = pl.ds(r0, n)
                q, d = self.qa[h, r, :], self.da[r, :]
                p = jnp.exp2(nt(q, self.ka[h]) * CS)
                ds = (p * nt(d, self.va[h])).astype(BF16)
                dv += tn(p.astype(BF16), d)
                dk += tn(ds, q)
                self.dq[c, r, 0:128] = (nn(ds, self.ka[h]) * 0.125).astype(BF16)
            self.dq[c, :, 0:128] = jnp.where(left, self.dq[c, :, 0:128], dv.astype(BF16))
            self.dq[c, :, 128:256] = jnp.where(left, (dk * 0.125).astype(BF16), none)
            sums = jnp.sum(self.dq[c].astype(F32).reshape(ROWS // 8, 8, 256), axis=0)
            self.hs[h] = jnp.sum(sums, axis=0, keepdims=True)
            pause(c)
        for r0, n in PARTS:
            r = pl.ds(r0, n)
            self.gn[r, :] += nt(self.dq[0, r, :], self.mat(j, y, 0)) + nt(
                self.dq[1, r, :], self.mat(j, y, 1)
            )
        outg = tn(self.gb[...], self.att[j, y])
        first = lax.broadcasted_iota(jnp.int32, (DM, 128), 1) < 64
        for c in range(2):
            g = tn(self.n1[...], self.dq[c])
            mine = pltpu.roll(outg, 64, 1) if c == 0 else outg
            self.put(j, y, c, jnp.concatenate([g[:, :128], jnp.where(first, g[:, 128:], mine)], axis=1))
        pause(2)

    def token_back(self):
        def step(i, _):
            r = rows_of(i)
            scaled, inverse = standard(self.tok[r, :].astype(F32))
            g = self.gn[r, :]
            grad = self.res[r, :] + norm_pull(g, scaled, inverse, self.vec[0:1, :])
            self.gtok[r, :] = grad.astype(BF16)
            self.vs[0] += fold(g * scaled)
            self.vs[1] += fold(g)
            return 0

        lax.fori_loop(0, ROWS // STEP, step, 0)

    def collect(self):
        for h in range(24):
            self.vsum[h : h + 1, :] = self.hs[h]
        for k in range(6):
            row = jnp.sum(self.vs[k], axis=0, keepdims=True)
            for b in range(3):
                self.vsum[24 + 3 * k + b : 25 + 3 * k + b, :] = row[:, 256 * b : 256 * b + 256]
        self.vsum[42:48, :] = jnp.zeros((6, 256), F32)


def layer_scratch():
    return dict(
        w=pltpu.VMEM(WSHAPE, BF16),
        n1=pltpu.VMEM((ROWS, DM), BF16),
        n2=pltpu.VMEM((ROWS, DM), BF16),
        gb=pltpu.VMEM((ROWS, DM), BF16),
        qa=pltpu.VMEM((12, ROWS, 128), BF16),
        ka=pltpu.VMEM((12, ROWS, 128), BF16),
        va=pltpu.VMEM((12, ROWS, 128), BF16),
        att=pltpu.VMEM((3, 2, ROWS, 128), BF16),
        ot=pltpu.VMEM((3, 2, DM, 128), BF16),
        res=pltpu.VMEM((ROWS, DM), F32),
        acc=pltpu.VMEM((ROWS, DM), F32),
        gn=pltpu.VMEM((ROWS, DM), F32),
        mq=pltpu.VMEM((ROWS, 128), BF16),
        mk=pltpu.VMEM((ROWS, 128), BF16),
        act=pltpu.VMEM((ROWS, 512), BF16),
        gp=pltpu.VMEM((ROWS, 512), BF16),
        da=pltpu.VMEM((ROWS, 128), BF16),
        dq=pltpu.VMEM((2, ROWS, 256), BF16),
        vs=pltpu.VMEM((6, 8, DM), F32),
        hs=pltpu.VMEM((24, 1, 256), F32),
        own=pltpu.VMEM((NCH, 96, 256), BF16),
        vec=pltpu.VMEM((12, DM), F32),
        bias=pltpu.VMEM((24, 1, 256), F32),
    )


NAMES_IN = ("tok", "cot", "qkv", "wout", "up", "down", "flat", "pat")
NAMES_OUT = ("out", "gtok", "gsh", "vsum")


def slots_of(u):
    late = u - 7
    early_ok = (u >= 0) & (u <= 5)
    late_ok = (late >= 0) & (late <= 4) & (lax.rem(jnp.maximum(late, 0), 2) == 0)
    return jnp.where(early_ok, u, 6 + lax.div(jnp.maximum(late, 0), 2)), early_ok | late_ok


def gather_slot(gather, t):
    for s in range(gather.STAGES):
        n = t - s
        if isinstance(t, int):
            if 0 <= n < NCH:
                gather.stage(n, s)
        else:
            pl.when((n >= 0) & (n < NCH))(functools.partial(gather.stage, n, s))


def scatter_slot(scatter, t):
    for s in range(scatter.STAGES):
        m, ok = slots_of(t - s)
        pl.when(ok)(functools.partial(scatter.stage, m, s))


class Totals:
    def __init__(self, p, value, vr, ss, rs):
        self.p, self.value, self.vr, self.ss, self.rs = p, value, vr, ss, rs
        z1 = (lax.rem(p.zpair * 2 + p.x, 8), lax.axis_index("tensor"))
        self.devs = (p.core, p.ynb, p.xnb, z1, p.zfar)

    def copy(self, k):
        src = self.vr.at[0, k]
        return pltpu.make_async_remote_copy(
            src, self.vr.at[1, k], send_sem=self.ss.at[k], recv_sem=self.rs.at[k],
            device_id=self.devs[k], device_id_type=MESH,
        )

    def start(self, k, total):
        self.vr[0, k] = total
        self.copy(k).start()

    def end(self, k):
        self.copy(k).wait_recv()
        return self.vr[0, k] + self.vr[1, k]


def mega_kernel(names, *refs):
    r = dict(zip(names, refs))
    layer = Layer(r)
    p = Place()
    p.barrier()
    gather = Gather(p, r["own"], r["w"], r["gss"], r["grs"])
    scatter = Scatter(p, r["w"], r["gsh"], r["rc"], r["rd"], r["rl"], r["rz"], r["sss"], r["srs"])
    totals = Totals(p, r["vsum"], r["vr"], r["vss"], r["vrs"])

    layer.pack()
    for n in range(NCH):
        r["w"][n, p.y, p.c, p.z, p.x] = r["own"][n]
    gather_slot(gather, 0)
    layer.prepare(lax.axis_index("tensor"))
    layer.masks()
    gather_slot(gather, 1)
    layer.norm1()
    lax.fori_loop(2, 6, lambda t, c: (gather_slot(gather, t), c)[1], 0)

    def attend(i, _):
        pl.when(lax.rem(i, 2) == 0)(lambda: gather_slot(gather, 6 + lax.div(i, 2)))
        layer.attend(i)
        return 0

    lax.fori_loop(0, 6, attend, 0)
    gather_slot(gather, jnp.int32(9))
    layer.project()
    gather_slot(gather, jnp.int32(10))

    def feed(i, _):
        @pl.when(lax.rem(i, 2) == 0)
        def _():
            gather.finish(3 + i)
            gather.finish(4 + i)

        layer.feed(i, lambda k: None)
        gather_slot(gather, 11 + i)
        scatter_slot(scatter, i - 1)
        return 0

    lax.fori_loop(0, 6, feed, 0)
    layer.residual_back()
    scatter_slot(scatter, jnp.int32(5))
    for n in range(3):
        gather.finish(n)

    def back(i, _):
        layer.attend_back(i, lambda k: None)
        scatter_slot(scatter, 6 + i)
        return 0

    lax.fori_loop(0, 6, back, 0)
    layer.token_back()
    layer.collect()
    value = r["vsum"][...]
    scatter_slot(scatter, jnp.int32(12))
    for k in range(5):
        totals.start(k, value)
        scatter_slot(scatter, jnp.int32(13 + k))
        value = totals.end(k)
    r["vsum"][...] = value
    lax.fori_loop(0, NCH, lambda m, c: (scatter.finish(m), c)[1], 0)
    for k in range(5):
        totals.copy(k).wait_send()


def mega_scratch():
    return dict(
        layer_scratch(),
        rc=pltpu.VMEM((NCH, 2, 4, 2, 96, 256), BF16),
        rd=pltpu.VMEM((NCH, 2, 4, HALF, 256), BF16),
        rl=pltpu.VMEM((NCH, 2, 4, 96, 256), BF16),
        rz=pltpu.VMEM((NCH, 3, 96, 256), BF16),
        vr=pltpu.VMEM((2, 5, 48, 256), F32),
        gss=pltpu.SemaphoreType.DMA((NCH, Gather.COPIES)),
        grs=pltpu.SemaphoreType.DMA((NCH, Gather.COPIES)),
        sss=pltpu.SemaphoreType.DMA((NCH, Scatter.COPIES)),
        srs=pltpu.SemaphoreType.DMA((NCH, Scatter.COPIES)),
        vss=pltpu.SemaphoreType.DMA((5,)),
        vrs=pltpu.SemaphoreType.DMA((5,)),
    )


def mega_call(*args):
    scratch = mega_scratch()
    names = NAMES_IN + NAMES_OUT + tuple(scratch)
    vm = pl.BlockSpec(memory_space=pltpu.VMEM)
    shape = jax.ShapeDtypeStruct
    return pl.pallas_call(
        functools.partial(mega_kernel, names),
        out_shape=(
            shape((ROWS, DM), BF16),
            shape((ROWS, DM), BF16),
            shape((NCH, 96, 256), F32),
            shape((48, 256), F32),
        ),
        in_specs=[vm] * (len(NAMES_IN) - 1) + [pl.BlockSpec(memory_space=pltpu.SMEM)],
        out_specs=(vm,) * len(NAMES_OUT),
        scratch_shapes=list(scratch.values()),
        compiler_params=pltpu.CompilerParams(collective_id=0, has_side_effects=True, vmem_limit_bytes=62 << 20),
    )(*args)


def tail_kernel(names, *refs):
    r = dict(zip(names, refs))
    r["out"][...] = r["out_in"][...]
    r["gtok"][...] = r["gtok_in"][...]
    g = r["gsh"]
    for j in range(3):
        cols = slice(64 * j, 64 * j + 64)
        for a, k in enumerate((0, 128, 64)):
            r["gqkv"][a, :, cols] = g[j, :, k : k + 64]
        r["gup"][:, 256 * j : 256 * j + 256] = g[3 + 2 * j]
        r["gdown"][:, 256 * j : 256 * j + 256] = g[4 + 2 * j]
        r["gout"][cols, :] = g[j, :, 128:256].T[64:128, :]
    v, gv = r["vsum"], r["gvec"]
    for k, row in enumerate((0, 1, 2, 3, 6, 11)):
        for b in range(6):
            gv[6 * row + b : 6 * row + b + 1, :] = v[24 + 3 * k + b // 2 : 25 + 3 * k + b // 2, 128 * (b % 2) : 128 * (b % 2) + 128]
    for half in range(2):
        for b in range(6):
            two = [v[h : h + 1, 64 * half : 64 * half + 64] for h in (head_slot(2 * b), head_slot(2 * b + 1))]
            gv[24 + 6 * half + b : 25 + 6 * half + b, :] = jnp.concatenate(two, axis=1)
    for t in range(4):
        for b in range(6):
            row = 12 + (b // 2) * 4 + t
            gv[42 + 6 * t + b : 43 + 6 * t + b, :] = v[row : row + 1, 128 * (b % 2) : 128 * (b % 2) + 128]
    rate = r["rate"][0]
    for name in ("qkv", "wout", "up", "down", "vec"):
        r["next_" + name][...] = rate * r["target_" + name][...] + (1.0 - rate) * r[name][...].astype(F32)


def tail_call(results, online, targets, momentum):
    five = ("qkv", "wout", "up", "down", "vec")
    ins = ("out_in", "gtok_in", "gsh", "vsum") + five + tuple("target_" + a for a in five) + ("rate",)
    outs = ("out", "gtok", "gqkv", "gout", "gup", "gdown", "gvec") + tuple("next_" + a for a in five)
    vm = pl.BlockSpec(memory_space=pltpu.VMEM)
    shape = jax.ShapeDtypeStruct
    like = [shape(a.shape, F32) for a in online]
    return pl.pallas_call(
        functools.partial(tail_kernel, ins + outs),
        out_shape=[shape(results[0].shape, BF16), shape(results[1].shape, BF16)] + like + like,
        in_specs=[vm] * 14 + [pl.BlockSpec(memory_space=pltpu.SMEM)],
        out_specs=[vm] * 12,
    )(*results, *online, *targets, momentum)


HD = 64
BOTH = ("dp", "tensor")


def unpack(vectors, d, ff):
    cuts = [d * i for i in range(8)] + [7 * d + ff, 8 * d + ff]
    return tuple(vectors[a:b] for a, b in zip(cuts[:-1], cuts[1:]))


def norm_parts(values):
    centred = values - jnp.mean(values, axis=-1, keepdims=True)
    inverse = lax.rsqrt(jnp.mean(centred * centred, axis=-1, keepdims=True) + 1e-06)
    return centred * inverse, inverse


def norm_backward(grad_normed, scaled, inverse, gain):
    weighted = grad_normed * gain
    return inverse * (
        weighted
        - jnp.mean(weighted, axis=-1, keepdims=True)
        - scaled * jnp.mean(weighted * scaled, axis=-1, keepdims=True)
    )


def gelu_parts(v):
    cdf = 0.5 * (1.0 + lax.erf(v * (0.5**0.5)))
    return v * cdf, cdf + v * jnp.exp(-0.5 * v * v) * ((2.0 * jnp.pi) ** -0.5)


def dot(a, b, dims):
    return lax.dot_general(a, b, (dims, ((), ())), preferred_element_type=F32)


def pack_shards(qkv, out, up, down):
    first = jnp.concatenate([qkv[0], qkv[1], qkv[2], out.T], axis=1)
    return jnp.stack([first, up, down.T])


def gather_blocks(shards, dp, tensor):
    every = lax.all_gather(shards, BOTH, axis=0)
    b, r, c = shards.shape
    every = every.reshape(dp, tensor, b, r, c).transpose(2, 1, 0, 3, 4)
    return every.reshape(b, tensor, dp * r, c)


def scatter_blocks(blocks, dp, tensor):
    b, t, rows, c = blocks.shape
    r = rows // dp
    pieces = blocks.reshape(b, tensor, dp, r, c).transpose(2, 1, 0, 3, 4)
    pieces = pieces.reshape(dp * tensor, b, r, c)
    return lax.psum_scatter(pieces, BOTH, scatter_dimension=0, tiled=True)[0]


def local_layer(tokens, cotangent, patches, blocks, vectors):
    rows, d = tokens.shape
    tensor, c = blocks.shape[1], blocks.shape[3]
    w = c // 4
    ff = tensor * c
    heads = d // HD
    gain1, bias1, gain2, bias2, bias_q, bias_v, bias_out, bias_up, bias_down = unpack(
        vectors, d, ff
    )
    first, up, downt = blocks[0], blocks[1], blocks[2]
    factor = HD**-0.5

    x = tokens.astype(F32)
    scaled1, inverse1 = norm_parts(x)
    normed1 = (scaled1 * gain1 + bias1).astype(BF16)
    mixed = jnp.einsum("rd,tdc->rtc", normed1, first[:, :, : 3 * w], preferred_element_type=F32)
    query = (mixed[:, :, :w].reshape(rows, d) + bias_q).astype(BF16).reshape(rows, heads, HD)
    key = mixed[:, :, w : 2 * w].reshape(rows, d).astype(BF16).reshape(rows, heads, HD)
    value = (mixed[:, :, 2 * w :].reshape(rows, d) + bias_v).astype(BF16).reshape(rows, heads, HD)
    images = jnp.arange(rows, dtype=jnp.int32) // patches
    allowed = images[:, None] == images[None, :]
    scores = jnp.einsum("qhd,khd->hqk", query, key, preferred_element_type=F32) * factor
    scores = jnp.where(allowed[None], scores, -1e30)
    raised = jnp.exp(scores - jnp.max(scores, axis=-1, keepdims=True))
    soft = raised / jnp.sum(raised, axis=-1, keepdims=True)
    soft_low = soft.astype(BF16)
    attended = jnp.einsum("hqk,khd->qhd", soft_low, value, preferred_element_type=F32).astype(BF16)
    flat = attended.reshape(rows, tensor, w)
    outt = first[:, :, 3 * w :]
    residual = x + jnp.einsum("rte,tde->rd", flat, outt, preferred_element_type=F32) + bias_out
    scaled2, inverse2 = norm_parts(residual)
    normed2 = (scaled2 * gain2 + bias2).astype(BF16)
    pre = jnp.einsum("rd,tdf->rtf", normed2, up, preferred_element_type=F32) + bias_up.reshape(
        tensor, c
    )
    active, slope = gelu_parts(pre)
    active = active.astype(BF16)
    second = jnp.einsum("rtf,tdf->rd", active, downt, preferred_element_type=F32)
    output = (residual + second + bias_down).astype(BF16)

    grad_active = jnp.einsum("rd,tdf->rtf", cotangent, downt, preferred_element_type=F32)
    grad_pre = (grad_active * slope).astype(BF16)
    g_down = jnp.einsum("rd,rtf->tdf", cotangent, active, preferred_element_type=F32)
    g_up = jnp.einsum("rd,rtf->tdf", normed2, grad_pre, preferred_element_type=F32)
    grad_normed2 = jnp.einsum("rtf,tdf->rd", grad_pre, up, preferred_element_type=F32)
    grad_result = cotangent.astype(F32)
    grad_residual = grad_result + norm_backward(grad_normed2, scaled2, inverse2, gain2)
    grad_branch = grad_residual.astype(BF16)
    g_outt = jnp.einsum("rd,rte->tde", grad_branch, flat, preferred_element_type=F32)
    grad_att = jnp.einsum("rd,tde->rte", grad_branch, outt, preferred_element_type=F32)
    grad_att = grad_att.astype(BF16).reshape(rows, heads, HD)
    grad_value = jnp.einsum("hqk,qhd->khd", soft_low, grad_att, preferred_element_type=F32)
    grad_soft = jnp.einsum("qhd,khd->hqk", grad_att, value, preferred_element_type=F32)
    grad_scores = (
        soft * (grad_soft - jnp.sum(soft * grad_soft, axis=-1, keepdims=True))
    ).astype(BF16)
    grad_query = (
        jnp.einsum("hqk,khd->qhd", grad_scores, key, preferred_element_type=F32) * factor
    )
    grad_key = jnp.einsum("hqk,qhd->khd", grad_scores, query, preferred_element_type=F32) * factor
    three = [
        g.astype(BF16).reshape(rows, tensor, w) for g in (grad_query, grad_key, grad_value)
    ]
    grad_mixed = jnp.concatenate(three, axis=2)
    g_qkv = jnp.einsum("rd,rtc->tdc", normed1, grad_mixed, preferred_element_type=F32)
    grad_normed1 = jnp.einsum(
        "rtc,tdc->rd", grad_mixed, first[:, :, : 3 * w], preferred_element_type=F32
    )
    grad_tokens = (grad_residual + norm_backward(grad_normed1, scaled1, inverse1, gain1)).astype(
        BF16
    )
    grads = jnp.stack(
        [
            jnp.concatenate([g_qkv, g_outt], axis=2).astype(BF16),
            g_up.astype(BF16),
            g_down.astype(BF16),
        ]
    )

    def total(values):
        return jnp.sum(values.astype(F32), axis=0).reshape(-1)

    sums = jnp.concatenate(
        [
            total(grad_normed1 * scaled1),
            total(grad_normed1),
            total(grad_normed2 * scaled2),
            total(grad_normed2),
            total(three[0]),
            total(three[2]),
            total(grad_residual),
            total(grad_pre),
            total(grad_result),
        ]
    )
    return output, grad_tokens, grads, sums


def flat_views(arrays):
    qkv, out, up, down, vectors = arrays
    return qkv, out, up, down.T, vectors.reshape(72, 128)


def ringed(tokens, cotangent, block_patches, online, momentum, targets):
    online, targets = flat_views(online), flat_views(targets)
    results = mega_call(tokens, cotangent, *online, block_patches)
    final = tail_call(results, online, targets, momentum)
    return tuple(final[:2]) + tuple(
        a.T if k == 3 else a.reshape(-1) if k == 4 else a for five in (final[2:7], final[7:]) for k, a in enumerate(five)
    )


def general(dp, tensor, tokens, cotangent, patches, qkv, out, up, down, vectors):
    blocks = gather_blocks(pack_shards(qkv, out, up, down), dp, tensor)
    output, grad_tokens, grads, sums = local_layer(tokens, cotangent, patches, blocks, vectors)
    grads = scatter_blocks(grads, dp, tensor).astype(F32)
    w = qkv.shape[2]
    return (
        output,
        grad_tokens,
        jnp.stack([grads[0][:, i * w : (i + 1) * w] for i in range(3)]),
        grads[0][:, 3 * w :].T,
        grads[1],
        grads[2].T,
        lax.psum(sums, BOTH),
    )


def make_body(dp, tensor):
    def body(tokens, cotangent, block_patches, qkv, out, up, down, vectors, momentum, *targets):
        online = (qkv, out, up, down, vectors)
        if (dp, tensor) == (8, 4):
            return ringed(tokens, cotangent, block_patches, online, momentum, targets)
        patches = block_patches[lax.axis_index("tensor")]
        results = general(dp, tensor, tokens, cotangent, patches, *online)
        rate = momentum[0]
        return results + tuple(
            rate * target + (1.0 - rate) * weight.astype(F32) for target, weight in zip(targets, online)
        )

    return body


def solution(mesh):
    rows, matrices = P(BOTH, None), (
        P(None, "dp", "tensor"),
        P("tensor", "dp"),
        P("dp", "tensor"),
        P("tensor", "dp"),
    )
    return jax.shard_map(
        make_body(mesh.shape["dp"], mesh.shape["tensor"]),
        mesh=mesh,
        in_specs=(rows, rows, P("dp")) + matrices + (P(), P()) + matrices + (P(),),
        out_specs=(rows, rows) + matrices + (P(),) + matrices + (P(),),
        check_vma=False,
    )
```

```python
import functools
import math

import jax
import jax.numpy as jnp
from jax import lax
from jax.experimental import pallas as pl
from jax.experimental.pallas import tpu as pltpu
from jax.sharding import PartitionSpec as P

F32 = jnp.float32
BF16 = jnp.bfloat16
MESH = pl.DeviceIdType.MESH
NCH = 9
HALF = 48
SPLIT = (0, 1)


class Place:
    def __init__(self):
        d, t = lax.axis_index("dp"), lax.axis_index("tensor")
        self.x, self.z = lax.rem(d, 2), lax.div(d, 2)
        self.c, self.y = lax.rem(t, 2), lax.div(t, 2)
        self.core = (d, t + 1 - 2 * self.c)
        self.ynb = (d, lax.rem(t + 2, 4))
        self.xnb = (d + 1 - 2 * self.x, t)
        self.zup = (lax.rem(d + 2, 8), t)
        self.zdn = (lax.rem(d + 6, 8), t)
        self.zfar = (lax.rem(d + 4, 8), t)
        self.along = (self.zup, self.zfar, self.zdn)
        self.diag = (d + 1 - 2 * self.x, lax.rem(t + 2, 4))

    def zrel(self, s):
        return lax.rem(self.z + 4 - s, 4)

    def barrier(self):
        bar = pltpu.get_barrier_semaphore()
        near = (self.core, self.ynb, self.xnb, self.diag, self.zup, self.zdn, self.zfar)
        for dev in near:
            pl.semaphore_signal(bar, inc=1, device_id=dev, device_id_type=MESH)
        pl.semaphore_wait(bar, len(near))


class Gather:
    COPIES = 11

    def __init__(self, p, own, w, ss, rs):
        self.p, self.own, self.w, self.ss, self.rs = p, own, w, ss, rs

    def copy(self, src, dst, n, k, dev):
        return pltpu.make_async_remote_copy(
            src, dst, send_sem=self.ss.at[n, k], recv_sem=self.rs.at[n, k], device_id=dev, device_id_type=MESH
        )

    def part(self, n, k):
        p, w = self.p, self.w
        x, y, c = p.x, p.y, p.c
        lo, hi = pl.ds(0, HALF), pl.ds(HALF, HALF)
        line = lambda yy, cc, xx: w.at[n, yy, cc, :, xx]
        if k < 3:
            return w.at[n, y, c, p.z, x], w.at[n, y, c, p.zrel(k + 1), x], p.along[k]
        if k == 3:
            return line(y, c, x), line(y, c, 1 - x), p.xnb
        if k == 4:
            return line(y, c, x), line(1 - y, c, x), p.ynb
        if k == 5:
            return line(y, c, x), line(y, 1 - c, x), p.core
        if k == 6:
            return w.at[n, y, c, :, 1 - x, lo], w.at[n, 1 - y, c, :, 1 - x, lo], p.ynb
        if k == 7:
            return line(y, c, 1 - x), line(y, 1 - c, 1 - x), p.core
        if k == 8:
            return w.at[n, 1 - y, c, :, x, hi], w.at[n, 1 - y, c, :, 1 - x, hi], p.xnb
        if k == 9:
            return line(1 - y, c, x), line(1 - y, 1 - c, x), p.core
        return line(1 - y, c, 1 - x), line(1 - y, 1 - c, 1 - x), p.core

    def start(self, n, *ks):
        for k in ks:
            src, _, dev = self.part(n, k)
            self.copy(src, src, n, k, dev).start()

    def pieces(self, n, hops):
        p = self.p
        for s in hops:
            at = self.w.at[n, p.y, p.c, p.zrel(s), p.x]
            for k, dev in ((3, p.xnb), (4, p.ynb), (5, p.core)):
                self.copy(self.own.at[n] if s == 0 else at, at, n, k, dev).start()

    def arrive(self, n, *ks):
        for k in ks:
            _, mine, dev = self.part(n, k)
            self.copy(mine, mine, n, k, dev).wait_recv()

    def finish(self, n):
        for k in range(self.COPIES):
            src, _, dev = self.part(n, k)
            self.copy(src, src, n, k, dev).wait_send()

    def stage(self, n, s):
        p = self.p
        if s == 0:
            at = self.w.at[n, p.y, p.c, p.z, p.x]
            for k in range(3):
                self.copy(self.own.at[n], at, n, k, p.along[k]).start()
            if n in SPLIT:
                self.pieces(n, (0,))
        elif s == 1 and n in SPLIT:
            for k in range(3):
                self.arrive(n, k)
                self.pieces(n, (k + 1,))
        elif s == 1:
            self.arrive(n, 0, 1, 2)
            self.start(n, 3, 4, 5)
        elif s == 2:
            self.arrive(n, 3)
            self.start(n, 6, 7)
        elif s == 3:
            self.arrive(n, 4)
            self.start(n, 8, 9)
        elif s == 4:
            self.arrive(n, 6, 8)
            self.start(n, 10)
        else:
            self.arrive(n, 5, 7, 9, 10)


class Scatter:
    COPIES = 8

    def __init__(self, p, g, out, rc, rd, rl, rz, ss, rs):
        self.p, self.g, self.out, self.rc, self.rd, self.rl, self.rz = p, g, out, rc, rd, rl, rz
        self.ss, self.rs = ss, rs

    def chunk(self, m):
        return (m + 3) % NCH

    def at(self, m, y, c, *rest):
        n = self.chunk(m)
        if n > 2:
            return self.g.at[(n, y, c) + rest]
        return self.rc.at[(pl.ds(2 * n, 2) if isinstance(y, slice) else 2 * n + y, c) + rest]

    def part(self, m, k):
        p, every = self.p, slice(None)
        x, y, c = p.x, p.y, p.c
        lo, hi = pl.ds(0, HALF), pl.ds(HALF, HALF)
        if k == 0:
            return self.at(m, every, 1 - c), self.rc.at[m], p.core
        if k == 1:
            return self.at(m, 1 - y, c, every, 1 - x, lo), self.rd.at[m, 0], p.ynb
        if k == 2:
            return self.at(m, 1 - y, c, every, 1 - x, hi), self.rd.at[m, 1], p.xnb
        if k == 3:
            return self.at(m, y, c, every, 1 - x), self.rl.at[m, 0], p.xnb
        if k == 4:
            return self.at(m, 1 - y, c, every, x), self.rl.at[m, 1], p.ynb
        return self.at(m, y, c, p.zrel(8 - k), x), self.rz.at[m, k - 5], p.along[k - 5]

    def copy(self, m, k):
        src, dst, dev = self.part(m, k)
        return pltpu.make_async_remote_copy(
            src, dst, send_sem=self.ss.at[m, k], recv_sem=self.rs.at[m, k], device_id=dev, device_id_type=MESH
        )

    def start(self, m, *ks):
        for k in ks:
            self.copy(m, k).start()

    def arrive(self, m, *ks):
        for k in ks:
            self.copy(m, k).wait_recv()

    def finish(self, m):
        for k in range(self.COPIES):
            self.copy(m, k).wait_send()

    def add(self, ref, *others):
        if len(others) == 1:
            ref[...] += others[0][...]
        else:
            ref[...] = sum((o[...].astype(F32) for o in others), ref[...].astype(F32)).astype(BF16)

    def stage(self, m, s):
        p, every = self.p, slice(None)
        x, y, c = p.x, p.y, p.c
        lo, hi = pl.ds(0, HALF), pl.ds(HALF, HALF)
        if s == 0:
            self.start(m, 0)
        elif s == 1:
            self.arrive(m, 0)
            self.add(self.at(m, 1 - y, c, every, 1 - x), self.rc.at[m, 1 - y, :, 1 - x])
            self.start(m, 1, 2)
            self.add(self.at(m, y, c), self.rc.at[m, y])
            self.add(self.at(m, 1 - y, c, every, x), self.rc.at[m, 1 - y, :, x])
        elif s == 2:
            self.arrive(m, 1)
            self.add(self.at(m, y, c, every, 1 - x, lo), self.rd.at[m, 0])
            self.start(m, 3)
        elif s == 3:
            self.arrive(m, 2)
            self.add(self.at(m, 1 - y, c, every, x, hi), self.rd.at[m, 1])
            self.start(m, 4)
        elif s == 4:
            self.arrive(m, 3, 4)
            self.add(self.at(m, y, c, every, x), self.rl.at[m, 0], self.rl.at[m, 1])
            self.start(m, 5, 6, 7)
        else:
            self.arrive(m, 5, 6, 7)
            total = self.at(m, y, c, p.z, x)[...].astype(F32)
            for k in range(3):
                total += self.rz[m, k].astype(F32)
            self.out[self.chunk(m)] = total


WSHAPE = (NCH, 2, 2, 4, 2, 96, 256)
ROWS = 784
DM = 768
PARTS = ((0, 400), (400, 384))
STEP = 112
LOG2E = math.log2(math.e)
CS = LOG2E / 8
BIG = 1e30


def nt(a, b):
    return lax.dot_general(a, b, (((1,), (1,)), ((), ())), preferred_element_type=F32)


def tn(a, b):
    return lax.dot_general(a, b, (((0,), (0,)), ((), ())), preferred_element_type=F32)


def nn(a, b):
    return jnp.dot(a, b, preferred_element_type=F32)


def split3(a):
    one = a.astype(BF16)
    rest = a - one.astype(F32)
    two = rest.astype(BF16)
    return one, two, (rest - two.astype(F32)).astype(BF16)


def turn(a):
    return pltpu.roll(a.astype(F32), 64, 1)


def standard(values):
    centred = values - jnp.mean(values, axis=-1, keepdims=True)
    inverse = lax.rsqrt(jnp.mean(centred * centred, axis=-1, keepdims=True) + 1e-06)
    return centred * inverse, inverse


def norm_pull(grad, scaled, inverse, gain):
    g = grad * gain
    return inverse * (
        g - jnp.mean(g, axis=-1, keepdims=True) - scaled * jnp.mean(g * scaled, axis=-1, keepdims=True)
    )


def gelu_slope(v):
    cdf = 0.5 + 0.5 * lax.erf(v * math.sqrt(0.5))
    return v * cdf, cdf + v * (jnp.exp(-0.5 * v * v) * (1.0 / math.sqrt(2.0 * math.pi)))


def rows_of(i):
    return pl.ds(pl.multiple_of(i * STEP, 16), STEP)


def fold(values):
    return jnp.sum(values.reshape(STEP // 8, 8, values.shape[1]), axis=0)


def head_slot(g):
    return (g % 3) * 4 + g // 3


class Layer:
    def __init__(self, refs):
        self.__dict__.update(refs)

    def mat(self, n, y, c):
        return self.w[n, y, c].reshape(DM, 256)

    def put(self, n, y, c, value):
        self.w[n, y, c] = value.astype(BF16).reshape(4, 2, 96, 256)

    def pack(self, which):
        outt = self.wout[...].astype(F32).T
        q, k, v = (self.qkv[a].astype(F32) for a in range(3))
        for j in which:
            cols = slice(64 * j, 64 * j + 64)
            self.own[j] = jnp.concatenate([a[:, cols] for a in (q, v, k, outt)], axis=1).astype(BF16)
            if j > 0:
                for i in (0, j) if j == 1 else (j,):
                    wide = slice(256 * i, 256 * i + 256)
                    self.own[3 + 2 * i] = self.up[:, wide]
                    self.own[4 + 2 * i] = self.down[:, wide]

    def prepare(self, t):
        for k in range(12):
            for b in range(6):
                self.vec[k : k + 1, 128 * b : 128 * b + 128] = self.flat[6 * k + b : 6 * k + b + 1, :]
        none = jnp.zeros((1, 128), F32)
        for g in range(12):
            cols = slice(64 * g, 64 * g + 64)
            self.bias[head_slot(g)] = jnp.concatenate([self.vec[4:5, cols], self.vec[5:6, cols], none], axis=1)
            self.bias[12 + head_slot(g)] = self.vec[7 + g // 3 : 8 + g // 3, 256 * (g % 3) : 256 * (g % 3) + 256]
        self.patches = self.pat[t]

    def masks(self):
        row = lax.broadcasted_iota(jnp.int32, (ROWS, 128), 0)
        lane = lax.broadcasted_iota(jnp.int32, (ROWS, 128), 1)
        p = jnp.full((ROWS, 128), self.patches, jnp.int32)
        image = sum(jnp.where(row >= k * p, 1, 0) for k in (1, 2, 3))
        same = jnp.where(image == lane - 64, 1.0, 0.0)
        slot = (lane >= 64) & (lane < 68)
        self.mq[...] = jnp.where(slot, (same - 1.0) * BIG, 0.0).astype(BF16)
        self.mk[...] = jnp.where(slot, same, jnp.where((lane >= 68) & (lane < 71), 1.0, 0.0)).astype(BF16)

    def norm1(self, half):
        def step(i, _):
            r = rows_of(i)
            scaled, _ = standard(self.tok[r, :].astype(F32))
            self.n1[r, :] = (scaled * self.vec[0:1, :] + self.vec[1:2, :]).astype(BF16)
            return 0

        lax.fori_loop(4 * half, 4 + 3 * half, step, 0)

    def attend(self, i):
        j, y = lax.div(i, 2), lax.rem(i, 2)
        lane = lax.broadcasted_iota(jnp.int32, (ROWS, 128), 1)
        left = lane < 64
        out_halves = []
        for c in range(2):
            h = i * 2 + c
            mixed = (nn(self.n1[...], self.mat(j, y, c)) + self.bias[h]).astype(BF16)
            self.qa[h] = jnp.where(left, mixed[:, :128], self.mq[...])
            self.ka[h] = jnp.where(left, mixed[:, 128:], self.mk[...])
            self.va[h] = jnp.where(left, jnp.ones((), BF16), mixed[:, :128])
            out_halves.append(self.mat(j, y, c)[:, 128:])
        first = lax.broadcasted_iota(jnp.int32, (DM, 128), 1) < 64
        self.ot[j, y] = jnp.where(first, turn(out_halves[0]), out_halves[1].astype(F32)).astype(BF16)
        for r0, n in PARTS:
            r = pl.ds(r0, n)
            lanes = lax.broadcasted_iota(jnp.int32, (n, 128), 1)
            results = []
            for c in range(2):
                h = i * 2 + c
                q = self.qa[h, r, :]
                s = nt(q, self.ka[h])
                top = jnp.max(s, axis=1, keepdims=True) * CS
                p = jnp.exp2(s * CS - top).astype(BF16)
                a = nn(p, self.va[h])
                total = pltpu.roll(a, 64, 1)
                results.append(a * (1.0 / total))
                h1, h2, h3 = split3((top + jnp.log2(total)) * (-1.0 / CS))
                self.qa[h, r, :] = jnp.where(
                    lanes == 68, h1, jnp.where(lanes == 69, h2, jnp.where(lanes == 70, h3, q))
                )
            pair = jnp.where(lanes < 64, pltpu.roll(results[0], 64, 1), results[1])
            self.att[j, y, r, :] = pair.astype(BF16)

    def pair(self, ref, j, r=slice(None)):
        return jnp.concatenate([ref[j, 0, r, :], ref[j, 1, r, :]], axis=1)

    def project(self):
        for r0, n in PARTS:
            r = pl.ds(r0, n)
            total = sum(nt(self.pair(self.att, j, r), self.pair(self.ot, j)) for j in range(3))
            self.res[r, :] = total + (self.tok[r, :].astype(F32) + self.vec[6:7, :])

        def step(i, _):
            r = rows_of(i)
            v = self.res[r, :]
            scaled, _ = standard(v)
            self.n2[r, :] = (scaled * self.vec[2:3, :] + self.vec[3:4, :]).astype(BF16)
            self.acc[r, :] = v + self.vec[11:12, :]
            self.gn[r, :] = jnp.zeros((STEP, DM), F32)
            return 0

        lax.fori_loop(0, ROWS // STEP, step, 0)

    def feed(self, i, pause):
        j, y = lax.div(i, 2), lax.rem(i, 2)
        nb, nc = 3 + 2 * j, 4 + 2 * j
        sums = [0.0, 0.0]
        for half, (r0, n) in enumerate(PARTS):
            r = pl.ds(r0, n)
            for c in range(2):
                cols = slice(c * 256, c * 256 + 256)
                pre = nn(self.n2[r, :], self.mat(nb, y, c)) + self.bias[12 + i * 2 + c]
                up = nn(self.cot[r, :], self.mat(nc, y, c))
                active, slope = gelu_slope(pre)
                grad = (up * slope).astype(BF16)
                self.act[r, cols] = active.astype(BF16)
                self.gp[r, cols] = grad
                sums[c] += jnp.sum(grad.astype(F32).reshape(n // 8, 8, 256), axis=0)
            self.acc[r, :] += nt(self.act[r, 0:256], self.mat(nc, y, 0)) + nt(
                self.act[r, 256:512], self.mat(nc, y, 1)
            )
            self.gn[r, :] += nt(self.gp[r, 0:256], self.mat(nb, y, 0)) + nt(
                self.gp[r, 256:512], self.mat(nb, y, 1)
            )
            pause(half)
        for c in range(2):
            cols = slice(c * 256, c * 256 + 256)
            self.hs[12 + i * 2 + c] = jnp.sum(sums[c], axis=0, keepdims=True)
            self.put(nc, y, c, tn(self.cot[...], self.act[:, cols]))
            self.put(nb, y, c, tn(self.n2[...], self.gp[:, cols]))
        pause(2)

    def residual_back(self):
        self.vs[...] = jnp.zeros(self.vs.shape, F32)

        def step(i, _):
            r = rows_of(i)
            self.out[r, :] = self.acc[r, :].astype(BF16)
            scaled, inverse = standard(self.res[r, :])
            g = self.gn[r, :]
            ct = self.cot[r, :].astype(F32)
            grad = ct + norm_pull(g, scaled, inverse, self.vec[2:3, :])
            self.res[r, :] = grad
            self.gb[r, :] = grad.astype(BF16)
            self.gn[r, :] = jnp.zeros((STEP, DM), F32)
            for k, v in ((2, g * scaled), (3, g), (4, grad), (5, ct)):
                self.vs[k] += fold(v)
            return 0

        lax.fori_loop(0, ROWS // STEP, step, 0)

    def attend_back(self, i, pause):
        j, y = lax.div(i, 2), lax.rem(i, 2)
        lane = lax.broadcasted_iota(jnp.int32, (ROWS, 128), 1)
        left = lane < 64
        low = nn(self.gb[...], self.ot[j, y]).astype(BF16)
        wide = low.astype(F32)
        product = wide * self.att[j, y].astype(F32)
        for c in range(2):
            h = i * 2 + c
            delta = jnp.sum(jnp.where(left == (c == 0), product, 0.0), axis=1, keepdims=True)
            d1, d2, d3 = split3(jnp.broadcast_to(-delta, (ROWS, 128)))
            moved = pltpu.roll(wide, 64, 1).astype(BF16) if c == 0 else low
            none = jnp.zeros((), BF16)
            extra = jnp.where(lane == 0, d1, jnp.where(lane == 1, d2, jnp.where(lane == 2, d3, none)))
            self.act[:, 0:128] = jnp.where(left, extra, moved)
            dv = dk = 0.0
            for r0, n in PARTS:
                r = pl.ds(r0, n)
                q, d = self.qa[h, r, :], self.act[r, 0:128]
                p = jnp.exp2(nt(q, self.ka[h]) * CS)
                ds = (p * nt(d, self.va[h])).astype(BF16)
                dv += tn(p.astype(BF16), d)
                dk += tn(ds, q)
                self.acc[r, 0:128] = nn(ds, self.ka[h])
            self.qa[h] = jnp.where(left, self.acc[:, 0:128] * 0.125, dv).astype(BF16)
            self.ka[h] = jnp.where(left, (dk * 0.125).astype(BF16), none)
            sums = jnp.sum(self.mixed_grad(h).astype(F32).reshape(ROWS // 8, 8, 256), axis=0)
            self.hs[h] = jnp.sum(sums, axis=0, keepdims=True)
            pause(c)
        outg = tn(self.gb[...], self.att[j, y])
        first = lax.broadcasted_iota(jnp.int32, (DM, 128), 1) < 64
        for c in range(2):
            g = tn(self.n1[...], self.mixed_grad(i * 2 + c))
            mine = pltpu.roll(outg, 64, 1) if c == 0 else outg
            whole = jnp.concatenate([g[:, :128], jnp.where(first, g[:, 128:], mine)], axis=1)
            self.rc[i, c] = whole.astype(BF16).reshape(4, 2, 96, 256)
        pause(2)

    def mixed_grad(self, h, r=slice(None)):
        return jnp.concatenate([self.qa[h, r, :], self.ka[h, r, :]], axis=1)

    def mixed_back(self, j):
        for r0, n in PARTS:
            r = pl.ds(r0, n)
            self.gn[r, :] += sum(
                nt(self.mixed_grad(4 * j + 2 * y + c, r), self.mat(j, y, c)) for y in range(2) for c in range(2)
            )

    def token_back(self, half):
        def step(i, _):
            r = rows_of(i)
            scaled, inverse = standard(self.tok[r, :].astype(F32))
            g = self.gn[r, :]
            grad = self.res[r, :] + norm_pull(g, scaled, inverse, self.vec[0:1, :])
            self.gtok[r, :] = grad.astype(BF16)
            self.vs[0] += fold(g * scaled)
            self.vs[1] += fold(g)
            return 0

        lax.fori_loop(4 * half, 4 + 3 * half, step, 0)

    def collect(self):
        for h in range(24):
            self.vsum[h : h + 1, :] = self.hs[h]
        for k in range(6):
            row = jnp.sum(self.vs[k], axis=0, keepdims=True)
            for b in range(3):
                self.vsum[24 + 3 * k + b : 25 + 3 * k + b, :] = row[:, 256 * b : 256 * b + 256]
        self.vsum[42:48, :] = jnp.zeros((6, 256), F32)


def layer_scratch():
    return dict(
        w=pltpu.VMEM(WSHAPE, BF16),
        n1=pltpu.VMEM((ROWS, DM), BF16),
        n2=pltpu.VMEM((ROWS, DM), BF16),
        gb=pltpu.VMEM((ROWS, DM), BF16),
        qa=pltpu.VMEM((12, ROWS, 128), BF16),
        ka=pltpu.VMEM((12, ROWS, 128), BF16),
        va=pltpu.VMEM((12, ROWS, 128), BF16),
        att=pltpu.VMEM((3, 2, ROWS, 128), BF16),
        ot=pltpu.VMEM((3, 2, DM, 128), BF16),
        res=pltpu.VMEM((ROWS, DM), F32),
        acc=pltpu.VMEM((ROWS, DM), F32),
        gn=pltpu.VMEM((ROWS, DM), F32),
        mq=pltpu.VMEM((ROWS, 128), BF16),
        mk=pltpu.VMEM((ROWS, 128), BF16),
        act=pltpu.VMEM((ROWS, 512), BF16),
        gp=pltpu.VMEM((ROWS, 512), BF16),
        vs=pltpu.VMEM((6, 8, DM), F32),
        hs=pltpu.VMEM((24, 1, 256), F32),
        own=pltpu.VMEM((NCH, 96, 256), BF16),
        vec=pltpu.VMEM((12, DM), F32),
        bias=pltpu.VMEM((24, 1, 256), F32),
    )


NAMES_IN = ("tok", "cot", "qkv", "wout", "up", "down", "flat", "pat")
NAMES_OUT = ("out", "gtok", "gsh", "vsum")


PLAN = {
    "s0": ((0, 0, 0),),
    "s1": ((0, 1, 0),),
    "s2": ((0, 2, 0), (0, 3, 0),),
    "s3": ((0, 4, 0), (0, 5, 0), (0, 0, 1), (0, 1, 1), (0, 0, 2), (0, 0, 3), (0, 2, 1), (0, 1, 2), (0, 1, 3), (0, 0, 4), (0, 3, 1), (0, 0, 5),),
    ("a", 0, 0): ((0, 2, 2), (0, 2, 3), (0, 4, 1),),
    ("a", 1, 0): ((0, 1, 4), (0, 5, 1), (0, 1, 5),),
    ("a", 2, 0): ((0, 2, 4), (0, 3, 2), (0, 3, 3), (0, 6, 0),),
    ("a", 3, 0): ((0, 2, 5), (0, 7, 0),),
    ("a", 4, 0): ((0, 4, 2), (0, 4, 3), (0, 6, 1),),
    ("a", 5, 0): ((0, 3, 4), (0, 5, 2), (0, 5, 3),),
    "p": ((0, 3, 5), (0, 4, 4), (0, 7, 1), (0, 8, 0), (0, 4, 5),),
    ("f", 0, 0): ((0, 6, 2), (0, 6, 3),),
    ("f", 0, 1): ((0, 5, 4),),
    ("f", 0, 2): ((0, 5, 5),),
    ("f", 1, 0): ((0, 8, 1),),
    ("f", 1, 1): ((0, 7, 2), (0, 7, 3),),
    ("f", 1, 2): ((0, 6, 4), (1, 0, 0), (1, 1, 0), (0, 6, 5),),
    ("f", 2, 0): ((1, 0, 1),),
    ("f", 2, 1): ((0, 8, 2), (0, 8, 3), (1, 1, 1),),
    ("f", 2, 2): ((0, 7, 4),),
    ("f", 3, 0): ((0, 7, 5), (1, 0, 2), (1, 0, 3),),
    ("f", 3, 1): ((0, 8, 4),),
    ("f", 3, 2): ((0, 8, 5), (1, 1, 2), (1, 1, 3), (1, 2, 0), (1, 3, 0),),
    ("f", 4, 1): ((1, 2, 1),),
    ("f", 4, 2): ((1, 0, 4), (1, 3, 1),),
    ("f", 5, 1): ((1, 1, 4),),
    ("f", 5, 2): ((1, 2, 2), (1, 2, 3), (1, 4, 0), (1, 5, 0),),
    "q": ((1, 0, 5), (1, 3, 2), (1, 3, 3), (1, 4, 1), (1, 5, 1),),
    ("b", 0, 0): ((1, 1, 5), (1, 2, 4),),
    ("b", 0, 2): ((1, 3, 4),),
    ("b", 1, 0): ((1, 2, 5), (1, 4, 2), (1, 4, 3),),
    ("b", 1, 1): ((1, 5, 2), (1, 5, 3),),
    ("b", 1, 2): ((1, 3, 5), (1, 6, 0),),
    ("b", 2, 0): ((1, 4, 4), (1, 6, 1),),
    ("b", 2, 2): ((1, 5, 4),),
    ("b", 3, 0): ((1, 4, 5), (1, 6, 2), (1, 6, 3),),
    ("b", 3, 2): ((1, 5, 5), (1, 7, 0),),
    ("b", 4, 0): ((1, 6, 4), (1, 7, 1),),
    ("b", 4, 2): ((1, 7, 2), (1, 7, 3),),
    ("b", 5, 0): ((1, 6, 5),),
    ("b", 5, 2): ((1, 8, 0), (1, 7, 4),),
    ("u", 1): ((1, 8, 1),),
    ("t", 1): ((1, 7, 5), (1, 8, 2), (1, 8, 3),),
    "end": ((2, 0, 0), (2, 0, 1), (1, 8, 4), (2, 0, 2), (1, 8, 5), (2, 0, 3),),
}


class Totals:
    def __init__(self, p, value, vr, ss, rs):
        self.p, self.value, self.vr, self.ss, self.rs = p, value, vr, ss, rs
        self.mine = (1 + 2 * p.y + p.x, 5 + p.z)
        self.to = (p.core, p.xnb, p.ynb, p.diag) + p.along
        x, y = p.x, p.y
        self.there = (0, 1 + 2 * y + 1 - x, 1 + 2 * (1 - y) + x, 1 + 2 * (1 - y) + 1 - x) + tuple(
            5 + p.zrel(s) for s in (1, 2, 3)
        )

    def copy(self, k, src, dst):
        return pltpu.make_async_remote_copy(
            src, dst, send_sem=self.ss.at[k], recv_sem=self.rs.at[k], device_id=self.to[k], device_id_type=MESH
        )

    def arrive(self, *ks):
        for k in ks:
            slot = self.vr.at[self.there[k]]
            self.copy(k, slot, slot).wait_recv()

    def send(self, *ks):
        slot = self.vr.at[self.mine[0] if ks[0] < 4 else self.mine[1]]
        for k in ks:
            self.copy(k, slot, slot).start()

    def finish(self, _):
        for k in range(1, 7):
            self.copy(k, self.vr.at[0], self.vr.at[0]).wait_send()

    def stage(self, _, s):
        if s == 0:
            self.copy(0, self.value, self.vr.at[0]).start()
        elif s == 1:
            self.arrive(0)
            self.vr[self.mine[0]] = self.value[...] + self.vr[0]
            self.send(1, 2, 3)
        elif s == 2:
            self.arrive(1, 2, 3)
            self.vr[self.mine[1]] = (self.vr[1] + self.vr[2]) + (self.vr[3] + self.vr[4])
            self.send(4, 5, 6)
        else:
            self.arrive(4, 5, 6)
            self.copy(0, self.value, self.value).wait_send()
            self.value[...] = (self.vr[5] + self.vr[6]) + (self.vr[7] + self.vr[8])


def mega_kernel(names, *refs):
    r = dict(zip(names, refs))
    layer = Layer(r)
    p = Place()
    p.barrier()
    gather = Gather(p, r["own"], r["w"], r["gss"], r["grs"])
    scatter = Scatter(p, r["w"], r["gsh"], r["rc"], r["rd"], r["rl"], r["rz"], r["sss"], r["srs"])
    totals = Totals(p, r["vsum"], r["vr"], r["vss"], r["vrs"])

    engines = (gather, scatter, totals)

    def at(site):
        for e, n, s in PLAN.get(site, ()):
            engines[e].stage(n, s)

    def within(kind, i, k=0):
        for turn in range(6):
            if (kind, turn, k) in PLAN:
                pl.when(i == turn)(functools.partial(at, (kind, turn, k)))

    def loop(count, body):
        lax.fori_loop(0, count, lambda i, c: (body(i), c)[1], 0)

    layer.pack((0,))
    at("s0")
    layer.pack((1, 2))
    for n in range(NCH):
        r["w"][n, p.y, p.c, p.z, p.x] = r["own"][n]
    layer.prepare(lax.axis_index("tensor"))
    layer.masks()
    at("s1")
    layer.norm1(0)
    at("s2")
    layer.norm1(1)
    at("s3")

    def attend(i):
        layer.attend(i)
        within("a", i)

    loop(6, attend)
    layer.project()
    at("p")

    def feed(i):
        @pl.when(lax.rem(i, 2) == 0)
        def _():
            gather.finish(3 + i)
            gather.finish(4 + i)

        layer.feed(i, functools.partial(within, "f", i))

    loop(6, feed)
    layer.residual_back()
    at("q")
    loop(6, lambda i: layer.attend_back(i, functools.partial(within, "b", i)))
    for j in range(3):
        layer.mixed_back(j)
        at(("u", j))
    for half in range(2):
        layer.token_back(half)
        at(("t", half))
    layer.collect()
    at("end")
    for n in range(3):
        gather.finish(n)
    for m in range(NCH):
        scatter.finish(m)
    totals.finish(0)


def mega_scratch():
    return dict(
        layer_scratch(),
        rc=pltpu.VMEM((NCH, 2, 4, 2, 96, 256), BF16),
        rd=pltpu.VMEM((NCH, 2, 4, HALF, 256), BF16),
        rl=pltpu.VMEM((NCH, 2, 4, 96, 256), BF16),
        rz=pltpu.VMEM((NCH, 3, 96, 256), BF16),
        vr=pltpu.VMEM((9, 48, 256), F32),
        gss=pltpu.SemaphoreType.DMA((NCH, Gather.COPIES)),
        grs=pltpu.SemaphoreType.DMA((NCH, Gather.COPIES)),
        sss=pltpu.SemaphoreType.DMA((NCH, Scatter.COPIES)),
        srs=pltpu.SemaphoreType.DMA((NCH, Scatter.COPIES)),
        vss=pltpu.SemaphoreType.DMA((7,)),
        vrs=pltpu.SemaphoreType.DMA((7,)),
    )


def mega_call(*args):
    scratch = mega_scratch()
    names = NAMES_IN + NAMES_OUT + tuple(scratch)
    vm = pl.BlockSpec(memory_space=pltpu.VMEM)
    shape = jax.ShapeDtypeStruct
    return pl.pallas_call(
        functools.partial(mega_kernel, names),
        out_shape=(
            shape((ROWS, DM), BF16),
            shape((ROWS, DM), BF16),
            shape((NCH, 96, 256), F32),
            shape((48, 256), F32),
        ),
        in_specs=[vm] * (len(NAMES_IN) - 1) + [pl.BlockSpec(memory_space=pltpu.SMEM)],
        out_specs=(vm,) * len(NAMES_OUT),
        scratch_shapes=list(scratch.values()),
        compiler_params=pltpu.CompilerParams(collective_id=0, has_side_effects=True, vmem_limit_bytes=62 << 20),
    )(*args)


def tail_kernel(names, *refs):
    r = dict(zip(names, refs))
    r["out"][...] = r["out_in"][...]
    r["gtok"][...] = r["gtok_in"][...]
    g = r["gsh"]
    for j in range(3):
        cols = slice(64 * j, 64 * j + 64)
        for a, k in enumerate((0, 128, 64)):
            r["gqkv"][a, :, cols] = g[j, :, k : k + 64]
        r["gup"][:, 256 * j : 256 * j + 256] = g[3 + 2 * j]
        r["gdown"][:, 256 * j : 256 * j + 256] = g[4 + 2 * j]
        r["gout"][cols, :] = g[j, :, 128:256].T[64:128, :]
    v, gv = r["vsum"], r["gvec"]
    for k, row in enumerate((0, 1, 2, 3, 6, 11)):
        for b in range(6):
            gv[6 * row + b : 6 * row + b + 1, :] = v[24 + 3 * k + b // 2 : 25 + 3 * k + b // 2, 128 * (b % 2) : 128 * (b % 2) + 128]
    for half in range(2):
        for b in range(6):
            two = [v[h : h + 1, 64 * half : 64 * half + 64] for h in (head_slot(2 * b), head_slot(2 * b + 1))]
            gv[24 + 6 * half + b : 25 + 6 * half + b, :] = jnp.concatenate(two, axis=1)
    for t in range(4):
        for b in range(6):
            row = 12 + (b // 2) * 4 + t
            gv[42 + 6 * t + b : 43 + 6 * t + b, :] = v[row : row + 1, 128 * (b % 2) : 128 * (b % 2) + 128]
    rate = r["rate"][0]
    for name in ("qkv", "wout", "up", "down", "vec"):
        r["next_" + name][...] = rate * r["target_" + name][...] + (1.0 - rate) * r[name][...].astype(F32)


def tail_call(results, online, targets, momentum):
    five = ("qkv", "wout", "up", "down", "vec")
    ins = ("out_in", "gtok_in", "gsh", "vsum") + five + tuple("target_" + a for a in five) + ("rate",)
    outs = ("out", "gtok", "gqkv", "gout", "gup", "gdown", "gvec") + tuple("next_" + a for a in five)
    vm = pl.BlockSpec(memory_space=pltpu.VMEM)
    shape = jax.ShapeDtypeStruct
    like = [shape(a.shape, F32) for a in online]
    return pl.pallas_call(
        functools.partial(tail_kernel, ins + outs),
        out_shape=[shape(results[0].shape, BF16), shape(results[1].shape, BF16)] + like + like,
        in_specs=[vm] * 14 + [pl.BlockSpec(memory_space=pltpu.SMEM)],
        out_specs=[vm] * 12,
    )(*results, *online, *targets, momentum)


HD = 64
BOTH = ("dp", "tensor")


def unpack(vectors, d, ff):
    cuts = [d * i for i in range(8)] + [7 * d + ff, 8 * d + ff]
    return tuple(vectors[a:b] for a, b in zip(cuts[:-1], cuts[1:]))


def norm_parts(values):
    centred = values - jnp.mean(values, axis=-1, keepdims=True)
    inverse = lax.rsqrt(jnp.mean(centred * centred, axis=-1, keepdims=True) + 1e-06)
    return centred * inverse, inverse


def norm_backward(grad_normed, scaled, inverse, gain):
    weighted = grad_normed * gain
    return inverse * (
        weighted
        - jnp.mean(weighted, axis=-1, keepdims=True)
        - scaled * jnp.mean(weighted * scaled, axis=-1, keepdims=True)
    )


def gelu_parts(v):
    cdf = 0.5 * (1.0 + lax.erf(v * (0.5**0.5)))
    return v * cdf, cdf + v * jnp.exp(-0.5 * v * v) * ((2.0 * jnp.pi) ** -0.5)


def dot(a, b, dims):
    return lax.dot_general(a, b, (dims, ((), ())), preferred_element_type=F32)


def pack_shards(qkv, out, up, down):
    first = jnp.concatenate([qkv[0], qkv[1], qkv[2], out.T], axis=1)
    return jnp.stack([first, up, down.T])


def gather_blocks(shards, dp, tensor):
    every = lax.all_gather(shards, BOTH, axis=0)
    b, r, c = shards.shape
    every = every.reshape(dp, tensor, b, r, c).transpose(2, 1, 0, 3, 4)
    return every.reshape(b, tensor, dp * r, c)


def scatter_blocks(blocks, dp, tensor):
    b, t, rows, c = blocks.shape
    r = rows // dp
    pieces = blocks.reshape(b, tensor, dp, r, c).transpose(2, 1, 0, 3, 4)
    pieces = pieces.reshape(dp * tensor, b, r, c)
    return lax.psum_scatter(pieces, BOTH, scatter_dimension=0, tiled=True)[0]


def local_layer(tokens, cotangent, patches, blocks, vectors):
    rows, d = tokens.shape
    tensor, c = blocks.shape[1], blocks.shape[3]
    w = c // 4
    ff = tensor * c
    heads = d // HD
    gain1, bias1, gain2, bias2, bias_q, bias_v, bias_out, bias_up, bias_down = unpack(
        vectors, d, ff
    )
    first, up, downt = blocks[0], blocks[1], blocks[2]
    factor = HD**-0.5

    x = tokens.astype(F32)
    scaled1, inverse1 = norm_parts(x)
    normed1 = (scaled1 * gain1 + bias1).astype(BF16)
    mixed = jnp.einsum("rd,tdc->rtc", normed1, first[:, :, : 3 * w], preferred_element_type=F32)
    query = (mixed[:, :, :w].reshape(rows, d) + bias_q).astype(BF16).reshape(rows, heads, HD)
    key = mixed[:, :, w : 2 * w].reshape(rows, d).astype(BF16).reshape(rows, heads, HD)
    value = (mixed[:, :, 2 * w :].reshape(rows, d) + bias_v).astype(BF16).reshape(rows, heads, HD)
    images = jnp.arange(rows, dtype=jnp.int32) // patches
    allowed = images[:, None] == images[None, :]
    scores = jnp.einsum("qhd,khd->hqk", query, key, preferred_element_type=F32) * factor
    scores = jnp.where(allowed[None], scores, -1e30)
    raised = jnp.exp(scores - jnp.max(scores, axis=-1, keepdims=True))
    soft = raised / jnp.sum(raised, axis=-1, keepdims=True)
    soft_low = soft.astype(BF16)
    attended = jnp.einsum("hqk,khd->qhd", soft_low, value, preferred_element_type=F32).astype(BF16)
    flat = attended.reshape(rows, tensor, w)
    outt = first[:, :, 3 * w :]
    residual = x + jnp.einsum("rte,tde->rd", flat, outt, preferred_element_type=F32) + bias_out
    scaled2, inverse2 = norm_parts(residual)
    normed2 = (scaled2 * gain2 + bias2).astype(BF16)
    pre = jnp.einsum("rd,tdf->rtf", normed2, up, preferred_element_type=F32) + bias_up.reshape(
        tensor, c
    )
    active, slope = gelu_parts(pre)
    active = active.astype(BF16)
    second = jnp.einsum("rtf,tdf->rd", active, downt, preferred_element_type=F32)
    output = (residual + second + bias_down).astype(BF16)

    grad_active = jnp.einsum("rd,tdf->rtf", cotangent, downt, preferred_element_type=F32)
    grad_pre = (grad_active * slope).astype(BF16)
    g_down = jnp.einsum("rd,rtf->tdf", cotangent, active, preferred_element_type=F32)
    g_up = jnp.einsum("rd,rtf->tdf", normed2, grad_pre, preferred_element_type=F32)
    grad_normed2 = jnp.einsum("rtf,tdf->rd", grad_pre, up, preferred_element_type=F32)
    grad_result = cotangent.astype(F32)
    grad_residual = grad_result + norm_backward(grad_normed2, scaled2, inverse2, gain2)
    grad_branch = grad_residual.astype(BF16)
    g_outt = jnp.einsum("rd,rte->tde", grad_branch, flat, preferred_element_type=F32)
    grad_att = jnp.einsum("rd,tde->rte", grad_branch, outt, preferred_element_type=F32)
    grad_att = grad_att.astype(BF16).reshape(rows, heads, HD)
    grad_value = jnp.einsum("hqk,qhd->khd", soft_low, grad_att, preferred_element_type=F32)
    grad_soft = jnp.einsum("qhd,khd->hqk", grad_att, value, preferred_element_type=F32)
    grad_scores = (
        soft * (grad_soft - jnp.sum(soft * grad_soft, axis=-1, keepdims=True))
    ).astype(BF16)
    grad_query = (
        jnp.einsum("hqk,khd->qhd", grad_scores, key, preferred_element_type=F32) * factor
    )
    grad_key = jnp.einsum("hqk,qhd->khd", grad_scores, query, preferred_element_type=F32) * factor
    three = [
        g.astype(BF16).reshape(rows, tensor, w) for g in (grad_query, grad_key, grad_value)
    ]
    grad_mixed = jnp.concatenate(three, axis=2)
    g_qkv = jnp.einsum("rd,rtc->tdc", normed1, grad_mixed, preferred_element_type=F32)
    grad_normed1 = jnp.einsum(
        "rtc,tdc->rd", grad_mixed, first[:, :, : 3 * w], preferred_element_type=F32
    )
    grad_tokens = (grad_residual + norm_backward(grad_normed1, scaled1, inverse1, gain1)).astype(
        BF16
    )
    grads = jnp.stack(
        [
            jnp.concatenate([g_qkv, g_outt], axis=2).astype(BF16),
            g_up.astype(BF16),
            g_down.astype(BF16),
        ]
    )

    def total(values):
        return jnp.sum(values.astype(F32), axis=0).reshape(-1)

    sums = jnp.concatenate(
        [
            total(grad_normed1 * scaled1),
            total(grad_normed1),
            total(grad_normed2 * scaled2),
            total(grad_normed2),
            total(three[0]),
            total(three[2]),
            total(grad_residual),
            total(grad_pre),
            total(grad_result),
        ]
    )
    return output, grad_tokens, grads, sums


def flat_views(arrays):
    qkv, out, up, down, vectors = arrays
    return qkv, out, up, down.T, vectors.reshape(72, 128)


def ringed(tokens, cotangent, block_patches, online, momentum, targets):
    online, targets = flat_views(online), flat_views(targets)
    results = mega_call(tokens, cotangent, *online, block_patches)
    final = tail_call(results, online, targets, momentum)
    return tuple(final[:2]) + tuple(
        a.T if k == 3 else a.reshape(-1) if k == 4 else a for five in (final[2:7], final[7:]) for k, a in enumerate(five)
    )


def general(dp, tensor, tokens, cotangent, patches, qkv, out, up, down, vectors):
    blocks = gather_blocks(pack_shards(qkv, out, up, down), dp, tensor)
    output, grad_tokens, grads, sums = local_layer(tokens, cotangent, patches, blocks, vectors)
    grads = scatter_blocks(grads, dp, tensor).astype(F32)
    w = qkv.shape[2]
    return (
        output,
        grad_tokens,
        jnp.stack([grads[0][:, i * w : (i + 1) * w] for i in range(3)]),
        grads[0][:, 3 * w :].T,
        grads[1],
        grads[2].T,
        lax.psum(sums, BOTH),
    )


def make_body(dp, tensor):
    def body(tokens, cotangent, block_patches, qkv, out, up, down, vectors, momentum, *targets):
        online = (qkv, out, up, down, vectors)
        if (dp, tensor) == (8, 4):
            return ringed(tokens, cotangent, block_patches, online, momentum, targets)
        patches = block_patches[lax.axis_index("tensor")]
        results = general(dp, tensor, tokens, cotangent, patches, *online)
        rate = momentum[0]
        return results + tuple(
            rate * target + (1.0 - rate) * weight.astype(F32) for target, weight in zip(targets, online)
        )

    return body


def solution(mesh):
    rows, matrices = P(BOTH, None), (
        P(None, "dp", "tensor"),
        P("tensor", "dp"),
        P("dp", "tensor"),
        P("tensor", "dp"),
    )
    return jax.shard_map(
        make_body(mesh.shape["dp"], mesh.shape["tensor"]),
        mesh=mesh,
        in_specs=(rows, rows, P("dp")) + matrices + (P(), P()) + matrices + (P(),),
        out_specs=(rows, rows) + matrices + (P(),) + matrices + (P(),),
        check_vma=False,
    )
```

```python
import functools
import math

import jax
import jax.numpy as jnp
from jax import lax
from jax.experimental import pallas as pl
from jax.experimental.pallas import tpu as pltpu
from jax.sharding import PartitionSpec as P

F32 = jnp.float32
BF16 = jnp.bfloat16
MESH = pl.DeviceIdType.MESH
NCH = 9
HALF = 48
SPLIT = (0, 1)


class Place:
    def __init__(self):
        d, t = lax.axis_index("dp"), lax.axis_index("tensor")
        self.x, self.z = lax.rem(d, 2), lax.div(d, 2)
        self.c, self.y = lax.rem(t, 2), lax.div(t, 2)
        self.core = (d, t + 1 - 2 * self.c)
        self.ynb = (d, lax.rem(t + 2, 4))
        self.xnb = (d + 1 - 2 * self.x, t)
        self.zup = (lax.rem(d + 2, 8), t)
        self.zdn = (lax.rem(d + 6, 8), t)
        self.zfar = (lax.rem(d + 4, 8), t)
        self.along = (self.zup, self.zfar, self.zdn)
        self.diag = (d + 1 - 2 * self.x, lax.rem(t + 2, 4))

    def zrel(self, s):
        return lax.rem(self.z + 4 - s, 4)

    def barrier(self):
        bar = pltpu.get_barrier_semaphore()
        near = (self.core, self.ynb, self.xnb, self.diag, self.zup, self.zdn, self.zfar)
        for dev in near:
            pl.semaphore_signal(bar, inc=1, device_id=dev, device_id_type=MESH)
        pl.semaphore_wait(bar, len(near))


class Gather:
    COPIES = 13

    def __init__(self, p, own, w, ss, rs):
        self.p, self.own, self.w, self.ss, self.rs = p, own, w, ss, rs

    def copy(self, src, dst, n, k, dev):
        return pltpu.make_async_remote_copy(
            src, dst, send_sem=self.ss.at[n, k], recv_sem=self.rs.at[n, k], device_id=dev, device_id_type=MESH
        )

    def part(self, n, k):
        p, w = self.p, self.w
        x, y, c = p.x, p.y, p.c
        lo, hi = pl.ds(0, HALF), pl.ds(HALF, HALF)
        line = lambda yy, cc, xx: w.at[n, yy, cc, :, xx]
        if k < 3:
            return w.at[n, y, c, p.z, x], w.at[n, y, c, p.zrel(k + 1), x], p.along[k]
        if k in (3, 11):
            rows = lo if k == 3 else hi
            return w.at[n, y, c, :, x, rows], w.at[n, y, c, :, 1 - x, rows], p.xnb
        if k in (4, 12):
            rows = hi if k == 4 else lo
            return w.at[n, y, c, :, x, rows], w.at[n, 1 - y, c, :, x, rows], p.ynb
        if k == 5:
            return line(y, c, x), line(y, 1 - c, x), p.core
        if k == 6:
            return w.at[n, y, c, :, 1 - x, lo], w.at[n, 1 - y, c, :, 1 - x, lo], p.ynb
        if k == 7:
            return line(y, c, 1 - x), line(y, 1 - c, 1 - x), p.core
        if k == 8:
            return w.at[n, 1 - y, c, :, x, hi], w.at[n, 1 - y, c, :, 1 - x, hi], p.xnb
        if k == 9:
            return line(1 - y, c, x), line(1 - y, 1 - c, x), p.core
        return line(1 - y, c, 1 - x), line(1 - y, 1 - c, 1 - x), p.core

    def start(self, n, *ks):
        for k in ks:
            src, _, dev = self.part(n, k)
            self.copy(src, src, n, k, dev).start()

    def pieces(self, n, hops):
        p = self.p
        lo, hi, both = pl.ds(0, HALF), pl.ds(HALF, HALF), pl.ds(0, 2 * HALF)
        for s in hops:
            for k, rows, dev in ((3, lo, p.xnb), (4, hi, p.ynb), (11, hi, p.xnb), (12, lo, p.ynb), (5, both, p.core)):
                at = self.w.at[n, p.y, p.c, p.zrel(s), p.x, rows]
                self.copy(self.own.at[n, rows] if s == 0 else at, at, n, k, dev).start()

    def arrive(self, n, *ks):
        for k in ks:
            _, mine, dev = self.part(n, k)
            self.copy(mine, mine, n, k, dev).wait_recv()

    def finish(self, n):
        for k in range(self.COPIES):
            src, _, dev = self.part(n, k)
            self.copy(src, src, n, k, dev).wait_send()

    def stage(self, n, s):
        p = self.p
        if s == 0:
            at = self.w.at[n, p.y, p.c, p.z, p.x]
            for k in range(3):
                self.copy(self.own.at[n], at, n, k, p.along[k]).start()
            if n in SPLIT:
                self.pieces(n, (0,))
        elif s == 1 and n in SPLIT:
            for k in range(3):
                self.arrive(n, k)
                self.pieces(n, (k + 1,))
        elif s == 1:
            self.arrive(n, 0, 1, 2)
            self.start(n, 3, 4, 11, 12, 5)
        elif s == 2:
            self.arrive(n, 3)
            self.start(n, 6)
        elif s == 3:
            self.arrive(n, 4)
            self.start(n, 8)
        elif s == 4:
            self.arrive(n, 11, 12)
            self.start(n, 7, 9)
        elif s == 5:
            self.arrive(n, 6, 8)
            self.start(n, 10)
        else:
            self.arrive(n, 5, 7, 9, 10)


class Scatter:
    COPIES = 10

    def __init__(self, p, g, out, rc, rd, rl, rz, ss, rs):
        self.p, self.g, self.out, self.rc, self.rd, self.rl, self.rz = p, g, out, rc, rd, rl, rz
        self.ss, self.rs = ss, rs

    def chunk(self, m):
        return (m + 3) % NCH

    def at(self, m, y, c, *rest):
        n = self.chunk(m)
        if n > 2:
            return self.g.at[(n, y, c) + rest]
        return self.rc.at[(pl.ds(2 * n, 2) if isinstance(y, slice) else 2 * n + y, c) + rest]

    def part(self, m, k):
        p, every = self.p, slice(None)
        x, y, c = p.x, p.y, p.c
        lo, hi = pl.ds(0, HALF), pl.ds(HALF, HALF)
        if k == 0:
            return self.at(m, every, 1 - c), self.rc.at[m], p.core
        if k == 1:
            return self.at(m, 1 - y, c, every, 1 - x, lo), self.rd.at[m, 0], p.ynb
        if k == 2:
            return self.at(m, 1 - y, c, every, 1 - x, hi), self.rd.at[m, 1], p.xnb
        if k in (3, 8):
            rows = lo if k == 3 else hi
            return self.at(m, y, c, every, 1 - x, rows), self.rl.at[m, 0, :, rows], p.xnb
        if k in (4, 9):
            rows = hi if k == 4 else lo
            return self.at(m, 1 - y, c, every, x, rows), self.rl.at[m, 1, :, rows], p.ynb
        return self.at(m, y, c, p.zrel(8 - k), x), self.rz.at[m, k - 5], p.along[k - 5]

    def copy(self, m, k):
        src, dst, dev = self.part(m, k)
        return pltpu.make_async_remote_copy(
            src, dst, send_sem=self.ss.at[m, k], recv_sem=self.rs.at[m, k], device_id=dev, device_id_type=MESH
        )

    def start(self, m, *ks):
        for k in ks:
            self.copy(m, k).start()

    def arrive(self, m, *ks):
        for k in ks:
            self.copy(m, k).wait_recv()

    def finish(self, m):
        for k in range(self.COPIES):
            self.copy(m, k).wait_send()

    def add(self, ref, *others):
        if len(others) == 1:
            ref[...] += others[0][...]
        else:
            ref[...] = sum((o[...].astype(F32) for o in others), ref[...].astype(F32)).astype(BF16)

    def stage(self, m, s):
        p, every = self.p, slice(None)
        x, y, c = p.x, p.y, p.c
        lo, hi = pl.ds(0, HALF), pl.ds(HALF, HALF)
        if s == 0:
            self.start(m, 0)
        elif s == 1:
            self.arrive(m, 0)
            self.add(self.at(m, 1 - y, c, every, 1 - x), self.rc.at[m, 1 - y, :, 1 - x])
            self.start(m, 1, 2)
            self.add(self.at(m, y, c), self.rc.at[m, y])
            self.add(self.at(m, 1 - y, c, every, x), self.rc.at[m, 1 - y, :, x])
            self.start(m, 8, 9)
        elif s == 2:
            self.arrive(m, 1)
            self.add(self.at(m, y, c, every, 1 - x, lo), self.rd.at[m, 0])
            self.start(m, 3)
        elif s == 3:
            self.arrive(m, 2)
            self.add(self.at(m, 1 - y, c, every, x, hi), self.rd.at[m, 1])
            self.start(m, 4)
        elif s == 4:
            self.arrive(m, 3, 4, 8, 9)
            self.add(self.at(m, y, c, every, x), self.rl.at[m, 0], self.rl.at[m, 1])
            self.start(m, 5, 6, 7)
        else:
            self.arrive(m, 5, 6, 7)
            total = self.at(m, y, c, p.z, x)[...].astype(F32)
            for k in range(3):
                total += self.rz[m, k].astype(F32)
            self.out[self.chunk(m)] = total


WSHAPE = (NCH, 2, 2, 4, 2, 96, 256)
ROWS = 784
DM = 768
PARTS = ((0, 400), (400, 384))
STEP = 112
LOG2E = math.log2(math.e)
CS = LOG2E / 8
BIG = 1e30


def nt(a, b):
    return lax.dot_general(a, b, (((1,), (1,)), ((), ())), preferred_element_type=F32)


def tn(a, b):
    return lax.dot_general(a, b, (((0,), (0,)), ((), ())), preferred_element_type=F32)


def nn(a, b):
    return jnp.dot(a, b, preferred_element_type=F32)


def split3(a):
    one = a.astype(BF16)
    rest = a - one.astype(F32)
    two = rest.astype(BF16)
    return one, two, (rest - two.astype(F32)).astype(BF16)


def turn(a):
    return pltpu.roll(a.astype(F32), 64, 1)


def standard(values):
    centred = values - jnp.mean(values, axis=-1, keepdims=True)
    inverse = lax.rsqrt(jnp.mean(centred * centred, axis=-1, keepdims=True) + 1e-06)
    return centred * inverse, inverse


def norm_pull(grad, scaled, inverse, gain):
    g = grad * gain
    return inverse * (
        g - jnp.mean(g, axis=-1, keepdims=True) - scaled * jnp.mean(g * scaled, axis=-1, keepdims=True)
    )


def gelu_slope(v):
    cdf = 0.5 + 0.5 * lax.erf(v * math.sqrt(0.5))
    return v * cdf, cdf + v * (jnp.exp(-0.5 * v * v) * (1.0 / math.sqrt(2.0 * math.pi)))


def rows_of(i):
    return pl.ds(pl.multiple_of(i * STEP, 16), STEP)


def fold(values):
    return jnp.sum(values.reshape(STEP // 8, 8, values.shape[1]), axis=0)


def head_slot(g):
    return (g % 3) * 4 + g // 3


class Layer:
    def __init__(self, refs):
        self.__dict__.update(refs)

    def mat(self, n, y, c):
        return self.w[n, y, c].reshape(DM, 256)

    def put(self, n, y, c, value):
        self.w[n, y, c] = value.astype(BF16).reshape(4, 2, 96, 256)

    def pack(self, which):
        outt = self.wout[...].astype(F32).T
        q, k, v = (self.qkv[a].astype(F32) for a in range(3))
        for j in which:
            cols = slice(64 * j, 64 * j + 64)
            self.own[j] = jnp.concatenate([a[:, cols] for a in (q, v, k, outt)], axis=1).astype(BF16)
            if j > 0:
                for i in (0, j) if j == 1 else (j,):
                    wide = slice(256 * i, 256 * i + 256)
                    self.own[3 + 2 * i] = self.up[:, wide]
                    self.own[4 + 2 * i] = self.down[:, wide]

    def prepare(self, t):
        for k in range(12):
            for b in range(6):
                self.vec[k : k + 1, 128 * b : 128 * b + 128] = self.flat[6 * k + b : 6 * k + b + 1, :]
        none = jnp.zeros((1, 128), F32)
        for g in range(12):
            cols = slice(64 * g, 64 * g + 64)
            self.bias[head_slot(g)] = jnp.concatenate([self.vec[4:5, cols], self.vec[5:6, cols], none], axis=1)
            self.bias[12 + head_slot(g)] = self.vec[7 + g // 3 : 8 + g // 3, 256 * (g % 3) : 256 * (g % 3) + 256]
        self.patches = self.pat[t]

    def masks(self):
        row = lax.broadcasted_iota(jnp.int32, (ROWS, 128), 0)
        lane = lax.broadcasted_iota(jnp.int32, (ROWS, 128), 1)
        p = jnp.full((ROWS, 128), self.patches, jnp.int32)
        image = sum(jnp.where(row >= k * p, 1, 0) for k in (1, 2, 3))
        same = jnp.where(image == lane - 64, 1.0, 0.0)
        slot = (lane >= 64) & (lane < 68)
        self.mq[...] = jnp.where(slot, (same - 1.0) * BIG, 0.0).astype(BF16)
        self.mk[...] = jnp.where(slot, same, jnp.where((lane >= 68) & (lane < 71), 1.0, 0.0)).astype(BF16)

    def norm1(self, half):
        def step(i, _):
            r = rows_of(i)
            scaled, _ = standard(self.tok[r, :].astype(F32))
            self.n1[r, :] = (scaled * self.vec[0:1, :] + self.vec[1:2, :]).astype(BF16)
            return 0

        lax.fori_loop(4 * half, 4 + 3 * half, step, 0)

    def attend(self, i):
        j, y = lax.div(i, 2), lax.rem(i, 2)
        lane = lax.broadcasted_iota(jnp.int32, (ROWS, 128), 1)
        left = lane < 64
        out_halves = []
        for c in range(2):
            h = i * 2 + c
            mixed = (nn(self.n1[...], self.mat(j, y, c)) + self.bias[h]).astype(BF16)
            self.qa[h] = jnp.where(left, mixed[:, :128], self.mq[...])
            self.ka[h] = jnp.where(left, mixed[:, 128:], self.mk[...])
            self.va[h] = jnp.where(left, jnp.ones((), BF16), mixed[:, :128])
            out_halves.append(self.mat(j, y, c)[:, 128:])
        first = lax.broadcasted_iota(jnp.int32, (DM, 128), 1) < 64
        self.ot[j, y] = jnp.where(first, turn(out_halves[0]), out_halves[1].astype(F32)).astype(BF16)
        for r0, n in PARTS:
            r = pl.ds(r0, n)
            lanes = lax.broadcasted_iota(jnp.int32, (n, 128), 1)
            results = []
            for c in range(2):
                h = i * 2 + c
                q = self.qa[h, r, :]
                s = nt(q, self.ka[h])
                top = jnp.max(s, axis=1, keepdims=True) * CS
                p = jnp.exp2(s * CS - top).astype(BF16)
                a = nn(p, self.va[h])
                total = pltpu.roll(a, 64, 1)
                results.append(a * (1.0 / total))
                h1, h2, h3 = split3((top + jnp.log2(total)) * (-1.0 / CS))
                self.qa[h, r, :] = jnp.where(
                    lanes == 68, h1, jnp.where(lanes == 69, h2, jnp.where(lanes == 70, h3, q))
                )
            pair = jnp.where(lanes < 64, pltpu.roll(results[0], 64, 1), results[1])
            self.att[j, y, r, :] = pair.astype(BF16)

    def pair(self, ref, j, r=slice(None)):
        return jnp.concatenate([ref[j, 0, r, :], ref[j, 1, r, :]], axis=1)

    def project(self):
        for r0, n in PARTS:
            r = pl.ds(r0, n)
            total = sum(nt(self.pair(self.att, j, r), self.pair(self.ot, j)) for j in range(3))
            self.res[r, :] = total + (self.tok[r, :].astype(F32) + self.vec[6:7, :])

        def step(i, _):
            r = rows_of(i)
            v = self.res[r, :]
            scaled, _ = standard(v)
            self.n2[r, :] = (scaled * self.vec[2:3, :] + self.vec[3:4, :]).astype(BF16)
            self.acc[r, :] = v + self.vec[11:12, :]
            self.gn[r, :] = jnp.zeros((STEP, DM), F32)
            return 0

        lax.fori_loop(0, ROWS // STEP, step, 0)

    def feed(self, i, pause):
        j, y = lax.div(i, 2), lax.rem(i, 2)
        nb, nc = 3 + 2 * j, 4 + 2 * j
        sums = [0.0, 0.0]
        for half, (r0, n) in enumerate(PARTS):
            r = pl.ds(r0, n)
            for c in range(2):
                cols = slice(c * 256, c * 256 + 256)
                pre = nn(self.n2[r, :], self.mat(nb, y, c)) + self.bias[12 + i * 2 + c]
                up = nn(self.cot[r, :], self.mat(nc, y, c))
                active, slope = gelu_slope(pre)
                grad = (up * slope).astype(BF16)
                self.act[r, cols] = active.astype(BF16)
                self.gp[r, cols] = grad
                sums[c] += jnp.sum(grad.astype(F32).reshape(n // 8, 8, 256), axis=0)
            self.acc[r, :] += nt(self.act[r, 0:256], self.mat(nc, y, 0)) + nt(
                self.act[r, 256:512], self.mat(nc, y, 1)
            )
            self.gn[r, :] += nt(self.gp[r, 0:256], self.mat(nb, y, 0)) + nt(
                self.gp[r, 256:512], self.mat(nb, y, 1)
            )
            pause(half)
        for c in range(2):
            cols = slice(c * 256, c * 256 + 256)
            self.hs[12 + i * 2 + c] = jnp.sum(sums[c], axis=0, keepdims=True)
            self.put(nc, y, c, tn(self.cot[...], self.act[:, cols]))
            self.put(nb, y, c, tn(self.n2[...], self.gp[:, cols]))
        pause(2)

    def residual_back(self):
        self.vs[...] = jnp.zeros(self.vs.shape, F32)

        def step(i, _):
            r = rows_of(i)
            self.out[r, :] = self.acc[r, :].astype(BF16)
            scaled, inverse = standard(self.res[r, :])
            g = self.gn[r, :]
            ct = self.cot[r, :].astype(F32)
            grad = ct + norm_pull(g, scaled, inverse, self.vec[2:3, :])
            self.res[r, :] = grad
            self.gb[r, :] = grad.astype(BF16)
            self.gn[r, :] = jnp.zeros((STEP, DM), F32)
            for k, v in ((2, g * scaled), (3, g), (4, grad), (5, ct)):
                self.vs[k] += fold(v)
            return 0

        lax.fori_loop(0, ROWS // STEP, step, 0)

    def attend_back(self, i, pause):
        j, y = lax.div(i, 2), lax.rem(i, 2)
        lane = lax.broadcasted_iota(jnp.int32, (ROWS, 128), 1)
        left = lane < 64

        @pl.when(y == 0)
        def _():
            self.act[:, 256:512] = nn(self.gb[...], self.pair(self.ot, j)).astype(BF16)
            self.acc[0:DM, 128:384] = tn(self.gb[...], self.pair(self.att, j))

        low = self.act[:, pl.ds(pl.multiple_of(256 + 128 * y, 128), 128)]
        wide = low.astype(F32)
        product = wide * self.att[j, y].astype(F32)
        for c in range(2):
            h = i * 2 + c
            delta = jnp.sum(jnp.where(left == (c == 0), product, 0.0), axis=1, keepdims=True)
            d1, d2, d3 = split3(jnp.broadcast_to(-delta, (ROWS, 128)))
            moved = pltpu.roll(wide, 64, 1).astype(BF16) if c == 0 else low
            none = jnp.zeros((), BF16)
            extra = jnp.where(lane == 0, d1, jnp.where(lane == 1, d2, jnp.where(lane == 2, d3, none)))
            self.act[:, 0:128] = jnp.where(left, extra, moved)
            dv = dk = 0.0
            for r0, n in PARTS:
                r = pl.ds(r0, n)
                q, d = self.qa[h, r, :], self.act[r, 0:128]
                p = jnp.exp2(nt(q, self.ka[h]) * CS)
                ds = (p * nt(d, self.va[h])).astype(BF16)
                dv += tn(p.astype(BF16), d)
                dk += tn(ds, q)
                self.acc[r, 0:128] = nn(ds, self.ka[h])
            self.qa[h] = jnp.where(left, self.acc[:, 0:128] * 0.125, dv).astype(BF16)
            self.ka[h] = jnp.where(left, (dk * 0.125).astype(BF16), none)
            sums = jnp.sum(self.mixed_grad(h).astype(F32).reshape(ROWS // 8, 8, 256), axis=0)
            self.hs[h] = jnp.sum(sums, axis=0, keepdims=True)
            pause(c)
        outg = self.acc[0:DM, pl.ds(pl.multiple_of(128 + 128 * y, 128), 128)]
        first = lax.broadcasted_iota(jnp.int32, (DM, 128), 1) < 64
        for c in range(2):
            g = tn(self.n1[...], self.mixed_grad(i * 2 + c))
            mine = pltpu.roll(outg, 64, 1) if c == 0 else outg
            whole = jnp.concatenate([g[:, :128], jnp.where(first, g[:, 128:], mine)], axis=1)
            self.rc[i, c] = whole.astype(BF16).reshape(4, 2, 96, 256)
        pause(2)

    def mixed_grad(self, h, r=slice(None)):
        return jnp.concatenate([self.qa[h, r, :], self.ka[h, r, :]], axis=1)

    def mixed_back(self, j, half):
        r0, n = PARTS[half]
        r = pl.ds(r0, n)
        self.gn[r, :] += sum(
            nt(self.mixed_grad(4 * j + 2 * y + c, r), self.mat(j, y, c)) for y in range(2) for c in range(2)
        )

    def token_back(self, half):
        def step(i, _):
            r = rows_of(i)
            scaled, inverse = standard(self.tok[r, :].astype(F32))
            g = self.gn[r, :]
            grad = self.res[r, :] + norm_pull(g, scaled, inverse, self.vec[0:1, :])
            self.gtok[r, :] = grad.astype(BF16)
            self.vs[0] += fold(g * scaled)
            self.vs[1] += fold(g)
            return 0

        lax.fori_loop(4 * half, 4 + 3 * half, step, 0)

    def collect(self, group):
        for h in range(12):
            if group == 0:
                self.vsum[h : h + 1, :] = self.hs[12 + h]
            if group == 1:
                self.vsum[24 + h : 25 + h, :] = self.hs[h]
        for k, at in {0: ((2, 12), (3, 15), (4, 18), (5, 21)), 1: (), 2: ((0, 40), (1, 43))}[group]:
            row = jnp.sum(self.vs[k], axis=0, keepdims=True)
            for b in range(3):
                self.vsum[at + b : at + b + 1, :] = row[:, 256 * b : 256 * b + 256]
        if group:
            lo, hi = ((36, 40), (46, 48))[group - 1]
            self.vsum[lo:hi, :] = jnp.zeros((hi - lo, 256), F32)


def layer_scratch():
    return dict(
        w=pltpu.VMEM(WSHAPE, BF16),
        tok=pltpu.VMEM((ROWS, DM), BF16),
        cot=pltpu.VMEM((ROWS, DM), BF16),
        out=pltpu.VMEM((ROWS, DM), BF16),
        gtok=pltpu.VMEM((ROWS, DM), BF16),
        io=pltpu.SemaphoreType.DMA((5,)),
        n1=pltpu.VMEM((ROWS, DM), BF16),
        n2=pltpu.VMEM((ROWS, DM), BF16),
        gb=pltpu.VMEM((ROWS, DM), BF16),
        qa=pltpu.VMEM((12, ROWS, 128), BF16),
        ka=pltpu.VMEM((12, ROWS, 128), BF16),
        va=pltpu.VMEM((12, ROWS, 128), BF16),
        att=pltpu.VMEM((3, 2, ROWS, 128), BF16),
        ot=pltpu.VMEM((3, 2, DM, 128), BF16),
        res=pltpu.VMEM((ROWS, DM), F32),
        acc=pltpu.VMEM((ROWS, DM), F32),
        gn=pltpu.VMEM((ROWS, DM), F32),
        mq=pltpu.VMEM((ROWS, 128), BF16),
        mk=pltpu.VMEM((ROWS, 128), BF16),
        act=pltpu.VMEM((ROWS, 512), BF16),
        gp=pltpu.VMEM((ROWS, 512), BF16),
        vs=pltpu.VMEM((6, 8, DM), F32),
        hs=pltpu.VMEM((24, 1, 256), F32),
        own=pltpu.VMEM((NCH, 96, 256), BF16),
        vec=pltpu.VMEM((12, DM), F32),
        bias=pltpu.VMEM((24, 1, 256), F32),
    )


NAMES_IN = ("tok_in", "cot_in", "qkv", "wout", "up", "down", "flat", "pat")
NAMES_OUT = ("out_to", "gtok_to", "gsh", "vsum")


PLAN = {
    "s0": ((0, 0, 0),),
    "s2": ((0, 1, 0), (0, 2, 0),),
    "s3": ((0, 3, 0), (0, 4, 0), (0, 0, 1), (0, 1, 1), (0, 0, 2), (0, 0, 3), (0, 0, 4), (0, 2, 1), (0, 1, 2), (0, 1, 3), (0, 1, 4), (0, 0, 5), (0, 3, 1), (0, 0, 6),),
    ("a", 0, 0): ((0, 2, 2), (0, 2, 3), (0, 2, 4), (0, 4, 1), (0, 5, 0),),
    ("a", 1, 0): ((0, 1, 5), (0, 3, 2), (0, 3, 3), (0, 1, 6),),
    ("a", 2, 0): ((0, 2, 5), (0, 3, 4), (0, 5, 1), (0, 6, 0),),
    ("a", 3, 0): ((0, 2, 6), (0, 4, 2), (0, 4, 3), (0, 7, 0),),
    ("a", 4, 0): ((0, 3, 5), (0, 4, 4), (0, 6, 1),),
    ("a", 5, 0): ((0, 3, 6), (0, 5, 2), (0, 5, 3), (0, 5, 4),),
    "p": ((0, 4, 5), (0, 6, 2), (0, 6, 3), (0, 7, 1), (0, 8, 0), (0, 4, 6),),
    ("f", 0, 0): ((0, 6, 4),),
    ("f", 0, 1): ((0, 5, 5),),
    ("f", 0, 2): ((0, 5, 6), (0, 6, 5),),
    ("f", 1, 0): ((0, 6, 6), (0, 8, 1),),
    ("f", 1, 1): ((0, 7, 2), (0, 7, 3),),
    ("f", 1, 2): ((0, 7, 4), (1, 0, 0), (1, 1, 0),),
    ("f", 2, 0): ((0, 8, 2), (0, 8, 3),),
    ("f", 2, 2): ((0, 8, 4),),
    ("f", 3, 0): ((0, 7, 5),),
    ("f", 3, 1): ((0, 7, 6), (0, 8, 5),),
    ("f", 3, 2): ((0, 8, 6), (1, 0, 1), (1, 1, 1), (1, 2, 0), (1, 3, 0),),
    ("f", 4, 1): ((1, 2, 1),),
    ("f", 4, 2): ((1, 0, 2), (1, 0, 3), (1, 3, 1),),
    ("f", 5, 1): ((1, 1, 2), (1, 1, 3),),
    ("f", 5, 2): ((1, 4, 0), (1, 5, 0),),
    "q": ((2, 0, 0), (1, 2, 2), (1, 2, 3), (1, 4, 1), (1, 5, 1),),
    ("b", 0, 0): ((2, 0, 1), (1, 0, 4),),
    ("b", 0, 1): ((1, 3, 2), (1, 3, 3),),
    ("b", 1, 0): ((1, 1, 4),),
    ("b", 1, 1): ((1, 0, 5), (1, 2, 4),),
    ("b", 1, 2): ((1, 4, 2), (1, 4, 3), (1, 6, 0),),
    ("b", 2, 0): ((1, 6, 1), (1, 1, 5),),
    ("b", 2, 1): ((1, 5, 2), (1, 5, 3),),
    ("b", 2, 2): ((2, 0, 2), (1, 2, 5),),
    ("b", 3, 0): ((1, 3, 4),),
    ("b", 3, 1): ((1, 4, 4), (2, 0, 3),),
    ("b", 3, 2): ((1, 6, 2), (1, 6, 3), (1, 7, 0),),
    ("b", 4, 0): ((1, 7, 1), (1, 3, 5),),
    ("b", 4, 1): ((1, 5, 4),),
    ("b", 4, 2): ((1, 4, 5), (1, 6, 4),),
    ("b", 5, 0): ((1, 7, 2), (1, 7, 3),),
    ("b", 5, 2): ((1, 5, 5), (1, 8, 0),),
    ("u", 0): ((2, 1, 0),),
    ("u", 1): ((1, 7, 4),),
    ("u", 3): ((2, 1, 1), (1, 6, 5), (1, 8, 1),),
    ("t", 0): ((2, 1, 2),),
    ("t", 1): ((1, 7, 5), (1, 8, 2), (1, 8, 3),),
    "end": ((2, 2, 0), (2, 2, 1), (2, 1, 3), (1, 8, 4), (2, 2, 2), (1, 8, 5), (2, 2, 3),),
}


class Totals:
    ROWS = (pl.ds(0, 24), pl.ds(24, 16), pl.ds(40, 8))

    def __init__(self, p, value, vr, ss, rs):
        self.p, self.value, self.vr, self.ss, self.rs = p, value, vr, ss, rs
        self.mine = (1 + 2 * p.y + p.x, 5 + p.z)
        self.to = (p.core, p.xnb, p.ynb, p.diag) + p.along
        x, y = p.x, p.y
        self.there = (0, 1 + 2 * y + 1 - x, 1 + 2 * (1 - y) + x, 1 + 2 * (1 - y) + 1 - x) + tuple(
            5 + p.zrel(s) for s in (1, 2, 3)
        )

    def copy(self, g, k, src, dst):
        return pltpu.make_async_remote_copy(
            src, dst, send_sem=self.ss.at[g, k], recv_sem=self.rs.at[g, k], device_id=self.to[k], device_id_type=MESH
        )

    def arrive(self, g, *ks):
        for k in ks:
            slot = self.vr.at[self.there[k], self.ROWS[g]]
            self.copy(g, k, slot, slot).wait_recv()

    def send(self, g, *ks):
        slot = self.vr.at[self.mine[0] if ks[0] < 4 else self.mine[1], self.ROWS[g]]
        for k in ks:
            self.copy(g, k, slot, slot).start()

    def finish(self, g):
        slot = self.vr.at[0, self.ROWS[g]]
        for k in range(1, 7):
            self.copy(g, k, slot, slot).wait_send()

    def stage(self, g, s):
        rows, value = self.ROWS[g], self.value.at[self.ROWS[g]]
        part = [self.vr.at[k, rows] for k in range(9)]
        if s == 0:
            self.copy(g, 0, value, part[0]).start()
        elif s == 1:
            self.arrive(g, 0)
            self.vr[self.mine[0], rows] = value[...] + part[0][...]
            self.send(g, 1, 2, 3)
        elif s == 2:
            self.arrive(g, 1, 2, 3)
            self.vr[self.mine[1], rows] = (part[1][...] + part[2][...]) + (part[3][...] + part[4][...])
            self.send(g, 4, 5, 6)
        else:
            self.arrive(g, 4, 5, 6)
            self.copy(g, 0, value, value).wait_send()
            value[...] = (part[5][...] + part[6][...]) + (part[7][...] + part[8][...])


def mega_kernel(names, *refs):
    r = dict(zip(names, refs))
    layer = Layer(r)
    cut = STEP * 4
    moves = [
        pltpu.make_async_copy(a, b, r["io"].at[k])
        for k, (a, b) in enumerate(
            (
                (r["tok_in"], r["tok"]),
                (r["cot_in"], r["cot"]),
                (r["out"], r["out_to"]),
                (r["gtok"].at[0:cut], r["gtok_to"].at[0:cut]),
                (r["gtok"].at[cut:ROWS], r["gtok_to"].at[cut:ROWS]),
            )
        )
    ]
    moves[0].start()
    moves[1].start()
    p = Place()
    p.barrier()
    gather = Gather(p, r["own"], r["w"], r["gss"], r["grs"])
    scatter = Scatter(p, r["w"], r["gsh"], r["rc"], r["rd"], r["rl"], r["rz"], r["sss"], r["srs"])
    totals = Totals(p, r["vsum"], r["vr"], r["vss"], r["vrs"])

    engines = (gather, scatter, totals)

    def at(site):
        for e, n, s in PLAN.get(site, ()):
            engines[e].stage(n, s)

    def within(kind, i, k=0):
        for turn in range(6):
            if (kind, turn, k) in PLAN:
                pl.when(i == turn)(functools.partial(at, (kind, turn, k)))

    def loop(count, body):
        lax.fori_loop(0, count, lambda i, c: (body(i), c)[1], 0)

    layer.pack((0,))
    at("s0")
    layer.pack((1, 2))
    for n in range(NCH):
        r["w"][n, p.y, p.c, p.z, p.x] = r["own"][n]
    layer.prepare(lax.axis_index("tensor"))
    layer.masks()
    at("s1")
    moves[0].wait()
    layer.norm1(0)
    at("s2")
    layer.norm1(1)
    at("s3")

    def attend(i):
        layer.attend(i)
        within("a", i)

    loop(6, attend)
    moves[1].wait()
    layer.project()
    at("p")

    def feed(i):
        @pl.when(lax.rem(i, 2) == 0)
        def _():
            gather.finish(3 + i)
            gather.finish(4 + i)

        layer.feed(i, functools.partial(within, "f", i))

    loop(6, feed)
    layer.residual_back()
    moves[2].start()
    layer.collect(0)
    at("q")
    loop(6, lambda i: layer.attend_back(i, functools.partial(within, "b", i)))
    layer.collect(1)
    for k in range(6):
        layer.mixed_back(k // 2, k % 2)
        at(("u", k))
    for half in range(2):
        layer.token_back(half)
        moves[3 + half].start()
        at(("t", half))
    layer.collect(2)
    at("end")
    for move in moves[2:]:
        move.wait()
    for n in range(3):
        gather.finish(n)
    for m in range(NCH):
        scatter.finish(m)
    for g in range(3):
        totals.finish(g)


def mega_scratch():
    return dict(
        layer_scratch(),
        rc=pltpu.VMEM((NCH, 2, 4, 2, 96, 256), BF16),
        rd=pltpu.VMEM((NCH, 2, 4, HALF, 256), BF16),
        rl=pltpu.VMEM((NCH, 2, 4, 96, 256), BF16),
        rz=pltpu.VMEM((NCH, 3, 96, 256), BF16),
        vr=pltpu.VMEM((9, 48, 256), F32),
        gss=pltpu.SemaphoreType.DMA((NCH, Gather.COPIES)),
        grs=pltpu.SemaphoreType.DMA((NCH, Gather.COPIES)),
        sss=pltpu.SemaphoreType.DMA((NCH, Scatter.COPIES)),
        srs=pltpu.SemaphoreType.DMA((NCH, Scatter.COPIES)),
        vss=pltpu.SemaphoreType.DMA((3, 7)),
        vrs=pltpu.SemaphoreType.DMA((3, 7)),
    )


def mega_call(*args):
    scratch = mega_scratch()
    names = NAMES_IN + NAMES_OUT + tuple(scratch)
    vm = pl.BlockSpec(memory_space=pltpu.VMEM)
    shape = jax.ShapeDtypeStruct
    return pl.pallas_call(
        functools.partial(mega_kernel, names),
        out_shape=(
            shape((ROWS, DM), BF16),
            shape((ROWS, DM), BF16),
            shape((NCH, 96, 256), F32),
            shape((48, 256), F32),
        ),
        in_specs=[pl.BlockSpec(memory_space=pl.ANY)] * 2 + [vm] * (len(NAMES_IN) - 3) + [pl.BlockSpec(memory_space=pltpu.SMEM)],
        out_specs=(pl.BlockSpec(memory_space=pl.ANY),) * 2 + (vm,) * 2,
        scratch_shapes=list(scratch.values()),
        compiler_params=pltpu.CompilerParams(collective_id=0, has_side_effects=True, vmem_limit_bytes=62 << 20),
    )(*args)


def tail_kernel(names, *refs):
    r = dict(zip(names, refs))
    r["out"][...] = r["out_in"][...]
    r["gtok"][...] = r["gtok_in"][...]
    g = r["gsh"]
    for j in range(3):
        cols = slice(64 * j, 64 * j + 64)
        for a, k in enumerate((0, 128, 64)):
            r["gqkv"][a, :, cols] = g[j, :, k : k + 64]
        r["gup"][:, 256 * j : 256 * j + 256] = g[3 + 2 * j]
        r["gdown"][:, 256 * j : 256 * j + 256] = g[4 + 2 * j]
        r["gout"][cols, :] = g[j, :, 128:256].T[64:128, :]
    v, gv = r["vsum"], r["gvec"]
    for row, at in ((0, 40), (1, 43), (2, 12), (3, 15), (6, 18), (11, 21)):
        for b in range(6):
            k = at + b // 2
            gv[6 * row + b : 6 * row + b + 1, :] = v[k : k + 1, 128 * (b % 2) : 128 * (b % 2) + 128]
    for half in range(2):
        for b in range(6):
            two = [v[24 + h : 25 + h, 64 * half : 64 * half + 64] for h in (head_slot(2 * b), head_slot(2 * b + 1))]
            gv[24 + 6 * half + b : 25 + 6 * half + b, :] = jnp.concatenate(two, axis=1)
    for t in range(4):
        for b in range(6):
            row = (b // 2) * 4 + t
            gv[42 + 6 * t + b : 43 + 6 * t + b, :] = v[row : row + 1, 128 * (b % 2) : 128 * (b % 2) + 128]
    rate = r["rate"][0]
    for name in ("qkv", "wout", "up", "down", "vec"):
        r["next_" + name][...] = rate * r["target_" + name][...] + (1.0 - rate) * r[name][...].astype(F32)


def tail_call(results, online, targets, momentum):
    five = ("qkv", "wout", "up", "down", "vec")
    ins = ("out_in", "gtok_in", "gsh", "vsum") + five + tuple("target_" + a for a in five) + ("rate",)
    outs = ("out", "gtok", "gqkv", "gout", "gup", "gdown", "gvec") + tuple("next_" + a for a in five)
    vm = pl.BlockSpec(memory_space=pltpu.VMEM)
    shape = jax.ShapeDtypeStruct
    like = [shape(a.shape, F32) for a in online]
    return pl.pallas_call(
        functools.partial(tail_kernel, ins + outs),
        out_shape=[shape(results[0].shape, BF16), shape(results[1].shape, BF16)] + like + like,
        in_specs=[vm] * 14 + [pl.BlockSpec(memory_space=pltpu.SMEM)],
        out_specs=[vm] * 12,
    )(*results, *online, *targets, momentum)


HD = 64
BOTH = ("dp", "tensor")


def unpack(vectors, d, ff):
    cuts = [d * i for i in range(8)] + [7 * d + ff, 8 * d + ff]
    return tuple(vectors[a:b] for a, b in zip(cuts[:-1], cuts[1:]))


def norm_parts(values):
    centred = values - jnp.mean(values, axis=-1, keepdims=True)
    inverse = lax.rsqrt(jnp.mean(centred * centred, axis=-1, keepdims=True) + 1e-06)
    return centred * inverse, inverse


def norm_backward(grad_normed, scaled, inverse, gain):
    weighted = grad_normed * gain
    return inverse * (
        weighted
        - jnp.mean(weighted, axis=-1, keepdims=True)
        - scaled * jnp.mean(weighted * scaled, axis=-1, keepdims=True)
    )


def gelu_parts(v):
    cdf = 0.5 * (1.0 + lax.erf(v * (0.5**0.5)))
    return v * cdf, cdf + v * jnp.exp(-0.5 * v * v) * ((2.0 * jnp.pi) ** -0.5)


def dot(a, b, dims):
    return lax.dot_general(a, b, (dims, ((), ())), preferred_element_type=F32)


def pack_shards(qkv, out, up, down):
    first = jnp.concatenate([qkv[0], qkv[1], qkv[2], out.T], axis=1)
    return jnp.stack([first, up, down.T])


def gather_blocks(shards, dp, tensor):
    every = lax.all_gather(shards, BOTH, axis=0)
    b, r, c = shards.shape
    every = every.reshape(dp, tensor, b, r, c).transpose(2, 1, 0, 3, 4)
    return every.reshape(b, tensor, dp * r, c)


def scatter_blocks(blocks, dp, tensor):
    b, t, rows, c = blocks.shape
    r = rows // dp
    pieces = blocks.reshape(b, tensor, dp, r, c).transpose(2, 1, 0, 3, 4)
    pieces = pieces.reshape(dp * tensor, b, r, c)
    return lax.psum_scatter(pieces, BOTH, scatter_dimension=0, tiled=True)[0]


def local_layer(tokens, cotangent, patches, blocks, vectors):
    rows, d = tokens.shape
    tensor, c = blocks.shape[1], blocks.shape[3]
    w = c // 4
    ff = tensor * c
    heads = d // HD
    gain1, bias1, gain2, bias2, bias_q, bias_v, bias_out, bias_up, bias_down = unpack(
        vectors, d, ff
    )
    first, up, downt = blocks[0], blocks[1], blocks[2]
    factor = HD**-0.5

    x = tokens.astype(F32)
    scaled1, inverse1 = norm_parts(x)
    normed1 = (scaled1 * gain1 + bias1).astype(BF16)
    mixed = jnp.einsum("rd,tdc->rtc", normed1, first[:, :, : 3 * w], preferred_element_type=F32)
    query = (mixed[:, :, :w].reshape(rows, d) + bias_q).astype(BF16).reshape(rows, heads, HD)
    key = mixed[:, :, w : 2 * w].reshape(rows, d).astype(BF16).reshape(rows, heads, HD)
    value = (mixed[:, :, 2 * w :].reshape(rows, d) + bias_v).astype(BF16).reshape(rows, heads, HD)
    images = jnp.arange(rows, dtype=jnp.int32) // patches
    allowed = images[:, None] == images[None, :]
    scores = jnp.einsum("qhd,khd->hqk", query, key, preferred_element_type=F32) * factor
    scores = jnp.where(allowed[None], scores, -1e30)
    raised = jnp.exp(scores - jnp.max(scores, axis=-1, keepdims=True))
    soft = raised / jnp.sum(raised, axis=-1, keepdims=True)
    soft_low = soft.astype(BF16)
    attended = jnp.einsum("hqk,khd->qhd", soft_low, value, preferred_element_type=F32).astype(BF16)
    flat = attended.reshape(rows, tensor, w)
    outt = first[:, :, 3 * w :]
    residual = x + jnp.einsum("rte,tde->rd", flat, outt, preferred_element_type=F32) + bias_out
    scaled2, inverse2 = norm_parts(residual)
    normed2 = (scaled2 * gain2 + bias2).astype(BF16)
    pre = jnp.einsum("rd,tdf->rtf", normed2, up, preferred_element_type=F32) + bias_up.reshape(
        tensor, c
    )
    active, slope = gelu_parts(pre)
    active = active.astype(BF16)
    second = jnp.einsum("rtf,tdf->rd", active, downt, preferred_element_type=F32)
    output = (residual + second + bias_down).astype(BF16)

    grad_active = jnp.einsum("rd,tdf->rtf", cotangent, downt, preferred_element_type=F32)
    grad_pre = (grad_active * slope).astype(BF16)
    g_down = jnp.einsum("rd,rtf->tdf", cotangent, active, preferred_element_type=F32)
    g_up = jnp.einsum("rd,rtf->tdf", normed2, grad_pre, preferred_element_type=F32)
    grad_normed2 = jnp.einsum("rtf,tdf->rd", grad_pre, up, preferred_element_type=F32)
    grad_result = cotangent.astype(F32)
    grad_residual = grad_result + norm_backward(grad_normed2, scaled2, inverse2, gain2)
    grad_branch = grad_residual.astype(BF16)
    g_outt = jnp.einsum("rd,rte->tde", grad_branch, flat, preferred_element_type=F32)
    grad_att = jnp.einsum("rd,tde->rte", grad_branch, outt, preferred_element_type=F32)
    grad_att = grad_att.astype(BF16).reshape(rows, heads, HD)
    grad_value = jnp.einsum("hqk,qhd->khd", soft_low, grad_att, preferred_element_type=F32)
    grad_soft = jnp.einsum("qhd,khd->hqk", grad_att, value, preferred_element_type=F32)
    grad_scores = (
        soft * (grad_soft - jnp.sum(soft * grad_soft, axis=-1, keepdims=True))
    ).astype(BF16)
    grad_query = (
        jnp.einsum("hqk,khd->qhd", grad_scores, key, preferred_element_type=F32) * factor
    )
    grad_key = jnp.einsum("hqk,qhd->khd", grad_scores, query, preferred_element_type=F32) * factor
    three = [
        g.astype(BF16).reshape(rows, tensor, w) for g in (grad_query, grad_key, grad_value)
    ]
    grad_mixed = jnp.concatenate(three, axis=2)
    g_qkv = jnp.einsum("rd,rtc->tdc", normed1, grad_mixed, preferred_element_type=F32)
    grad_normed1 = jnp.einsum(
        "rtc,tdc->rd", grad_mixed, first[:, :, : 3 * w], preferred_element_type=F32
    )
    grad_tokens = (grad_residual + norm_backward(grad_normed1, scaled1, inverse1, gain1)).astype(
        BF16
    )
    grads = jnp.stack(
        [
            jnp.concatenate([g_qkv, g_outt], axis=2).astype(BF16),
            g_up.astype(BF16),
            g_down.astype(BF16),
        ]
    )

    def total(values):
        return jnp.sum(values.astype(F32), axis=0).reshape(-1)

    sums = jnp.concatenate(
        [
            total(grad_normed1 * scaled1),
            total(grad_normed1),
            total(grad_normed2 * scaled2),
            total(grad_normed2),
            total(three[0]),
            total(three[2]),
            total(grad_residual),
            total(grad_pre),
            total(grad_result),
        ]
    )
    return output, grad_tokens, grads, sums


def flat_views(arrays):
    qkv, out, up, down, vectors = arrays
    return qkv, out, up, down.T, vectors.reshape(72, 128)


def ringed(tokens, cotangent, block_patches, online, momentum, targets):
    online, targets = flat_views(online), flat_views(targets)
    results = mega_call(tokens, cotangent, *online, block_patches)
    final = tail_call(results, online, targets, momentum)
    return tuple(final[:2]) + tuple(
        a.T if k == 3 else a.reshape(-1) if k == 4 else a for five in (final[2:7], final[7:]) for k, a in enumerate(five)
    )


def general(dp, tensor, tokens, cotangent, patches, qkv, out, up, down, vectors):
    blocks = gather_blocks(pack_shards(qkv, out, up, down), dp, tensor)
    output, grad_tokens, grads, sums = local_layer(tokens, cotangent, patches, blocks, vectors)
    grads = scatter_blocks(grads, dp, tensor).astype(F32)
    w = qkv.shape[2]
    return (
        output,
        grad_tokens,
        jnp.stack([grads[0][:, i * w : (i + 1) * w] for i in range(3)]),
        grads[0][:, 3 * w :].T,
        grads[1],
        grads[2].T,
        lax.psum(sums, BOTH),
    )


def make_body(dp, tensor):
    def body(tokens, cotangent, block_patches, qkv, out, up, down, vectors, momentum, *targets):
        online = (qkv, out, up, down, vectors)
        if (dp, tensor) == (8, 4):
            return ringed(tokens, cotangent, block_patches, online, momentum, targets)
        patches = block_patches[lax.axis_index("tensor")]
        results = general(dp, tensor, tokens, cotangent, patches, *online)
        rate = momentum[0]
        return results + tuple(
            rate * target + (1.0 - rate) * weight.astype(F32) for target, weight in zip(targets, online)
        )

    return body


def solution(mesh):
    rows, matrices = P(BOTH, None), (
        P(None, "dp", "tensor"),
        P("tensor", "dp"),
        P("dp", "tensor"),
        P("tensor", "dp"),
    )
    return jax.shard_map(
        make_body(mesh.shape["dp"], mesh.shape["tensor"]),
        mesh=mesh,
        in_specs=(rows, rows, P("dp")) + matrices + (P(), P()) + matrices + (P(),),
        out_specs=(rows, rows) + matrices + (P(),) + matrices + (P(),),
        check_vma=False,
    )
```
